256 devices in a mesh: cfg: 2 (over core), img: 4 (over x), seq: 32 (over z, y).
Axes of the slice: x: 4, y: 4, z: 8, core: 2. Of those that a mesh axis runs over, the one named last changes fastest.
Arguments:
- img_qkv: bfloat16 [2, 4, 4096, 3, 2048], P('cfg', 'img', 'seq'), may hold values from -5 to 5
- txt_kv: bfloat16 [2, 4, 256, 2, 2048], P('cfg', 'img', 'seq'), may hold values from -5 to 5
- readout: bfloat16 [2048, 64], replicated, may hold values from -0.125 to 0.125
- old_velocity: float32 [4, 4096, 64], P('img', 'seq'), may hold values from -6 to 6
- noise: float32 [4, 4096, 64], P('img', 'seq'), may hold values from -5 to 5
- step_ratio: float32 [4], P('img'), may hold values from 0.2 to 0.8
- rewards: float32 [4], P('img'), may hold values from -6 to 6
- guidance: float32 [], replicated, may hold values from 1.5 to 3
Outputs:
- img_grad: bfloat16 [2, 4, 4096, 3, 2048], P('cfg', 'img', 'seq')
- txt_grad: bfloat16 [2, 4, 256, 2, 2048], P('cfg', 'img', 'seq')
- readout_grad: float32 [2048, 64], replicated
- ratio: float32 [4], P('img')
The draws below stay inside these ranges and needn't reach their ends.
All inputs are finite; a program needn't handle non-finite values.
Results may differ from the reference program's by a relative error of at most 0.009.
Values may be sent and summed in bfloat16 or wider, within the bound.
A program may use at most 128 MiB of HBM per device.

```python
import math
import jax
import jax.numpy as jnp
from jax import lax

HEADS = 16
HEAD_DIM = 128
CH = 64
IMAGES = 4
IMGTOK = 4096
TXTTOK = 256
HD = 2048


def draw_img_qkv(key, part):
    width = HEADS * HEAD_DIM
    shape = (2, IMAGES, IMGTOK, 3, width)
    base_key = jax.random.fold_in(key, 11)
    slot_scale = jnp.array([1.6, 1.6, 1.0], jnp.float32).reshape(1, 1, 1, 3, 1)
    values = jnp.clip(jax.random.normal(base_key, shape, jnp.float32) * slot_scale, -5.0, 5.0)
    return values.astype(jnp.bfloat16)


def draw_old_velocity(key, part):
    shape = (IMAGES, IMGTOK, CH)
    first_key = jax.random.fold_in(key, 21)
    place = jnp.arange(IMGTOK, dtype=jnp.float32) / max(IMGTOK - 1, 1)
    rising = (0.35 * 3.0 ** place).reshape(1, IMGTOK, 1)
    values = jax.random.normal(first_key, shape, jnp.float32) * rising
    return jnp.clip(values, -6.0, 6.0)


def levels(stream_key, shape, split, smallest, high):
    def one(axis_at, blocks):
        steps = jax.random.uniform(jax.random.fold_in(jax.random.fold_in(stream_key, 6), axis_at), (blocks,), jnp.float32, smallest / len(split), high / len(split))
        return jnp.repeat(jnp.exp(steps), shape[axis_at] // blocks).reshape((-1,) + (1,) * (len(shape) - axis_at - 1))

    factor_of = one(*split[0])
    for cut in split[1:]:
        factor_of = factor_of * one(*cut)
    return factor_of


def gaussian(own_key, extent, scale, reach, shards=(), held_as=jnp.bfloat16):
    level = levels(own_key, extent, shards, -0.22, 0.18) if shards else 1.0
    drawn = jax.random.normal(own_key, extent, jnp.float32) * scale * level
    return jnp.minimum(jnp.maximum(drawn, -reach), reach).astype(held_as)


def setup_inputs(seed: int = 0) -> dict:
    splits = jax.random.split(jax.random.key(seed), 9)
    return {
        "img_qkv": draw_img_qkv(jax.random.fold_in(splits[8], 71), 0),
        "txt_kv": gaussian(splits[1], (2, IMAGES, TXTTOK, 2, HD), 1.3, 5.0, ((0, 2), (1, 4), (2, 32))),
        "readout": gaussian(splits[2], (HD, CH), HD ** -0.5, 0.125),
        "old_velocity": draw_old_velocity(jax.random.fold_in(splits[8], 71), 0),
        "noise": gaussian(splits[4], (IMAGES, IMGTOK, CH), 1.0, 5.0, ((0, 4), (1, 32)), jnp.float32),
        "step_ratio": jnp.clip(jnp.exp(math.log(0.8) - 1.3862944 * jax.random.uniform(splits[5], (IMAGES,), jnp.float32) ** levels(splits[5], (IMAGES,), ((0, 4),), -0.2, 0.2)), 0.2, 0.8),
        "rewards": gaussian(splits[6], (IMAGES,), 2.0, 6.0, ((0, 4),), jnp.float32),
        "guidance": jnp.clip(jax.random.uniform(splits[7], (), jnp.float32, 1.5, 3.0), 1.5, 3.0),
    }


def probabilities(query, keys):
    scores = jnp.dot(query, keys.T, preferred_element_type=jnp.float32) * HEAD_DIM ** (-0.5)
    top = lax.optimization_barrier(jnp.max(scores, axis=-1, keepdims=True))
    raised = jnp.exp(scores - top)
    return (raised / lax.optimization_barrier(jnp.sum(raised, axis=-1, keepdims=True))).astype(jnp.bfloat16)

def per_head(x):
    return x.reshape(x.shape[0], HEADS, HEAD_DIM).transpose(1, 0, 2)

def join_heads(x):
    return x.transpose(1, 0, 2).reshape(x.shape[1], HEADS * HEAD_DIM)

def forward_pair(pair):
    qkv, text = pair
    query = per_head(qkv[:, 0])
    keys = per_head(jnp.concatenate([text[:, 0], qkv[:, 1]], axis=0))
    values = per_head(jnp.concatenate([text[:, 1], qkv[:, 2]], axis=0))

    def one_head(item):
        head_q, head_k, head_v = item
        return jnp.dot(probabilities(head_q, head_k), head_v, preferred_element_type=jnp.float32).astype(jnp.bfloat16)
    return join_heads(lax.map(one_head, (query, keys, values)))

def backward_pair(pair):
    qkv, text, grad_out = pair
    query = per_head(qkv[:, 0])
    keys = per_head(jnp.concatenate([text[:, 0], qkv[:, 1]], axis=0))
    values = per_head(jnp.concatenate([text[:, 1], qkv[:, 2]], axis=0))
    grads = per_head(grad_out)

    def one_head(item):
        head_q, head_k, head_v, head_g = item
        probs = probabilities(head_q, head_k)
        grad_probs = jnp.dot(head_g, head_v.T, preferred_element_type=jnp.float32)
        weights = probs.astype(jnp.float32)
        delta = lax.optimization_barrier(jnp.sum(weights * grad_probs, axis=-1, keepdims=True))
        grad_scores = (weights * (grad_probs - delta) * HEAD_DIM ** (-0.5)).astype(jnp.bfloat16)
        grad_query = jnp.dot(grad_scores, head_k, preferred_element_type=jnp.float32).astype(jnp.bfloat16)
        grad_keys = jnp.dot(grad_scores.T, head_q, preferred_element_type=jnp.float32)
        grad_values = jnp.dot(probs.T, head_g, preferred_element_type=jnp.float32)
        return (grad_query, grad_keys, grad_values)
    grad_query, grad_keys, grad_values = lax.map(one_head, (query, keys, values, grads))
    return (join_heads(grad_query), join_heads(grad_keys), join_heads(grad_values))

def surrogate_gain(ratio, advantage):
    clipped = jnp.clip(ratio, 0.8, 1.2)
    keep = ratio * advantage <= clipped * advantage
    return jnp.where(keep, -ratio * advantage, jnp.zeros_like(ratio))

def reference(img_qkv, txt_kv, readout, old_velocity, noise, step_ratio, rewards, guidance):
    width = HEADS * HEAD_DIM
    pairs_img = img_qkv.reshape(2 * IMAGES, IMGTOK, 3, width)
    pairs_txt = txt_kv.reshape(2 * IMAGES, TXTTOK, 2, width)
    attended = lax.map(forward_pair, (pairs_img, pairs_txt))
    velocity = jnp.einsum('pnd,dc->pnc', attended.astype(jnp.float32), readout.astype(jnp.float32), precision=lax.Precision.HIGHEST).reshape(2, IMAGES, IMGTOK, CH)
    guided = velocity[1] + guidance * (velocity[0] - velocity[1])
    rate = step_ratio[:, None, None]
    deviation = rate * (guided - old_velocity)
    log_ratio = lax.optimization_barrier(jnp.sum(noise * deviation - 0.5 * deviation * deviation, axis=(1, 2))) / (IMGTOK * CH)
    ratio = jnp.exp(log_ratio)
    mean = jnp.sum(rewards) / IMAGES
    square = jnp.sum(rewards * rewards) / IMAGES
    spread = jnp.sqrt(jnp.maximum(square - mean * mean, 0.0))
    advantage = (rewards - mean) / jnp.maximum(spread, 1.0)
    gain = surrogate_gain(ratio, advantage)
    grad_guided = gain[:, None, None] * rate * (noise - deviation)
    grad_velocity = jnp.stack([guidance * grad_guided, (1.0 - guidance) * grad_guided]).reshape(2 * IMAGES, IMGTOK, CH)
    readout_grad = jnp.einsum('pnd,pnc->dc', attended.astype(jnp.float32), grad_velocity, precision=lax.Precision.HIGHEST)
    grad_attended = jnp.einsum('pnc,dc->pnd', grad_velocity, readout.astype(jnp.float32), precision=lax.Precision.HIGHEST).astype(jnp.bfloat16)
    grad_query, grad_keys, grad_values = lax.map(backward_pair, (pairs_img, pairs_txt, grad_attended))
    img_grad = jnp.stack([grad_query, grad_keys[:, TXTTOK:].astype(jnp.bfloat16), grad_values[:, TXTTOK:].astype(jnp.bfloat16)], axis=2).reshape(2, IMAGES, IMGTOK, 3, width)
    txt_grad = jnp.stack([grad_keys[:, :TXTTOK], grad_values[:, :TXTTOK]], axis=2).astype(jnp.bfloat16).reshape(2, IMAGES, TXTTOK, 2, width)
    return (img_grad, txt_grad, readout_grad, ratio)
```

```python
import functools

import jax
import jax.numpy as jnp
from jax import lax
from jax.experimental import pallas as pl
from jax.experimental.pallas import tpu as pltpu
from jax.sharding import PartitionSpec as P

D = 128
C = 64
HALF = 64
TXT = 8
YN = 4
QB = 256
KB = 256
MESH = pl.DeviceIdType.MESH
F32 = jnp.float32
BF16 = jnp.bfloat16
NT = (((1,), (1,)), ((), ()))
TN = (((0,), (0,)), ((), ()))
ANY = pl.BlockSpec(memory_space=pl.ANY)
VMEM = pl.BlockSpec(memory_space=pltpu.VMEM)
SMEM = pl.BlockSpec(memory_space=pltpu.SMEM)
LIMIT = 60 * 1024 * 1024


def iota(shape, dim):
    return lax.broadcasted_iota(jnp.int32, shape, dim)


def put(src, dst, send, recv, core, chip):
    here = jnp.logical_and(core == lax.axis_index("cfg"), chip == lax.axis_index("seq"))

    @pl.when(here)
    def _():
        pltpu.make_async_copy(src, dst, recv).start()

    @pl.when(jnp.logical_not(here))
    def _():
        away(src, dst, send, recv, {"cfg": core, "seq": chip}).start()


def away(src, dst, send, recv, device):
    return pltpu.make_async_remote_copy(
        src_ref=src,
        dst_ref=dst,
        send_sem=send,
        recv_sem=recv,
        device_id=device,
        device_id_type=MESH,
    )


def drain(ref, sem):
    pltpu.make_async_copy(ref, ref, sem).wait()


def signal_plane(chips):
    c, s = lax.axis_index("cfg"), lax.axis_index("seq")
    barrier = pltpu.get_barrier_semaphore()

    def one(k, carry):
        n = lax.rem(c * chips + s + k, 2 * chips)
        pl.semaphore_signal(
            barrier,
            inc=1,
            device_id={"cfg": n // chips, "seq": lax.rem(n, chips)},
            device_id_type=MESH,
        )
        return carry

    lax.fori_loop(1, 2 * chips, one, 0)
    return barrier


def spread_kernel(S, img, tx, rt, kv, qo, txo, vbuf, vrp, txb, vsem, ks, kr, qs, qr, ts, tr, fs, fr, gs, gr):
    H = S // 2
    c, s = lax.axis_index("cfg"), lax.axis_index("seq")
    vcopy = pltpu.make_async_copy(img.at[2], vbuf, vsem)
    vcopy.start()
    barrier = signal_plane(S)
    vcopy.wait()

    def narrow(h, carry):
        cols = pl.ds(pl.multiple_of(h * D, D), D)
        r = rt[:, cols]
        twice = jnp.concatenate([r, r], axis=0)
        x = lax.dot_general(vbuf[:, cols], twice, NT, preferred_element_type=F32)
        low = iota((HALF // 2, D), 1) < C
        for j in range(2):
            first = x[HALF * j : HALF * j + HALF // 2]
            second = x[HALF * j + HALF // 2 : HALF * j + HALF]
            vrp[h, j] = jnp.where(low, first, second).astype(BF16)
        t = tx[:, cols]
        y = lax.dot_general(t, twice, NT, preferred_element_type=F32)
        y = jnp.where(iota(y.shape, 1) < C, y, 0.0)
        txb[h] = jnp.where(iota(y.shape, 0) < TXT, t.astype(F32), y).astype(BF16)
        return carry

    lax.fori_loop(0, H, narrow, 0)
    pl.semaphore_wait(barrier, 2 * S - 1)
    side = s // H

    def send_keys(k, carry):
        h = lax.rem(s // 2 + k, H)
        chip = 2 * h + c
        cols = pl.ds(pl.multiple_of(h * D, D), D)
        for j in range(2):
            put(img.at[1, pl.ds(HALF * j, HALF), cols], kv.at[0, s, pl.ds(0, HALF)], ks.at[h, j], kr.at[s], j, chip)
            put(vrp.at[h, j], kv.at[0, s, pl.ds(HALF, HALF // 2)], ks.at[h, j], kr.at[s], j, chip)
        put(txb.at[h], txo.at[0, lax.rem(s, H)], ts.at[h], tr.at[lax.rem(s, H)], side, chip)
        return carry

    lax.fori_loop(0, H, send_keys, 0)

    def send_queries(k, carry):
        h = lax.rem(s // 2 + k, H)
        chip = 2 * h + c
        cols = pl.ds(pl.multiple_of(h * D, D), D)
        for j in range(2):
            put(img.at[0, pl.ds(HALF * j, HALF), cols], qo.at[s], qs.at[h, j], qr.at[s], j, chip)
        return carry

    lax.fori_loop(0, H, send_queries, 0)

    other = {"cfg": 1 - c}

    def forward(k, carry):
        for odd in range(2):
            src = 2 * lax.rem(s // 2 - k + H, H) + odd
            drain(kv.at[0, src], kr.at[src])
            away(kv.at[0, src], kv.at[1, src], fs.at[src], fr.at[src], other).start()
        return carry

    lax.fori_loop(0, H, forward, 0)

    def forward_text(k, carry):
        drain(txo.at[0, k], tr.at[k])
        away(txo.at[0, k], txo.at[1, k], gs.at[k], gr.at[k], other).start()
        return carry

    lax.fori_loop(0, H, forward_text, 0)

    def finish(k, carry):
        for odd in range(2):
            src = 2 * k + odd
            drain(qo.at[src], qr.at[src])
            drain(kv.at[1, src], fr.at[src])
            drain(kv.at[1, src], fs.at[src])
        drain(txo.at[1, k], gr.at[k])
        drain(txo.at[1, k], gs.at[k])
        chip = 2 * k + c
        for j in range(2):
            @pl.when(jnp.logical_not(jnp.logical_and(chip == s, j == c)))
            def _():
                drain(kv.at[0, 0], ks.at[k, j])
                drain(qo.at[0], qs.at[k, j])

        @pl.when(jnp.logical_not(jnp.logical_and(chip == s, side == c)))
        def _():
            drain(txo.at[0, 0], ts.at[k])

        return carry

    lax.fori_loop(0, H, finish, 0)


def spread(S, img, tx, rt):
    H = S // 2
    dma = pltpu.SemaphoreType.DMA
    return pl.pallas_call(
        functools.partial(spread_kernel, S),
        out_shape=(
            jax.ShapeDtypeStruct((2, S, HALF + HALF // 2, D), BF16),
            jax.ShapeDtypeStruct((S, HALF, D), BF16),
            jax.ShapeDtypeStruct((2, H, 2 * TXT, D), BF16),
        ),
        in_specs=[ANY, VMEM, VMEM],
        out_specs=(ANY, ANY, ANY),
        scratch_shapes=[
            pltpu.VMEM(img.shape[1:], BF16),
            pltpu.VMEM((H, 2, HALF // 2, D), BF16),
            pltpu.VMEM((H, 2 * TXT, D), BF16),
            dma,
            dma((H, 2)),
            dma((S,)),
            dma((H, 2)),
            dma((S,)),
            dma((H,)),
            dma((H,)),
            dma((S,)),
            dma((S,)),
            dma((H,)),
            dma((H,)),
        ],
        compiler_params=pltpu.CompilerParams(collective_id=0, has_side_effects=True),
        name="spread",
    )(img, tx, rt)


def chunks(total):
    return [(at, min(KB, total - at)) for at in range(0, total, KB)]


def pack_pair(x):
    top, low = x[: C // 2], x[C // 2 :]
    lower = iota(top.shape, 1) < HALF
    return (
        jnp.where(lower, top, pltpu.roll(low, HALF, 1)),
        jnp.where(lower, pltpu.roll(top, HALF, 1), low),
    )


def unpack_pair(a, b):
    lower = iota(a.shape, 1) < HALF
    return jnp.concatenate(
        [jnp.where(lower, a, pltpu.roll(b, HALF, 1)), jnp.where(lower, pltpu.roll(a, HALF, 1), b)], axis=0
    )


def forward_kernel(S, guidance, kv, tx, q, e_out, msg, out_t, linv, keys, keys_t, narrow, narrow_t, scores):
    nk = keys.shape[0]
    third = HALF // 2

    @pl.when(pl.program_id(0) == 0)
    def _():
        for p in range(2):
            packed = kv[p, :, HALF:, :].reshape(third * S, D)
            turned = packed.astype(F32).T
            for ab in range(2):
                rows = pl.ds((2 * p + ab) * third * S, third * S)
                part = kv[p, :, third * ab : third * ab + third, :].reshape(third * S, D)
                keys[rows] = part
                keys_t[:, rows] = part.astype(F32).T.astype(BF16)
                one = turned[C * ab : C * ab + C]
                narrow_t[:, rows] = one.astype(BF16)
                narrow[rows] = one.T.astype(BF16)
        text = tx[...].astype(F32)
        tk = text[:, :, :TXT, :].reshape(TXT * S, D)
        tv = text[:, :, TXT:, :].reshape(TXT * S, D)
        rows = pl.ds(2 * HALF * S, TXT * S)
        keys[rows] = tk.astype(BF16)
        keys_t[:, rows] = tk.T.astype(BF16)
        tvt = tv.T[:C]
        narrow_t[:, rows] = tvt.astype(BF16)
        narrow[rows] = tvt.T.astype(BF16)

    q_t = q[...].reshape(QB, D).astype(F32).T.astype(BF16)
    top = jnp.full((8, QB), -jnp.inf, F32)
    for at, size in chunks(nk):
        st = jnp.dot(keys[at : at + size], q_t, preferred_element_type=F32)
        scores[at : at + size] = st
        top = jnp.maximum(top, jnp.max(st.reshape(size // 8, 8, QB), axis=0))
    top = jnp.max(top, axis=0, keepdims=True)
    scale = D ** (-0.5) * 1.4426950408889634
    total = jnp.zeros((8, QB), F32)
    mixed = jnp.zeros((C, QB), F32)
    for at, size in chunks(nk):
        e = jnp.exp2((scores[at : at + size] - top) * scale)
        total = total + jnp.sum(e.reshape(size // 8, 8, QB), axis=0)
        e = e.astype(BF16)
        e_out[0, at : at + size] = e
        mixed = mixed + jnp.dot(narrow_t[:, at : at + size], e, preferred_element_type=F32)
    inverse = 1.0 / jnp.sum(total, axis=0, keepdims=True)
    linv[0] = inverse
    mixed = mixed * inverse
    out_t[0] = mixed
    branch = lax.rem(lax.axis_index("seq"), 2)
    share = jnp.where(branch == 0, guidance[0, 0], 1.0 - guidance[0, 0])
    for m in range(QB // D):
        a, b = pack_pair(mixed[:, D * m : D * m + D] * share)
        msg[2 * m] = a.astype(BF16)
        msg[2 * m + 1] = b.astype(BF16)


def forward(S, guidance, kv, tx, q):
    nk = (2 * HALF + TXT) * S
    nb = S * HALF // QB
    per = QB // HALF
    whole = lambda *shape: pl.BlockSpec(shape, lambda i: (0,) * len(shape))
    block = lambda *shape: pl.BlockSpec(shape, lambda i: (i,) + (0,) * (len(shape) - 1))
    return pl.pallas_call(
        functools.partial(forward_kernel, S),
        grid=(nb,),
        out_shape=(
            jax.ShapeDtypeStruct((nb, nk, QB), BF16),
            jax.ShapeDtypeStruct((S, C // 2, D), BF16),
            jax.ShapeDtypeStruct((nb, C, QB), F32),
            jax.ShapeDtypeStruct((nb, 1, QB), F32),
            jax.ShapeDtypeStruct((nk, D), BF16),
            jax.ShapeDtypeStruct((D, nk), BF16),
            jax.ShapeDtypeStruct((nk, C), BF16),
        ),
        in_specs=[SMEM, whole(*kv.shape), whole(*tx.shape), block(per, HALF, D)],
        out_specs=(
            block(1, nk, QB),
            block(per, C // 2, D),
            block(1, C, QB),
            block(1, 1, QB),
            whole(nk, D),
            whole(D, nk),
            whole(nk, C),
        ),
        scratch_shapes=[pltpu.VMEM((C, nk), BF16), pltpu.VMEM((nk, QB), F32)],
        compiler_params=pltpu.CompilerParams(
            dimension_semantics=("arbitrary",), vmem_limit_bytes=LIMIT
        ),
        name="forward",
    )(guidance, kv, tx, q)


def own_tokens(x):
    a, b = pack_pair(x)
    return jnp.where(lax.axis_index("cfg") == 0, a, b)


def middle_kernel(
    S, NI, guidance, rate, msg, noise, old, reward,
    g_all, ratio, factor,
    got, g_own, part, parts, pair, rewards, s1, r1, s2, r2, ls, s3, r3, s4, r4, s5, r5,
):
    c, i, s = lax.axis_index("cfg"), lax.axis_index("img"), lax.axis_index("seq")
    barrier = pltpu.get_barrier_semaphore()

    def greet(k, carry):
        pl.semaphore_signal(
            barrier, inc=1, device_id={"seq": lax.rem(s + k, S)}, device_id_type=MESH
        )
        return carry

    lax.fori_loop(1, S, greet, 0)
    pl.semaphore_signal(barrier, inc=1, device_id={"cfg": 1 - c}, device_id_type=MESH)
    for k in range(1, NI):
        pl.semaphore_signal(
            barrier, inc=1, device_id={"img": lax.rem(i + k, NI)}, device_id_type=MESH
        )
    pl.semaphore_wait(barrier, S - 1 + 1 + NI - 1)

    def contribute(k, carry):
        t = lax.rem(s + k, S)
        away(msg.at[t], got.at[s], s1, r1, {"seq": t}).start()
        return carry

    lax.fori_loop(1, S, contribute, 0)
    for k in range(1, NI):
        away(reward, rewards.at[i], s5, r5, {"img": lax.rem(i + k, NI)}).start()
    noise_own = own_tokens(noise[...])
    old_own = own_tokens(old[...])
    drain(got.at[pl.ds(0, S - 1)], r1)
    got[s] = msg[s]
    guided = jnp.sum(got[...].astype(F32), axis=0)
    step = rate[0, 0]
    deviation = step * (guided - old_own)
    g_own[...] = (noise_own - deviation).astype(BF16)
    partial = jnp.sum(noise_own * deviation - 0.5 * deviation * deviation)
    part[...] = jnp.full(part.shape, partial, F32)
    mine = pltpu.make_async_copy(g_own, g_all.at[s], ls)
    mine.start()

    def share(k, carry):
        t = lax.rem(s + k, S)
        away(g_own, g_all.at[s], s2, r2, {"seq": t}).start()
        return carry

    lax.fori_loop(1, S, share, 0)

    def tell(k, carry):
        t = lax.rem(s + k, S)
        away(part, parts.at[s], s3, r3, {"seq": t}).start()
        return carry

    lax.fori_loop(1, S, tell, 0)
    drain(parts.at[pl.ds(0, S - 1)], r3)
    parts[s] = part[...]
    pair[0] = jnp.sum(parts[...], axis=0)
    swap = away(pair.at[0], pair.at[1], s4, r4, {"cfg": 1 - c})
    swap.start()
    if NI > 1:
        drain(rewards.at[pl.ds(0, NI - 1)], r5)
    rewards[i] = reward[...]
    mean = jnp.sum(rewards[...], axis=0) / NI
    square = jnp.sum(rewards[...] * rewards[...], axis=0) / NI
    spread_of = jnp.sqrt(jnp.maximum(square - mean * mean, 0.0))
    advantage = (reward[...] - mean) / jnp.maximum(spread_of, 1.0)
    swap.wait()
    log_ratio = (pair[0] + pair[1]) / (2 * S * HALF * C)
    ratio_now = jnp.exp(log_ratio)
    clipped = jnp.clip(ratio_now, 0.8, 1.2)
    keep = ratio_now * advantage <= clipped * advantage
    gain = jnp.where(keep, -ratio_now * advantage, 0.0)
    ratio[...] = ratio_now
    share_of = jnp.where(lax.rem(s, 2) == 0, guidance[0, 0], 1.0 - guidance[0, 0])
    factor[...] = gain * (step * share_of)
    mine.wait()
    drain(g_all.at[pl.ds(0, S - 1)], r2)
    drain(got.at[pl.ds(0, S - 1)], s1)
    drain(g_all.at[pl.ds(0, S - 1)], s2)
    drain(parts.at[pl.ds(0, S - 1)], s3)
    if NI > 1:
        drain(rewards.at[pl.ds(0, NI - 1)], s5)


def middle(S, NI, guidance, rate, msg, noise, old, reward):
    dma = pltpu.SemaphoreType.DMA
    tile = (8, D)
    return pl.pallas_call(
        functools.partial(middle_kernel, S, NI),
        out_shape=(
            jax.ShapeDtypeStruct((S, C // 2, D), BF16),
            jax.ShapeDtypeStruct(tile, F32),
            jax.ShapeDtypeStruct(tile, F32),
        ),
        in_specs=[SMEM, SMEM, VMEM, VMEM, VMEM, VMEM],
        out_specs=(ANY, VMEM, VMEM),
        scratch_shapes=[
            pltpu.VMEM((S, C // 2, D), BF16),
            pltpu.VMEM((C // 2, D), BF16),
            pltpu.VMEM(tile, F32),
            pltpu.VMEM((S, *tile), F32),
            pltpu.VMEM((2, *tile), F32),
            pltpu.VMEM((NI, *tile), F32),
            *([dma] * 11),
        ],
        compiler_params=pltpu.CompilerParams(collective_id=1, has_side_effects=True),
        name="middle",
    )(guidance, rate, msg, noise, old, reward)


def backward_kernel(
    S, factor, e_in, q, g, out_t, linv, keys_t, narrow,
    dq, own, oth, town, toth,
    gk, gv,
):
    nk = narrow.shape[0]
    step = pl.program_id(0)

    @pl.when(step == 0)
    def _():
        gk[...] = jnp.zeros_like(gk)
        gv[...] = jnp.zeros_like(gv)

    queries = q[...].reshape(QB, D)
    g_t = jnp.concatenate(
        [unpack_pair(g[2 * m].astype(F32), g[2 * m + 1].astype(F32)) for m in range(QB // D)], axis=1
    )
    gl_t = (g_t * linv[0]).astype(BF16)
    gl32 = gl_t.astype(F32)
    delta = jnp.sum(gl32 * out_t[0], axis=0, keepdims=True)
    gl_both = jnp.concatenate([gl32, gl32], axis=0).T.astype(BF16)
    dq_t = jnp.zeros((D, QB), F32)
    for at, size in chunks(nk):
        rows = slice(at, at + size)
        e = e_in[0, rows]
        gp = jnp.dot(narrow[rows], gl_t, preferred_element_type=F32)
        ds = (e.astype(F32) * (gp - delta)).astype(BF16)
        gv[rows] += jnp.dot(e, gl_both, preferred_element_type=F32)
        gk[rows] += jnp.dot(ds, queries, preferred_element_type=F32)
        dq_t = dq_t + jnp.dot(keys_t[:, rows], ds, preferred_element_type=F32)
    f = factor[0:1, 0:1]
    fs = f * D ** (-0.5)
    dq[...] = (dq_t * fs).T.astype(BF16).reshape(dq.shape)

    @pl.when(step == pl.num_programs(0) - 1)
    def _():
        third = HALF // 2
        n = third * S
        for p, out in ((0, own), (1, oth)):
            base = 2 * p * n
            for ab in range(2):
                rows = gk[base + ab * n : base + ab * n + n]
                out[:, third * ab : third * ab + third, :] = (rows * fs).astype(out.dtype).reshape(S, third, D)
            a, b = gv[base : base + n], gv[base + n : base + 2 * n]
            both = jnp.where(iota(a.shape, 1) < C, a, b) * f
            out[:, HALF:, :] = both.astype(out.dtype).reshape(S, third, D)
        H = S // 2
        for p, out in ((0, town), (1, toth)):
            base = 4 * n + p * H * TXT
            k = (gk[base : base + H * TXT] * fs).reshape(H, TXT, D)
            v = gv[base : base + H * TXT]
            v = (jnp.where(iota(v.shape, 1) < C, v, 0.0) * f).reshape(H, TXT, D)
            out[...] = jnp.concatenate([k, v], axis=1).astype(out.dtype)


def backward(S, factor, e, q, g, out_t, linv, keys_t, narrow):
    nb, nk, _ = e.shape
    H = S // 2
    per = QB // HALF
    whole = lambda *shape: pl.BlockSpec(shape, lambda i: (0,) * len(shape))
    block = lambda *shape: pl.BlockSpec(shape, lambda i: (i,) + (0,) * (len(shape) - 1))
    rows = HALF + HALF // 2
    return pl.pallas_call(
        functools.partial(backward_kernel, S),
        grid=(nb,),
        out_shape=(
            jax.ShapeDtypeStruct((S, HALF, D), BF16),
            jax.ShapeDtypeStruct((S, rows, D), F32),
            jax.ShapeDtypeStruct((S, rows, D), BF16),
            jax.ShapeDtypeStruct((H, 2 * TXT, D), F32),
            jax.ShapeDtypeStruct((H, 2 * TXT, D), BF16),
        ),
        in_specs=[
            whole(8, D),
            block(1, nk, QB),
            block(per, HALF, D),
            block(per, C // 2, D),
            block(1, C, QB),
            block(1, 1, QB),
            whole(D, nk),
            whole(nk, C),
        ],
        out_specs=(
            block(per, HALF, D),
            whole(S, rows, D),
            whole(S, rows, D),
            whole(H, 2 * TXT, D),
            whole(H, 2 * TXT, D),
        ),
        scratch_shapes=[pltpu.VMEM((nk, D), F32), pltpu.VMEM((nk, D), F32)],
        compiler_params=pltpu.CompilerParams(
            dimension_semantics=("arbitrary",), vmem_limit_bytes=LIMIT
        ),
        name="backward",
    )(factor, e, q, g, out_t, linv, keys_t, narrow)


def home_kernel(
    S, NI, dq, own, oth, town, toth, img, tx, rt,
    grad, tgrad, rg,
    vbuf, xu, xk, xt, uf, kf, tf, ub, tb, dv, rgp, r1, a1, r2, a2, r3, a3, r4,
    vsem, dvsem, xs, xr, us, ur, ts, tr, qs, qr, ks, kr, as_, ar, ls,
):
    H = S // 2
    ZN = S // YN
    NP = 2 * NI
    HD = rgp.shape[1]
    W = HD // NP
    third = HALF // 2
    c, i, s = lax.axis_index("cfg"), lax.axis_index("img"), lax.axis_index("seq")
    head, branch = s // 2, lax.rem(s, 2)
    y, z = lax.rem(s, YN), s // YN
    me = 2 * i + c
    barrier = signal_plane(S)
    for k in range(1, NI):
        for core in range(2):
            pl.semaphore_signal(
                barrier,
                inc=1,
                device_id={"cfg": core, "img": lax.rem(i + k, NI)},
                device_id_type=MESH,
            )
    vcopy = pltpu.make_async_copy(img.at[2], vbuf, vsem)
    vcopy.start()
    pl.semaphore_wait(barrier, 2 * S - 1 + 2 * (NI - 1))
    other = {"cfg": 1 - c}
    swaps = [
        away(oth.at[:, pl.ds(HALF, third)], xu, xs.at[0], xr.at[0], other),
        away(toth, xt, xs.at[1], xr.at[1], other),
        away(oth.at[:, pl.ds(0, HALF)], xk, xs.at[2], xr.at[2], other),
    ]
    for w in swaps:
        w.start()
    cols = pl.ds(pl.multiple_of(head * D, D), D)
    mine = pl.ds(pl.multiple_of(HALF * c, HALF), HALF)
    swaps[0].wait_recv()
    uf[...] = (own[:, HALF:, :] + xu[...].astype(F32)).astype(BF16)
    swaps[1].wait_recv()
    tf[...] = (town[...] + xt[...].astype(F32)).astype(BF16)

    def send_u(k, carry):
        t = lax.rem(s + k, S)
        put(uf.at[t], ub.at[head, c], us, ur, branch, t)
        return carry

    lax.fori_loop(0, S, send_u, 0)

    def send_text(k, carry):
        put(tf.at[k], tb.at[head], ts, tr, branch, c * H + k)
        return carry

    lax.fori_loop(0, H, send_text, 0)

    def send_queries(k, carry):
        t = lax.rem(s + k, S)
        put(dq.at[t], grad.at[0, mine, cols], qs, qr, branch, t)
        return carry

    lax.fori_loop(0, S, send_queries, 0)
    swaps[2].wait_recv()
    kf[...] = (own[:, :HALF, :] + xk[...].astype(F32)).astype(BF16)

    def send_keys(k, carry):
        t = lax.rem(s + k, S)
        put(kf.at[t], grad.at[1, mine, cols], ks, kr, branch, t)
        return carry

    lax.fori_loop(0, S, send_keys, 0)
    vcopy.wait()
    drain(ub, ur)
    drain(tb, tr)

    def widen(h, carry):
        at = pl.ds(pl.multiple_of(h * D, D), D)
        r = rt[:, at]
        twice = jnp.concatenate([r, r], axis=0)
        low = iota((third, D), 1) < C
        u0, u1 = ub[h, 0].astype(F32), ub[h, 1].astype(F32)
        t = tb[h].astype(F32)
        text = jnp.where(iota(t.shape, 0) < TXT, 0.0, t)
        spaced = jnp.concatenate(
            [
                jnp.where(low, u0, 0.0),
                jnp.where(low, 0.0, u0),
                jnp.where(low, u1, 0.0),
                jnp.where(low, 0.0, u1),
                text,
            ],
            axis=0,
        )
        wide = jnp.dot(spaced.astype(BF16), twice, preferred_element_type=F32)
        dv[:, at] = wide[: 2 * HALF].astype(BF16)
        tgrad[:, at] = jnp.where(iota(t.shape, 0) < TXT, t, wide[2 * HALF :]).astype(BF16)
        values = jnp.concatenate([vbuf[:, at], tx[:, at]], axis=0)
        res = jnp.dot(spaced.T.astype(BF16), values, preferred_element_type=F32)
        rgp[:, at] = res[:C] + res[C:]
        return carry

    lax.fori_loop(0, H, widen, 0)
    dvcopy = pltpu.make_async_copy(dv, grad.at[2], dvsem)
    dvcopy.start()

    def peers():
        for k in range(1, NP):
            p = lax.rem(me + k, NP)
            yield p, {"cfg": lax.rem(p, 2), "img": p // 2}

    def piece(p):
        return pl.ds(pl.multiple_of(p * W, D), W)

    for p, device in peers():
        away(rgp.at[:, piece(p)], r1.at[me], as_.at[0], ar.at[0], device).start()
    drain(r1.at[pl.ds(0, NP - 1)], ar.at[0])
    r1[me] = rgp[:, piece(me)]
    a1[...] = jnp.sum(r1[...], axis=0)
    RY = C // YN

    def strip(n):
        return pl.ds(pl.multiple_of(n * RY, 8), RY)

    for k in range(1, YN):
        n = lax.rem(y + k, YN)
        away(a1.at[strip(n)], r2.at[y], as_.at[1], ar.at[1], {"seq": z * YN + n}).start()
    drain(r2.at[pl.ds(0, YN - 1)], ar.at[1])
    r2[y] = a1[strip(y), :]
    a2[...] = jnp.sum(r2[...], axis=0)
    for k in range(1, ZN):
        n = lax.rem(z + k, ZN)
        away(a2, r3.at[z], as_.at[2], ar.at[2], {"seq": n * YN + y}).start()
    drain(r3.at[pl.ds(0, ZN - 1)], ar.at[2])
    r3[z] = a2[...]
    a3[...] = jnp.sum(r3[...], axis=0)
    for k in range(1, YN):
        n = lax.rem(y + k, YN)
        away(a3, r4.at[y], as_.at[3], ar.at[3], {"seq": z * YN + n}).start()
    drain(r4.at[pl.ds(0, YN - 1)], ar.at[3])
    r4[y] = a3[...]
    keep = pltpu.make_async_copy(r4, rg.at[:, :, piece(me)], ls)
    keep.start()
    for p, device in peers():
        away(r4, rg.at[:, :, piece(me)], as_.at[4], ar.at[4], device).start()

    keep.wait()
    drain(r1.at[pl.ds(0, NP - 1)], ar.at[4])
    dvcopy.wait()
    drain(grad.at[0], qr)
    drain(grad.at[1], kr)
    for w in swaps:
        w.wait_send()
    drain(r1.at[pl.ds(0, NP - 1)], as_.at[0])
    drain(r2.at[pl.ds(0, YN - 1)], as_.at[1])
    drain(r3.at[pl.ds(0, ZN - 1)], as_.at[2])
    drain(r4.at[pl.ds(0, YN - 1)], as_.at[3])
    drain(r1.at[pl.ds(0, NP - 1)], as_.at[4])

    text_here = jnp.logical_and(branch == c, s // H == c)

    @pl.when(branch == c)
    def _():
        drain(uf.at[pl.ds(0, S - 1)], us)
        drain(dq.at[pl.ds(0, S - 1)], qs)
        drain(kf.at[pl.ds(0, S - 1)], ks)

    @pl.when(branch != c)
    def _():
        drain(uf, us)
        drain(dq, qs)
        drain(kf, ks)

    @pl.when(text_here)
    def _():
        drain(tf.at[pl.ds(0, H - 1)], ts)

    @pl.when(jnp.logical_not(text_here))
    def _():
        drain(tf, ts)


def home(S, NI, dq, own, oth, town, toth, img, tx, rt):
    H = S // 2
    HD = rt.shape[1]
    NP = 2 * NI
    W = HD // NP
    RY = C // YN
    third = HALF // 2
    dma = pltpu.SemaphoreType.DMA
    return pl.pallas_call(
        functools.partial(home_kernel, S, NI),
        out_shape=(
            jax.ShapeDtypeStruct(img.shape, BF16),
            jax.ShapeDtypeStruct((2 * TXT, HD), BF16),
            jax.ShapeDtypeStruct((YN, RY, HD), F32),
        ),
        in_specs=[ANY, VMEM, ANY, VMEM, ANY, ANY, VMEM, VMEM],
        out_specs=(ANY, VMEM, ANY),
        scratch_shapes=[
            pltpu.VMEM(img.shape[1:], BF16),
            pltpu.VMEM((S, third, D), BF16),
            pltpu.VMEM((S, HALF, D), BF16),
            pltpu.VMEM((H, 2 * TXT, D), BF16),
            pltpu.VMEM((S, third, D), BF16),
            pltpu.VMEM((S, HALF, D), BF16),
            pltpu.VMEM((H, 2 * TXT, D), BF16),
            pltpu.VMEM((H, 2, third, D), BF16),
            pltpu.VMEM((H, 2 * TXT, D), BF16),
            pltpu.VMEM(img.shape[1:], BF16),
            pltpu.VMEM((C, HD), F32),
            pltpu.VMEM((NP, C, W), F32),
            pltpu.VMEM((C, W), F32),
            pltpu.VMEM((YN, RY, W), F32),
            pltpu.VMEM((RY, W), F32),
            pltpu.VMEM((S // YN, RY, W), F32),
            pltpu.VMEM((RY, W), F32),
            pltpu.VMEM((YN, RY, W), F32),
            dma,
            dma,
            dma((3,)),
            dma((3,)),
            *([dma] * 8),
            dma((5,)),
            dma((5,)),
            dma,
        ],
        compiler_params=pltpu.CompilerParams(
            collective_id=2, has_side_effects=True, vmem_limit_bytes=LIMIT
        ),
        name="home",
    )(dq, own, oth, town, toth, img, tx, rt)


def on_device(S, NI, img_qkv, txt_kv, readout, old_velocity, noise, step_ratio, rewards, guidance):
    img = img_qkv[0, 0].transpose(1, 0, 2)
    text = txt_kv[0, 0]
    tx = jnp.concatenate([text[:, 0], text[:, 1]], axis=0)
    rt = readout.T
    scalar = lambda x: x.reshape(1, 1)
    kv, q, txo = spread(S, img, tx, rt)
    e, msg, out_t, linv, keys, keys_t, narrow = forward(S, scalar(guidance), kv, txo, q)
    reward = jnp.broadcast_to(scalar(rewards), (8, D))
    g, ratio, factor = middle(
        S, NI, scalar(guidance), scalar(step_ratio), msg, noise[0].T, old_velocity[0].T, reward
    )
    dq, own, oth, town, toth = backward(S, factor, e, q, g, out_t, linv, keys_t, narrow)
    grad, tgrad, rg = home(S, NI, dq, own, oth, town, toth, img, tx, rt)
    img_grad = grad.transpose(1, 0, 2)[None, None]
    txt_grad = jnp.stack([tgrad[:TXT], tgrad[TXT:]], axis=1)[None, None]
    return (img_grad, txt_grad, rg.reshape(C, -1).T, ratio[0, :1])


def solution(mesh):
    S, NI = mesh.shape["seq"], mesh.shape["img"]
    placed = (
        P("cfg", "img", "seq", None, None),
        P("cfg", "img", "seq", None, None),
        P(),
        P("img", "seq", None),
        P("img", "seq", None),
        P("img"),
        P("img"),
        P(),
    )
    return jax.shard_map(
        functools.partial(on_device, S, NI),
        mesh=mesh,
        in_specs=placed,
        out_specs=(
            P("cfg", "img", "seq", None, None),
            P("cfg", "img", "seq", None, None),
            P(),
            P("img"),
        ),
        check_vma=False,
    )
```

```python
import functools

import jax
import jax.numpy as jnp
from jax import lax
from jax.experimental import pallas as pl
from jax.experimental.pallas import tpu as pltpu
from jax.sharding import PartitionSpec as P

D = 128
C = 64
HALF = 64
TXT = 8
YN = 4
QB = 256
KB = 1024
SB = 256
ONES = 16
MESH = pl.DeviceIdType.MESH
F32 = jnp.float32
BF16 = jnp.bfloat16
NT = (((1,), (1,)), ((), ()))
TN = (((0,), (0,)), ((), ()))
ANY = pl.BlockSpec(memory_space=pl.ANY)
VMEM = pl.BlockSpec(memory_space=pltpu.VMEM)
SMEM = pl.BlockSpec(memory_space=pltpu.SMEM)
LIMIT = 60 * 1024 * 1024


def iota(shape, dim):
    return lax.broadcasted_iota(jnp.int32, shape, dim)


def put(src, dst, send, recv, core, chip):
    here = jnp.logical_and(core == lax.axis_index("cfg"), chip == lax.axis_index("seq"))

    @pl.when(here)
    def _():
        pltpu.make_async_copy(src, dst, recv).start()

    @pl.when(jnp.logical_not(here))
    def _():
        away(src, dst, send, recv, {"cfg": core, "seq": chip}).start()


def away(src, dst, send, recv, device):
    return pltpu.make_async_remote_copy(
        src_ref=src,
        dst_ref=dst,
        send_sem=send,
        recv_sem=recv,
        device_id=device,
        device_id_type=MESH,
    )


def drain(ref, sem):
    pltpu.make_async_copy(ref, ref, sem).wait()


def signal_plane(chips):
    c, s = lax.axis_index("cfg"), lax.axis_index("seq")
    barrier = pltpu.get_barrier_semaphore()

    def one(k, carry):
        n = lax.rem(c * chips + s + k, 2 * chips)
        pl.semaphore_signal(
            barrier,
            inc=1,
            device_id={"cfg": n // chips, "seq": lax.rem(n, chips)},
            device_id_type=MESH,
        )
        return carry

    lax.fori_loop(1, 2 * chips, one, 0)
    return barrier


def pack_pair(x):
    top, low = x[: C // 2], x[C // 2 :]
    lower = iota(top.shape, 1) < HALF
    return (
        jnp.where(lower, top, pltpu.roll(low, HALF, 1)),
        jnp.where(lower, pltpu.roll(top, HALF, 1), low),
    )


def unpack_pair(a, b):
    lower = iota(a.shape, 1) < HALF
    return jnp.concatenate(
        [jnp.where(lower, a, pltpu.roll(b, HALF, 1)), jnp.where(lower, pltpu.roll(a, HALF, 1), b)], axis=0
    )


def own_tokens(x):
    a, b = pack_pair(x)
    return jnp.where(lax.axis_index("cfg") == 0, a, b)


def step_kernel(
    S, NI, guidance, rate, img, tx, rt, noise, old, reward,
    grad, tgrad, rg, ratio,
    vbuf, vrp, txb, kv, text, qbuf, keys, keys_t, narrow, narrow_t, scores_a, scores_b, hold_0, hold_1, hold_2, hold_3, hold_text, weights, out_t, linv,
    msg, got, g_own, g_all, part, parts, pair, rewards, gl, delta, gk, gv,
    uo, xu, uf, uto, xut, utf, ko, xk, kf, kto, xkt, ktf, dqb, ub, utb, ktb, dv, rgp, r1, a1, r2, a2, r3, a3, r4,
    vsem, ks, kr, qs, qr, ts, tr, fs, fr, fts, ftr, ms, mr, gs, gr, ps, pr, pairs, pairr, rs, rr,
    xs, xr, us, ur, uts, utr, dqs, dqr, dks, dkr, kts, ktr, dvsem, as_, ar, ls,
):
    H = S // 2
    ZN = S // YN
    NP = 2 * NI
    W = rgp.shape[1] // NP
    RY = C // YN
    NK = keys.shape[0]
    NKI = 2 * HALF * S
    holds = (hold_0, hold_1, hold_2, hold_3)[: min(KB, NKI) // SB]
    third = HALF // 2
    n3 = third * S
    c, i, s = lax.axis_index("cfg"), lax.axis_index("img"), lax.axis_index("seq")
    head, branch = s // 2, lax.rem(s, 2)
    y, z = lax.rem(s, YN), s // YN
    me = 2 * i + c
    other = {"cfg": 1 - c}

    vcopy = pltpu.make_async_copy(img.at[2], vbuf, vsem)
    vcopy.start()
    barrier = signal_plane(S)
    for k in range(1, NI):
        for core in range(2):
            pl.semaphore_signal(
                barrier, inc=1, device_id={"cfg": core, "img": lax.rem(i + k, NI)}, device_id_type=MESH
            )
    vcopy.wait()

    def squeeze(h, carry):
        cols = pl.ds(pl.multiple_of(h * D, D), D)
        r = rt[:, cols]
        twice = jnp.concatenate([r, r], axis=0)
        x = lax.dot_general(vbuf[:, cols], twice, NT, preferred_element_type=F32)
        low = iota((third, D), 1) < C
        for j in range(2):
            first = x[HALF * j : HALF * j + third]
            second = x[HALF * j + third : HALF * j + HALF]
            vrp[h, j] = jnp.where(low, first, second).astype(BF16)
        t = tx[:, cols]
        yv = lax.dot_general(t, twice, NT, preferred_element_type=F32)
        yv = jnp.where(iota(yv.shape, 1) < C, yv, 0.0)
        txb[h] = jnp.where(iota(yv.shape, 0) < TXT, t.astype(F32), yv).astype(BF16)
        return carry

    lax.fori_loop(0, H, squeeze, 0)
    pl.semaphore_wait(barrier, 2 * S - 1 + 2 * (NI - 1))

    side = s // H

    def at_distance(n, sign):
        far = (n + 1) // 2
        return lax.rem(z + jnp.where(lax.rem(n, 2) == 1, sign * far, -sign * far) + ZN, ZN)

    def send_keys(k, carry):
        zt = at_distance(k // 2, 1)
        h = 2 * zt + lax.rem(k, 2)
        chip = 2 * h + c
        cols = pl.ds(pl.multiple_of(h * D, D), D)
        for j in range(2):
            put(img.at[1, pl.ds(HALF * j, HALF), cols], kv.at[0, s, pl.ds(0, HALF)], ks.at[h, j], kr.at[s], j, chip)
            put(vrp.at[h, j], kv.at[0, s, pl.ds(HALF, third)], ks.at[h, j], kr.at[s], j, chip)
        put(txb.at[h], text.at[0, lax.rem(s, H)], ts.at[h], tr.at[lax.rem(s, H)], side, chip)
        return carry

    lax.fori_loop(0, H, send_keys, 0)

    def send_queries(k, carry):
        zt = at_distance(k // 2, 1)
        h = 2 * zt + lax.rem(k, 2)
        chip = 2 * h + c
        cols = pl.ds(pl.multiple_of(h * D, D), D)
        for j in range(2):
            put(img.at[0, pl.ds(HALF * j, HALF), cols], qbuf.at[s], qs.at[h, j], qr.at[s], j, chip)
        return carry

    lax.fori_loop(0, H, send_queries, 0)
    for k in range(1, NI):
        away(reward, rewards.at[i], rs, rr, {"img": lax.rem(i + k, NI)}).start()

    narrow_t[C:] = jnp.where(iota((ONES, NK), 0) == 0, 1.0, 0.0).astype(BF16)

    def lay_out(p, zs):
        four = pl.ds(zs * YN, YN)
        packed = kv[p, four, HALF:, :].reshape(third * YN, D)
        turned = packed.astype(F32).T
        for ab in range(2):
            rows = pl.ds(pl.multiple_of((2 * p + ab) * n3 + zs * (third * YN), third * YN), third * YN)
            block = kv[p, four, third * ab : third * ab + third, :].reshape(third * YN, D)
            keys[rows, :D] = block
            keys[rows, D:] = block
            keys_t[:, rows] = block.astype(F32).T.astype(BF16)
            one = turned[C * ab : C * ab + C]
            narrow_t[:C, rows] = one.astype(BF16)
            narrow[rows] = jnp.concatenate([one, one], axis=0).T.astype(BF16)

    def arrive(n, carry):
        zs = at_distance(n, -1)
        for yy in range(YN):
            src = zs * YN + yy
            drain(kv.at[0, src], kr.at[src])
            away(kv.at[0, src], kv.at[1, src], fs.at[src], fr.at[src], other).start()
        lay_out(0, zs)
        return carry

    lax.fori_loop(0, ZN, arrive, 0)

    def arrive_text(k, carry):
        drain(text.at[0, k], tr.at[k])
        away(text.at[0, k], text.at[1, k], fts.at[k], ftr.at[k], other).start()
        return carry

    lax.fori_loop(0, H, arrive_text, 0)

    def arrive_other(n, carry):
        zs = at_distance(n, -1)
        for yy in range(YN):
            drain(kv.at[1, zs * YN + yy], fr.at[zs * YN + yy])
        lay_out(1, zs)
        return carry

    lax.fori_loop(0, ZN, arrive_other, 0)

    def arrive_other_text(k, carry):
        drain(text.at[1, k], ftr.at[k])
        return carry

    lax.fori_loop(0, H, arrive_other_text, 0)
    words = text[...].astype(F32)
    tk = words[:, :, :TXT, :].reshape(TXT * S, D)
    tv = words[:, :, TXT:, :].reshape(TXT * S, D)
    last = pl.ds(NKI, TXT * S)
    keys[last, :D] = tk.astype(BF16)
    keys[last, D:] = tk.astype(BF16)
    keys_t[:, last] = tk.T.astype(BF16)
    tvt = tv.T[:C]
    narrow_t[:C, last] = tvt.astype(BF16)
    narrow[last] = jnp.concatenate([tvt, tvt], axis=0).T.astype(BF16)

    def over_keys(body, carry):
        for at in range(0, NK, SB):
            carry = body(slice(at, min(at + SB, NK)), carry)
        return carry

    def queries_t(zs):
        for yy in range(YN):
            drain(qbuf.at[zs * YN + yy], qr.at[zs * YN + yy])
        x = qbuf[pl.ds(zs * YN, YN)].reshape(QB, D).astype(F32).T * (D ** (-0.5) * 1.4426950408889634)
        hi = x.astype(BF16)
        return jnp.concatenate([hi, (x - hi.astype(F32)).astype(BF16)], axis=0)

    def score(buf, rows, q_t, top):
        st = jnp.dot(keys[rows], q_t, preferred_element_type=F32)
        buf[rows] = st
        return jnp.maximum(top, jnp.max(st.reshape(st.shape[0] // 8, 8, QB), axis=0))

    def weigh(buf, zs, rows, top, hold):
        e = jnp.exp2(buf[rows] - top).astype(BF16)
        weights[zs, rows] = e
        hold[...] = e

    def mix(rows, hold, mixed):
        return mixed + jnp.dot(narrow_t[:, rows], hold[...], preferred_element_type=F32)

    low_top = jnp.full((8, QB), -jnp.inf, F32)
    no_mix = jnp.zeros((C + ONES, QB), F32)
    branch_share = jnp.where(branch == 0, guidance[0, 0], 1.0 - guidance[0, 0])
    parts_of = NKI // KB
    subs = KB // SB

    def chunk(k, sub):
        return pl.ds(pl.multiple_of(k * KB + sub * SB, SB), SB)

    def first_scores(q_t):
        def body(k, t):
            for sub in range(subs):
                t = score(scores_a, chunk(k, sub), q_t, t)
            return t

        return score(scores_a, last, q_t, lax.fori_loop(0, parts_of, body, low_top))

    def attend(n, now, then, top8, ahead):
        zs = at_distance(n, -1)
        top = jnp.max(top8, axis=0, keepdims=True)
        q_t = queries_t(at_distance(n + 1, -1)) if ahead else None
        next8 = score(then, last, q_t, low_top) if ahead else low_top
        weigh(now, zs, last, top, hold_text)
        mixed = mix(last, hold_text, no_mix)
        holds[subs - 1][...] = jnp.zeros((SB, QB), BF16)

        def body(k, carry):
            next8, mixed = carry
            for sub in range(subs):
                before = chunk(jnp.maximum(k - 1, 0), subs - 1) if sub == 0 else chunk(k, sub - 1)
                mixed = mix(before, holds[sub - 1], mixed)
                if ahead:
                    next8 = score(then, chunk(k, sub), q_t, next8)
                weigh(now, zs, chunk(k, sub), top, holds[sub])
            return next8, mixed

        next8, mixed = lax.fori_loop(0, parts_of, body, (next8, mixed))
        mixed = mix(chunk(parts_of - 1, subs - 1), holds[subs - 1], mixed)
        inverse = 1.0 / mixed[C : C + 1]
        linv[zs] = inverse
        normal = mixed[:C] * inverse
        out_t[zs] = normal
        for m in range(QB // D):
            a, b = pack_pair(normal[:, D * m : D * m + D] * branch_share)
            for yy, part_of in ((2 * m, a), (2 * m + 1, b)):
                msg[zs * YN + yy] = part_of.astype(BF16)
        for yy in range(YN):
            t = zs * YN + yy
            put(msg.at[t], got.at[s], ms, mr, c, t)
        return next8

    top = first_scores(queries_t(at_distance(0, -1)))

    def two(m, top):
        top = attend(2 * m, scores_a, scores_b, top, True)
        return attend(2 * m + 1, scores_b, scores_a, top, True)

    top = lax.fori_loop(0, ZN // 2 - 1, two, top)
    if ZN > 1:
        top = attend(ZN - 2, scores_a, scores_b, top, True)
        attend(ZN - 1, scores_b, scores_a, top, False)
    else:
        attend(0, scores_a, scores_b, top, False)

    noise_own = own_tokens(noise[...])
    old_own = own_tokens(old[...])
    drain(got, mr)
    guided = jnp.sum(got[...].astype(F32), axis=0)
    step = rate[0, 0]
    deviation = step * (guided - old_own)
    g_own[...] = (noise_own - deviation).astype(BF16)

    def share(k, carry):
        t = at_distance(k // YN, 1) * YN + lax.rem(y + k, YN)
        put(g_own, g_all.at[s], gs, gr.at[s], c, t)
        return carry

    lax.fori_loop(0, S, share, 0)
    partial = jnp.sum(noise_own * deviation - 0.5 * deviation * deviation)
    part[...] = jnp.full(part.shape, partial, F32)

    def tell(k, carry):
        put(part, parts.at[s], ps, pr, c, lax.rem(s + k, S))
        return carry

    lax.fori_loop(0, S, tell, 0)

    gv[...] = jnp.zeros_like(gv)
    gk[...] = jnp.zeros_like(gk)

    def narrow_grads(n, carry):
        zs = at_distance(n, -1)
        for yy in range(YN):
            drain(g_all.at[zs * YN + yy], gr.at[zs * YN + yy])
        g_t = jnp.concatenate(
            [
                unpack_pair(g_all[zs * YN + 2 * m].astype(F32), g_all[zs * YN + 2 * m + 1].astype(F32))
                for m in range(QB // D)
            ],
            axis=1,
        )
        g_t = g_t * linv[zs]
        hi = g_t.astype(BF16)
        lo = (g_t - hi.astype(F32)).astype(BF16)
        gl[zs] = jnp.concatenate([hi, lo], axis=0)
        delta[zs] = jnp.sum((hi.astype(F32) + lo.astype(F32)) * out_t[zs], axis=0, keepdims=True)
        hi32 = hi.astype(F32)
        cols = jnp.concatenate([hi32, hi32], axis=0).T.astype(BF16)

        def one(rows, cr):
            gv[rows] += jnp.dot(weights[zs, rows], cols, preferred_element_type=F32)
            return cr

        return over_keys(one, carry)

    lax.fori_loop(0, ZN, narrow_grads, 0)

    drain(parts, pr)
    pair[0] = jnp.sum(parts[...], axis=0)
    swap = away(pair.at[0], pair.at[1], pairs, pairr, other)
    swap.start()
    if NI > 1:
        drain(rewards.at[pl.ds(0, NI - 1)], rr)
    rewards[i] = reward[...]
    mean = jnp.sum(rewards[...], axis=0) / NI
    square = jnp.sum(rewards[...] * rewards[...], axis=0) / NI
    deviates = jnp.sqrt(jnp.maximum(square - mean * mean, 0.0))
    advantage = (reward[...] - mean) / jnp.maximum(deviates, 1.0)
    swap.wait()
    ratio_now = jnp.exp((pair[0] + pair[1]) / (2 * S * HALF * C))
    clipped = jnp.clip(ratio_now, 0.8, 1.2)
    keep = ratio_now * advantage <= clipped * advantage
    gain = jnp.where(keep, -ratio_now * advantage, 0.0)
    ratio[...] = ratio_now
    f = (gain * (step * branch_share))[0:1, :]
    fscale = f * D ** (-0.5)

    def paired(p):
        base = 2 * p * n3
        a, b = gv[base : base + n3], gv[base + n3 : base + 2 * n3]
        return (jnp.where(iota(a.shape, 1) < C, a, b) * f).reshape(S, third, D)

    def text_values(p):
        v = gv[NKI + p * H * TXT : NKI + (p + 1) * H * TXT]
        v = (jnp.where(iota(v.shape, 1) < C, v, 0.0) * f).reshape(H, TXT, D)
        return jnp.concatenate([jnp.zeros_like(v), v], axis=1)

    uo[...] = paired(1).astype(BF16)
    uto[...] = text_values(1).astype(BF16)
    swaps = [
        away(uo, xu, xs.at[0], xr.at[0], other),
        away(uto, xut, xs.at[1], xr.at[1], other),
        away(ko, xk, xs.at[2], xr.at[2], other),
        away(kto, xkt, xs.at[3], xr.at[3], other),
    ]
    swaps[0].start()
    swaps[1].start()
    cols_home = pl.ds(pl.multiple_of(head * D, D), D)
    mine = pl.ds(pl.multiple_of(HALF * c, HALF), HALF)

    def send_narrow():
        swaps[0].wait_recv()
        uf[...] = (paired(0) + xu[...].astype(F32)).astype(BF16)
        swaps[1].wait_recv()
        utf[...] = (text_values(0) + xut[...].astype(F32)).astype(BF16)

        def one(k, carry):
            t = at_distance(k // YN, 1) * YN + lax.rem(y + k, YN)
            put(uf.at[t], ub.at[head, c], us, ur, branch, t)
            return carry

        lax.fori_loop(0, S, one, 0)

        def one_text(k, carry):
            put(utf.at[k], utb.at[head], uts, utr, branch, c * H + k)
            return carry

        lax.fori_loop(0, H, one_text, 0)

    def widen_all():
        drain(ub, ur)
        drain(utb, utr)

        def widen(h, carry):
            at = pl.ds(pl.multiple_of(h * D, D), D)
            r = rt[:, at]
            twice = jnp.concatenate([r, r], axis=0)
            low = iota((third, D), 1) < C
            u0, u1 = ub[h, 0].astype(F32), ub[h, 1].astype(F32)
            spaced = jnp.concatenate(
                [
                    jnp.where(low, u0, 0.0),
                    jnp.where(low, 0.0, u0),
                    jnp.where(low, u1, 0.0),
                    jnp.where(low, 0.0, u1),
                    utb[h].astype(F32),
                ],
                axis=0,
            )
            wide = jnp.dot(spaced.astype(BF16), twice, preferred_element_type=F32)
            dv[:, at] = wide[: 2 * HALF].astype(BF16)
            tgrad[:, at] = wide[2 * HALF :].astype(BF16)
            values = jnp.concatenate([vbuf[:, at], tx[:, at]], axis=0)
            res = jnp.dot(spaced.T.astype(BF16), values, preferred_element_type=F32)
            rgp[:, at] = res[:C] + res[C:]
            return carry

        lax.fori_loop(0, H, widen, 0)
        pltpu.make_async_copy(dv, grad.at[2], dvsem).start()

    def peers():
        for k in range(1, NP):
            p = lax.rem(me + k, NP)
            yield p, {"cfg": lax.rem(p, 2), "img": p // 2}

    def piece(p):
        return pl.ds(pl.multiple_of(p * W, D), W)

    def strip(n):
        return pl.ds(pl.multiple_of(n * RY, 8), RY)

    def readout_1():
        for p, device in peers():
            away(rgp.at[:, piece(p)], r1.at[me], as_.at[0], ar.at[0], device).start()

    def readout_2():
        drain(r1.at[pl.ds(0, NP - 1)], ar.at[0])
        r1[me] = rgp[:, piece(me)]
        a1[...] = jnp.sum(r1[...], axis=0)
        for k in range(1, YN):
            n = lax.rem(y + k, YN)
            away(a1.at[strip(n)], r2.at[y], as_.at[1], ar.at[1], {"seq": z * YN + n}).start()

    def readout_3():
        drain(r2.at[pl.ds(0, YN - 1)], ar.at[1])
        r2[y] = a1[strip(y), :]
        a2[...] = jnp.sum(r2[...], axis=0)
        for k in range(1, ZN):
            n = lax.rem(z + k, ZN)
            away(a2, r3.at[z], as_.at[2], ar.at[2], {"seq": n * YN + y}).start()

    def readout_4():
        if ZN > 1:
            drain(r3.at[pl.ds(0, ZN - 1)], ar.at[2])
        r3[z] = a2[...]
        a3[...] = jnp.sum(r3[...], axis=0)
        for k in range(1, YN):
            n = lax.rem(y + k, YN)
            away(a3, r4.at[y], as_.at[3], ar.at[3], {"seq": z * YN + n}).start()

    def readout_5():
        drain(r4.at[pl.ds(0, YN - 1)], ar.at[3])
        r4[y] = a3[...]
        pltpu.make_async_copy(r4, rg.at[:, :, piece(me)], ls).start()
        for p, device in peers():
            away(r4, rg.at[:, :, piece(me)], as_.at[4], ar.at[4], device).start()

    steps = dict(
        send_narrow=send_narrow, widen_all=widen_all, readout_1=readout_1, readout_2=readout_2,
        readout_3=readout_3, readout_4=readout_4, readout_5=readout_5,
    )

    def key_grads(n, carry):
        zs = at_distance(n, -1)
        block = qbuf[pl.ds(zs * YN, YN)].reshape(QB, D)
        g_t = gl[zs]
        shift = delta[zs]

        def one(rows, dq_t):
            gp = jnp.dot(narrow[rows], g_t, preferred_element_type=F32)
            ds = (weights[zs, rows].astype(F32) * (gp - shift)).astype(BF16)
            gk[rows] += jnp.dot(ds, block, preferred_element_type=F32)
            return dq_t + jnp.dot(keys_t[:, rows], ds, preferred_element_type=F32)

        dq_t = over_keys(one, jnp.zeros((D, QB), F32))
        dqb[pl.ds(zs * YN, YN)] = (dq_t.T * fscale).astype(BF16).reshape(YN, HALF, D)
        for yy in range(YN):
            t = zs * YN + yy
            put(dqb.at[t], grad.at[0, mine, cols_home], dqs, dqr, branch, t)
        for at, what in EVENTS:
            pl.when(n == min(at, ZN - 1))(steps[what])
        return carry

    lax.fori_loop(0, ZN, key_grads, 0)

    def image_keys(p):
        base = 2 * p * n3
        a = gk[base : base + n3].reshape(S, third, D)
        b = gk[base + n3 : base + 2 * n3].reshape(S, third, D)
        return jnp.concatenate([a, b], axis=1) * fscale

    def text_keys(p):
        k = gk[NKI + p * H * TXT : NKI + (p + 1) * H * TXT]
        k = (k * fscale).reshape(H, TXT, D)
        return jnp.concatenate([k, jnp.zeros_like(k)], axis=1)

    ko[...] = image_keys(1).astype(BF16)
    swaps[2].start()
    kto[...] = text_keys(1).astype(BF16)
    swaps[3].start()
    swaps[2].wait_recv()
    kf[...] = (image_keys(0) + xk[...].astype(F32)).astype(BF16)

    def send_key_grads(k, carry):
        t = at_distance(k // YN, 1) * YN + lax.rem(y + k, YN)
        put(kf.at[t], grad.at[1, mine, cols_home], dks, dkr, branch, t)
        return carry

    lax.fori_loop(0, S, send_key_grads, 0)
    swaps[3].wait_recv()
    ktf[...] = (text_keys(0) + xkt[...].astype(F32)).astype(BF16)

    def send_text_keys(k, carry):
        put(ktf.at[k], ktb.at[head], kts, ktr, branch, c * H + k)
        return carry

    lax.fori_loop(0, H, send_text_keys, 0)

    def sent(k, carry):
        chip = 2 * k + c
        for odd in range(2):
            src = 2 * k + odd
            drain(kv.at[1, src], fs.at[src])
        drain(text.at[1, k], fts.at[k])
        for j in range(2):
            @pl.when(jnp.logical_not(jnp.logical_and(chip == s, j == c)))
            def _():
                drain(kv.at[0, 0], ks.at[k, j])
                drain(qbuf.at[0], qs.at[k, j])

        @pl.when(jnp.logical_not(jnp.logical_and(chip == s, side == c)))
        def _():
            drain(text.at[0, 0], ts.at[k])

        return carry

    lax.fori_loop(0, H, sent, 0)
    drain(got.at[pl.ds(0, S - 1)], ms)
    drain(g_all.at[pl.ds(0, S - 1)], gs)
    drain(parts.at[pl.ds(0, S - 1)], ps)
    if NI > 1:
        drain(rewards.at[pl.ds(0, NI - 1)], rs)
    for w in swaps:
        w.wait_send()
    drain(r1.at[pl.ds(0, NP - 1)], as_.at[0])
    drain(r2.at[pl.ds(0, YN - 1)], as_.at[1])
    if ZN > 1:
        drain(r3.at[pl.ds(0, ZN - 1)], as_.at[2])
    drain(r4.at[pl.ds(0, YN - 1)], as_.at[3])
    drain(r1.at[pl.ds(0, NP - 1)], as_.at[4])
    drain(r4, ls)
    drain(r1.at[pl.ds(0, NP - 1)], ar.at[4])
    drain(dv, dvsem)
    text_here = jnp.logical_and(branch == c, s // H == c)

    @pl.when(branch == c)
    def _():
        drain(uf.at[pl.ds(0, S - 1)], us)
        drain(dqb.at[pl.ds(0, S - 1)], dqs)
        drain(kf.at[pl.ds(0, S - 1)], dks)

    @pl.when(branch != c)
    def _():
        drain(uf, us)
        drain(dqb, dqs)
        drain(kf, dks)

    @pl.when(text_here)
    def _():
        drain(utf.at[pl.ds(0, H - 1)], uts)
        drain(ktf.at[pl.ds(0, H - 1)], kts)

    @pl.when(jnp.logical_not(text_here))
    def _():
        drain(utf, uts)
        drain(ktf, kts)

    drain(ktb, ktr)

    def text_home(h, carry):
        at = pl.ds(pl.multiple_of(h * D, D), D)
        t = ktb[h].astype(F32)
        tgrad[:, at] = jnp.where(iota(t.shape, 0) < TXT, t, tgrad[:, at].astype(F32)).astype(BF16)
        return carry

    lax.fori_loop(0, H, text_home, 0)
    drain(grad.at[0], dqr)
    drain(grad.at[1], dkr)


EVENTS = (
    (0, "send_narrow"),
    (2, "widen_all"),
    (2, "readout_1"),
    (3, "readout_2"),
    (4, "readout_3"),
    (5, "readout_4"),
    (6, "readout_5"),
)


def step_call(S, NI, guidance, rate, img, tx, rt, noise, old, reward):
    H, ZN, NP = S // 2, S // YN, 2 * NI
    HD = rt.shape[1]
    W, RY, third = HD // NP, C // YN, HALF // 2
    NK = (2 * HALF + TXT) * S
    dma = pltpu.SemaphoreType.DMA
    tile = (8, D)
    b = lambda *shape: pltpu.VMEM(shape, BF16)
    w = lambda *shape: pltpu.VMEM(shape, F32)
    return pl.pallas_call(
        functools.partial(step_kernel, S, NI),
        out_shape=(
            jax.ShapeDtypeStruct(img.shape, BF16),
            jax.ShapeDtypeStruct((2 * TXT, HD), BF16),
            jax.ShapeDtypeStruct((YN, RY, HD), F32),
            jax.ShapeDtypeStruct(tile, F32),
        ),
        in_specs=[SMEM, SMEM, ANY, VMEM, VMEM, VMEM, VMEM, VMEM],
        out_specs=(ANY, VMEM, ANY, VMEM),
        scratch_shapes=[
            b(*img.shape[1:]),
            b(H, 2, third, D),
            b(H, 2 * TXT, D),
            b(2, S, HALF + third, D),
            b(2, H, 2 * TXT, D),
            b(S, HALF, D),
            b(NK, 2 * D),
            b(D, NK),
            b(NK, D),
            b(C + ONES, NK),
            w(NK, QB),
            w(NK, QB),
            *([b(SB, QB)] * 4),
            b(TXT * S, QB),
            b(ZN, NK, QB),
            w(ZN, C, QB),
            w(ZN, 1, QB),
            b(S, C // 2, D),
            b(S, C // 2, D),
            b(C // 2, D),
            b(S, C // 2, D),
            w(*tile),
            w(S, *tile),
            w(2, *tile),
            w(NI, *tile),
            b(ZN, 2 * C, QB),
            w(ZN, 1, QB),
            w(NK, D),
            w(NK, D),
            b(S, third, D),
            b(S, third, D),
            b(S, third, D),
            b(H, 2 * TXT, D),
            b(H, 2 * TXT, D),
            b(H, 2 * TXT, D),
            b(S, HALF, D),
            b(S, HALF, D),
            b(S, HALF, D),
            b(H, 2 * TXT, D),
            b(H, 2 * TXT, D),
            b(H, 2 * TXT, D),
            b(S, HALF, D),
            b(H, 2, third, D),
            b(H, 2 * TXT, D),
            b(H, 2 * TXT, D),
            b(*img.shape[1:]),
            w(C, HD),
            w(NP, C, W),
            w(C, W),
            w(YN, RY, W),
            w(RY, W),
            w(ZN, RY, W),
            w(RY, W),
            w(YN, RY, W),
            dma,
            dma((H, 2)), dma((S,)),
            dma((H, 2)), dma((S,)),
            dma((H,)), dma((H,)),
            dma((S,)), dma((S,)),
            dma((H,)), dma((H,)),
            dma, dma,
            dma, dma((S,)),
            dma, dma,
            dma, dma,
            dma, dma,
            dma((4,)), dma((4,)),
            dma, dma,
            dma, dma,
            dma, dma,
            dma, dma,
            dma, dma,
            dma,
            dma((5,)), dma((5,)),
            dma,
        ],
        compiler_params=pltpu.CompilerParams(
            collective_id=0, has_side_effects=True, vmem_limit_bytes=LIMIT
        ),
        name="step",
    )(guidance, rate, img, tx, rt, noise, old, reward)


def on_device(S, NI, img_qkv, txt_kv, readout, old_velocity, noise, step_ratio, rewards, guidance):
    img = img_qkv[0, 0].transpose(1, 0, 2)
    text = txt_kv[0, 0]
    tx = jnp.concatenate([text[:, 0], text[:, 1]], axis=0)
    scalar = lambda x: x.reshape(1, 1)
    reward = jnp.broadcast_to(scalar(rewards), (8, D))
    grad, tgrad, rg, ratio = step_call(
        S, NI, scalar(guidance), scalar(step_ratio), img, tx, readout.T, noise[0].T, old_velocity[0].T, reward
    )
    img_grad = grad.transpose(1, 0, 2)[None, None]
    txt_grad = jnp.stack([tgrad[:TXT], tgrad[TXT:]], axis=1)[None, None]
    return (img_grad, txt_grad, rg.reshape(C, -1).T, ratio[0, :1])


def solution(mesh):
    S, NI = mesh.shape["seq"], mesh.shape["img"]
    placed = (
        P("cfg", "img", "seq", None, None),
        P("cfg", "img", "seq", None, None),
        P(),
        P("img", "seq", None),
        P("img", "seq", None),
        P("img"),
        P("img"),
        P(),
    )
    return jax.shard_map(
        functools.partial(on_device, S, NI),
        mesh=mesh,
        in_specs=placed,
        out_specs=(
            P("cfg", "img", "seq", None, None),
            P("cfg", "img", "seq", None, None),
            P(),
            P("img"),
        ),
        check_vma=False,
    )
```

```python
import functools

import jax
import jax.numpy as jnp
from jax import lax
from jax.experimental import pallas as pl
from jax.experimental.pallas import tpu as pltpu
from jax.sharding import PartitionSpec as P

D = 128
C = 64
HALF = 64
TXT = 8
YN = 4
QB = 256
KB = 1024
SB = 256
ONES = 16
MESH = pl.DeviceIdType.MESH
F32 = jnp.float32
BF16 = jnp.bfloat16
NT = (((1,), (1,)), ((), ()))
TN = (((0,), (0,)), ((), ()))
ANY = pl.BlockSpec(memory_space=pl.ANY)
VMEM = pl.BlockSpec(memory_space=pltpu.VMEM)
SMEM = pl.BlockSpec(memory_space=pltpu.SMEM)
LIMIT = 60 * 1024 * 1024


def iota(shape, dim):
    return lax.broadcasted_iota(jnp.int32, shape, dim)


def put(src, dst, send, recv, core, chip):
    here = jnp.logical_and(core == lax.axis_index("cfg"), chip == lax.axis_index("seq"))

    @pl.when(here)
    def _():
        pltpu.make_async_copy(src, dst, recv).start()

    @pl.when(jnp.logical_not(here))
    def _():
        away(src, dst, send, recv, {"cfg": core, "seq": chip}).start()


def away(src, dst, send, recv, device):
    return pltpu.make_async_remote_copy(
        src_ref=src,
        dst_ref=dst,
        send_sem=send,
        recv_sem=recv,
        device_id=device,
        device_id_type=MESH,
    )


def drain(ref, sem):
    pltpu.make_async_copy(ref, ref, sem).wait()


def wrap(at, size):
    return jnp.where(at >= size, at - size, at)


def signal_plane(chips):
    c, s = lax.axis_index("cfg"), lax.axis_index("seq")
    barrier = pltpu.get_barrier_semaphore()

    def tell(device):
        pl.semaphore_signal(barrier, inc=1, device_id=device, device_id_type=MESH)

    def one(k, carry):
        chip = wrap(s + k, chips)
        tell({"cfg": c, "seq": chip})
        tell({"cfg": 1 - c, "seq": chip})
        return carry

    lax.fori_loop(1, chips, one, 0)
    tell({"cfg": 1 - c})
    return barrier


def pack_pair(x):
    top, low = x[: C // 2], x[C // 2 :]
    lower = iota(top.shape, 1) < HALF
    return (
        jnp.where(lower, top, pltpu.roll(low, HALF, 1)),
        jnp.where(lower, pltpu.roll(top, HALF, 1), low),
    )


def unpack_pair(a, b):
    lower = iota(a.shape, 1) < HALF
    return jnp.concatenate(
        [jnp.where(lower, a, pltpu.roll(b, HALF, 1)), jnp.where(lower, pltpu.roll(a, HALF, 1), b)], axis=0
    )


def own_tokens(x):
    a, b = pack_pair(x)
    return jnp.where(lax.axis_index("cfg") == 0, a, b)


def step_kernel(
    S, NI, guidance, rate, reward, img, tx, rt, noise, old,
    grad, tgrad, rg, ratio,
    vbuf, vrp, txb, kv, text, qbuf, keys, keys_t, narrow, narrow_t, scores_a, scores_b, hold_0, hold_1, hold_2, hold_3, hold_text, weights, out_t, linv,
    msg, got, g_own, g_all, part, parts, pair, rewards, reward_own, gl, gl_cols, delta, gk,
    uo, xu, uown, uf, uto, xut, utf, ko, xk, kf, kto, xkt, ktf, dqb, ub, utb, ktb, dv, rgp, rx, rh, rhb, r1, a1, r2, a2, r3, a3, r4,
    vsem, ks, kr, qs, qr, ts, tr, fs, fr, fts, ftr, ms, mr, gs, gr, ps, pr, pairs, pairr, rs, rr,
    xs, xr, xus, xur, us, ur, uts, utr, dqs, dqr, dks, dkr, kts, ktr, dvsem, as_, ar, ls,
):
    H = S // 2
    ZN = S // YN
    NP = 2 * NI
    W = rgp.shape[1] // NP
    RY = C // YN
    NK = keys.shape[0]
    NKI = 2 * HALF * S
    holds = (hold_0, hold_1, hold_2, hold_3)[: min(KB, NKI) // SB]
    third = HALF // 2
    n3 = third * S
    c, i, s = lax.axis_index("cfg"), lax.axis_index("img"), lax.axis_index("seq")
    head, branch = s // 2, lax.rem(s, 2)
    y, z = lax.rem(s, YN), s // YN
    other = {"cfg": 1 - c}

    vcopy = pltpu.make_async_copy(img.at[2], vbuf, vsem)
    vcopy.start()
    barrier = signal_plane(S)
    for k in range(1, NI):
        for core in range(2):
            pl.semaphore_signal(
                barrier, inc=1, device_id={"cfg": core, "img": wrap(i + k, NI)}, device_id_type=MESH
            )
    vcopy.wait()
    reward_own[...] = jnp.full(reward_own.shape, reward[0, 0], F32)

    def squeeze(h):
        cols = pl.ds(pl.multiple_of(h * D, D), D)
        r = rt[:, cols]
        twice = jnp.concatenate([r, r], axis=0)
        x = lax.dot_general(vbuf[:, cols], twice, NT, preferred_element_type=F32)
        low = iota((third, D), 1) < C
        for j in range(2):
            first = x[HALF * j : HALF * j + third]
            second = x[HALF * j + third : HALF * j + HALF]
            vrp[h, j] = jnp.where(low, first, second).astype(BF16)
        t = tx[:, cols]
        yv = lax.dot_general(t, twice, NT, preferred_element_type=F32)
        yv = jnp.where(iota(yv.shape, 1) < C, yv, 0.0)
        txb[h] = jnp.where(iota(yv.shape, 0) < TXT, t.astype(F32), yv).astype(BF16)

    def some(count, body):
        at_once = 4 if count % 4 == 0 else 1

        def trip(k, carry):
            for j in range(at_once):
                body(k * at_once + j)
            return carry

        lax.fori_loop(0, count // at_once, trip, 0)

    some(H, squeeze)
    pl.semaphore_wait(barrier, 2 * S - 1 + 2 * (NI - 1))

    side = s // H

    def at_distance(n, sign):
        half = (n + 1) // 2
        far = jnp.where(n == 2 * half, ZN - half, half)
        return wrap(z + far, ZN) if sign > 0 else wrap(z + ZN - far, ZN)

    def in_turn(n, sign):
        if ZN < 4:
            return at_distance(n, sign)
        return at_distance(jnp.where(n == 0, 0, jnp.where(n <= ZN - 3, n + 2, n - (ZN - 3))), sign)

    def send_keys(k, carry):
        zt = at_distance(k // 2, 1)
        h = 2 * zt + lax.rem(k, 2)
        chip = 2 * h + c
        cols = pl.ds(pl.multiple_of(h * D, D), D)
        for j in range(2):
            put(img.at[1, pl.ds(HALF * j, HALF), cols], kv.at[0, s, pl.ds(0, HALF)], ks.at[h, j], kr.at[s], j, chip)
            put(vrp.at[h, j], kv.at[0, s, pl.ds(HALF, third)], ks.at[h, j], kr.at[s], j, chip)
        put(txb.at[h], text.at[0, lax.rem(s, H)], ts.at[h], tr.at[lax.rem(s, H)], side, chip)
        return carry

    lax.fori_loop(0, H, send_keys, 0)

    def send_queries(k, carry):
        zt = in_turn(k // 2, 1)
        h = 2 * zt + lax.rem(k, 2)
        chip = 2 * h + c
        cols = pl.ds(pl.multiple_of(h * D, D), D)
        for j in range(2):
            put(img.at[0, pl.ds(HALF * j, HALF), cols], qbuf.at[s], qs.at[h, j], qr.at[s], j, chip)
        return carry

    lax.fori_loop(0, H, send_queries, 0)
    for k in range(1, NI):
        away(reward_own, rewards.at[i], rs, rr, {"img": wrap(i + k, NI)}).start()

    narrow_t[C:] = jnp.where(iota((ONES, NK), 0) == 0, 1.0, 0.0).astype(BF16)

    def lay_out(p, zs):
        four = pl.ds(zs * YN, YN)
        packed = kv[p, four, HALF:, :].reshape(third * YN, D)
        turned = packed.astype(F32).T
        for ab in range(2):
            rows = pl.ds(pl.multiple_of((2 * p + ab) * n3 + zs * (third * YN), third * YN), third * YN)
            block = kv[p, four, third * ab : third * ab + third, :].reshape(third * YN, D)
            keys[rows, :D] = block
            keys[rows, D:] = block
            keys_t[:, rows] = block.astype(F32).T.astype(BF16)
            one = turned[C * ab : C * ab + C]
            narrow_t[:C, rows] = one.astype(BF16)
            narrow[rows] = jnp.concatenate([one, one], axis=0).T.astype(BF16)

    def arrive(n, carry):
        zs = at_distance(n, -1)
        for yy in range(YN):
            src = zs * YN + yy
            drain(kv.at[0, src], kr.at[src])
            away(kv.at[0, src], kv.at[1, src], fs.at[src], fr.at[src], other).start()
        lay_out(0, zs)
        return carry

    lax.fori_loop(0, ZN, arrive, 0)

    def arrive_text(k, carry):
        drain(text.at[0, k], tr.at[k])
        away(text.at[0, k], text.at[1, k], fts.at[k], ftr.at[k], other).start()
        return carry

    lax.fori_loop(0, H, arrive_text, 0)

    def arrive_other(n, carry):
        zs = at_distance(n, -1)
        for yy in range(YN):
            drain(kv.at[1, zs * YN + yy], fr.at[zs * YN + yy])
        lay_out(1, zs)
        return carry

    lax.fori_loop(0, ZN, arrive_other, 0)

    def arrive_other_text(k, carry):
        drain(text.at[1, k], ftr.at[k])
        return carry

    lax.fori_loop(0, H, arrive_other_text, 0)
    words = text[...].astype(F32)
    tk = words[:, :, :TXT, :].reshape(TXT * S, D)
    tv = words[:, :, TXT:, :].reshape(TXT * S, D)
    last = pl.ds(NKI, TXT * S)
    keys[last, :D] = tk.astype(BF16)
    keys[last, D:] = tk.astype(BF16)
    keys_t[:, last] = tk.T.astype(BF16)
    tvt = tv.T[:C]
    narrow_t[:C, last] = tvt.astype(BF16)
    narrow[last] = jnp.concatenate([tvt, tvt], axis=0).T.astype(BF16)

    def over_keys(body, carry):
        for at in range(0, NK, SB):
            carry = body(slice(at, min(at + SB, NK)), carry)
        return carry

    def queries_t(zs):
        for yy in range(YN):
            drain(qbuf.at[zs * YN + yy], qr.at[zs * YN + yy])
        x = qbuf[pl.ds(zs * YN, YN)].reshape(QB, D).astype(F32).T * (D ** (-0.5) * 1.4426950408889634)
        hi = x.astype(BF16)
        return jnp.concatenate([hi, (x - hi.astype(F32)).astype(BF16)], axis=0)

    def score(buf, rows, q_t, top):
        st = jnp.dot(keys[rows], q_t, preferred_element_type=F32)
        buf[rows] = st
        return jnp.maximum(top, jnp.max(st.reshape(st.shape[0] // 8, 8, QB), axis=0))

    def weigh(buf, zs, rows, top, hold):
        e = jnp.exp2(buf[rows] - top).astype(BF16)
        weights[zs, rows] = e
        hold[...] = e

    def mix(rows, hold, mixed):
        return mixed + jnp.dot(narrow_t[:, rows], hold[...], preferred_element_type=F32)

    low_top = jnp.full((8, QB), -jnp.inf, F32)
    no_mix = jnp.zeros((C + ONES, QB), F32)
    branch_share = jnp.where(branch == 0, guidance[0, 0], 1.0 - guidance[0, 0])
    parts_of = NKI // KB
    subs = KB // SB

    def chunk(k, sub):
        return pl.ds(pl.multiple_of(k * KB + sub * SB, SB), SB)

    def first_scores(q_t):
        def body(k, t):
            for sub in range(subs):
                t = score(scores_a, chunk(k, sub), q_t, t)
            return t

        return score(scores_a, last, q_t, lax.fori_loop(0, parts_of, body, low_top))

    def attend(n, now, then, top8, ahead):
        zs = in_turn(n, -1)
        top = jnp.max(top8, axis=0, keepdims=True)
        q_t = queries_t(in_turn(n + 1, -1)) if ahead else None
        next8 = score(then, last, q_t, low_top) if ahead else low_top
        weigh(now, zs, last, top, hold_text)
        mixed = mix(last, hold_text, no_mix)
        holds[subs - 1][...] = jnp.zeros((SB, QB), BF16)

        def body(k, carry):
            next8, mixed = carry
            for sub in range(subs):
                before = chunk(jnp.maximum(k - 1, 0), subs - 1) if sub == 0 else chunk(k, sub - 1)
                mixed = mix(before, holds[sub - 1], mixed)
                if ahead:
                    next8 = score(then, chunk(k, sub), q_t, next8)
                weigh(now, zs, chunk(k, sub), top, holds[sub])
            return next8, mixed

        next8, mixed = lax.fori_loop(0, parts_of, body, (next8, mixed))
        mixed = mix(chunk(parts_of - 1, subs - 1), holds[subs - 1], mixed)
        inverse = 1.0 / mixed[C : C + 1]
        linv[zs] = inverse
        normal = mixed[:C] * inverse
        out_t[zs] = normal
        for m in range(QB // D):
            a, b = pack_pair(normal[:, D * m : D * m + D] * branch_share)
            for yy, part_of in ((2 * m, a), (2 * m + 1, b)):
                msg[zs * YN + yy] = part_of.astype(BF16)
        for yy in range(YN):
            t = zs * YN + yy
            put(msg.at[t], got.at[s], ms, mr, c, t)
        return next8

    top = first_scores(queries_t(in_turn(0, -1)))

    def two(m, top):
        top = attend(2 * m, scores_a, scores_b, top, True)
        return attend(2 * m + 1, scores_b, scores_a, top, True)

    top = lax.fori_loop(0, ZN // 2 - 1, two, top)
    if ZN > 1:
        top = attend(ZN - 2, scores_a, scores_b, top, True)
        attend(ZN - 1, scores_b, scores_a, top, False)
    else:
        attend(0, scores_a, scores_b, top, False)

    noise_own = own_tokens(noise[...])
    old_own = own_tokens(old[...])
    drain(got, mr)
    guided = jnp.sum(got[...].astype(F32), axis=0)
    step = rate[0, 0]
    deviation = step * (guided - old_own)
    g_own[...] = (noise_own - deviation).astype(BF16)

    def share(k, carry):
        zt = at_distance(k, 1)
        for yy in range(YN):
            put(g_own, g_all.at[s], gs, gr, c, zt * YN + yy)
        return carry

    lax.fori_loop(0, ZN, share, 0)
    partial = jnp.sum(noise_own * deviation - 0.5 * deviation * deviation)
    part[...] = jnp.full(part.shape, partial, F32)

    def tell(k, carry):
        put(part, parts.at[s], ps, pr, c, k)
        return carry

    lax.fori_loop(0, S, tell, 0)
    gk[...] = jnp.zeros_like(gk)

    drain(g_all, gr)

    def divide(zs, carry):
        g_t = jnp.concatenate(
            [
                unpack_pair(g_all[zs * YN + 2 * m].astype(F32), g_all[zs * YN + 2 * m + 1].astype(F32))
                for m in range(QB // D)
            ],
            axis=1,
        )
        g_t = g_t * linv[zs]
        hi = g_t.astype(BF16)
        lo = (g_t - hi.astype(F32)).astype(BF16)
        hi32 = hi.astype(F32)
        gl[zs] = jnp.concatenate([hi, lo], axis=0)
        delta[zs] = jnp.sum((hi32 + lo.astype(F32)) * out_t[zs], axis=0, keepdims=True)
        gl_cols[zs] = jnp.concatenate([hi32, hi32], axis=0).T.astype(BF16)
        return carry

    lax.fori_loop(0, ZN, divide, 0)

    drain(parts, pr)
    pair[0] = jnp.sum(parts[...], axis=0)
    swap = away(pair.at[0], pair.at[1], pairs, pairr, other)
    swap.start()
    if NI > 1:
        drain(rewards.at[pl.ds(0, NI - 1)], rr)
    own_reward = reward_own[...]
    rewards[i] = own_reward
    mean = jnp.sum(rewards[...], axis=0) / NI
    square = jnp.sum(rewards[...] * rewards[...], axis=0) / NI
    deviates = jnp.sqrt(jnp.maximum(square - mean * mean, 0.0))
    advantage = (own_reward - mean) / jnp.maximum(deviates, 1.0)
    swap.wait()
    ratio_now = jnp.exp((pair[0] + pair[1]) / (2 * S * HALF * C))
    clipped = jnp.clip(ratio_now, 0.8, 1.2)
    keep = ratio_now * advantage <= clipped * advantage
    gain = jnp.where(keep, -ratio_now * advantage, 0.0)
    ratio[0, 0] = jnp.max(ratio_now)
    f = (gain * (step * branch_share))[0:1, :]
    fscale = f * D ** (-0.5)

    cols_home = pl.ds(pl.multiple_of(head * D, D), D)
    mine = pl.ds(pl.multiple_of(HALF * c, HALF), HALF)
    NG = max(1, n3 // SB)
    GS = S // NG
    GR = third * GS

    def narrow_grad(rows):
        total = jnp.dot(weights[0, rows], gl_cols[0], preferred_element_type=F32)
        for zs in range(1, ZN):
            total = total + jnp.dot(weights[zs, rows], gl_cols[zs], preferred_element_type=F32)
        return total * f

    def paired(p, r):
        a, b = (
            narrow_grad(pl.ds(pl.multiple_of((2 * p + ab) * n3 + r * GR, GR), GR)) for ab in range(2)
        )
        return jnp.where(iota(a.shape, 1) < C, a, b).reshape(GS, third, D)

    def swap_u(r):
        srcs = pl.ds(r * GS, GS)
        return away(uo.at[srcs], xu.at[srcs], xus.at[r], xur.at[r], other)

    def send_u(r):
        swap_u(r).wait_recv()
        srcs = pl.ds(r * GS, GS)
        uf[srcs] = (uown[srcs] + xu[srcs].astype(F32)).astype(BF16)

        def one(k, carry):
            t = r * GS + k
            put(uf.at[t], ub.at[head, c], us, ur, branch, t)
            return carry

        lax.fori_loop(0, GS, one, 0)

    def group(k):
        return wrap(z * NG // ZN + k, NG)

    swaps = [
        away(uto, xut, xs.at[0], xr.at[0], other),
        away(ko, xk, xs.at[1], xr.at[1], other),
        away(kto, xkt, xs.at[2], xr.at[2], other),
    ]
    both_texts = narrow_grad(last)
    both_texts = jnp.where(iota(both_texts.shape, 1) < C, both_texts, 0.0).reshape(2, H, TXT, D)
    no_keys = jnp.zeros((H, TXT, D), F32)
    uto[...] = jnp.concatenate([no_keys, both_texts[1]], axis=1).astype(BF16)
    swaps[0].start()

    def narrow_group(k, carry):
        r = group(k)
        srcs = pl.ds(r * GS, GS)
        uo[srcs] = paired(1, r).astype(BF16)
        swap_u(r).start()
        uown[srcs] = paired(0, r)

        @pl.when(k > 0)
        def _():
            send_u(group(k - 1))

        return carry

    lax.fori_loop(0, NG, narrow_group, 0)
    swaps[0].wait_recv()
    utf[...] = (jnp.concatenate([no_keys, both_texts[0]], axis=1) + xut[...].astype(F32)).astype(BF16)

    def send_text(k, carry):
        put(utf.at[k], utb.at[head], uts, utr, branch, c * H + k)
        return carry

    lax.fori_loop(0, H, send_text, 0)
    send_u(group(NG - 1))

    def widen_all():
        drain(ub, ur)
        drain(utb, utr)

        def widen(h):
            at = pl.ds(pl.multiple_of(h * D, D), D)
            r = rt[:, at]
            twice = jnp.concatenate([r, r], axis=0)
            low = iota((third, D), 1) < C
            u0, u1 = ub[h, 0].astype(F32), ub[h, 1].astype(F32)
            spaced = jnp.concatenate(
                [
                    jnp.where(low, u0, 0.0),
                    jnp.where(low, 0.0, u0),
                    jnp.where(low, u1, 0.0),
                    jnp.where(low, 0.0, u1),
                    utb[h].astype(F32),
                ],
                axis=0,
            )
            wide = jnp.dot(spaced.astype(BF16), twice, preferred_element_type=F32)
            dv[:, at] = wide[: 2 * HALF].astype(BF16)
            tgrad[:, at] = wide[2 * HALF :].astype(BF16)
            values = jnp.concatenate([vbuf[:, at], tx[:, at]], axis=0)
            res = jnp.dot(spaced.T.astype(BF16), values, preferred_element_type=F32)
            rgp[:, at] = res[:C] + res[C:]

        some(H, widen)
        pltpu.make_async_copy(dv, grad.at[2], dvsem).start()

    HW = NI * W

    def half(core):
        return pl.ds(pl.multiple_of(core * HW, D), HW)

    def piece(n):
        return pl.ds(pl.multiple_of(n * W, D), W)

    def strip(n):
        return pl.ds(pl.multiple_of(n * RY, 8), RY)

    def readout_1():
        away(rgp.at[:, half(1 - c)], rx, as_.at[0], ar.at[0], other).start()

    def readout_2():
        drain(rx, ar.at[0])
        rh[...] = rgp[:, half(c)] + rx[...]
        rhb[...] = rh[...].astype(BF16)
        for k in range(1, NI):
            n = wrap(i + k, NI)
            away(rhb.at[:, piece(n)], r1.at[i], as_.at[5], ar.at[5], {"img": n}).start()

    def readout_3():
        if NI > 1:
            drain(r1.at[pl.ds(0, NI - 1)], ar.at[5])
        r1[i] = jnp.zeros((C, W), BF16)
        a1[...] = jnp.sum(r1[...].astype(F32), axis=0) + rh[:, piece(i)]
        for k in range(1, YN):
            n = wrap(y + k, YN)
            away(a1.at[strip(n)], r2.at[y], as_.at[1], ar.at[1], {"seq": z * YN + n}).start()

    def readout_4():
        drain(r2.at[pl.ds(0, YN - 1)], ar.at[1])
        r2[y] = a1[strip(y), :]
        a2[...] = jnp.sum(r2[...], axis=0)
        for k in range(1, ZN):
            n = wrap(z + k, ZN)
            away(a2, r3.at[z], as_.at[2], ar.at[2], {"seq": n * YN + y}).start()

    def readout_5():
        if ZN > 1:
            drain(r3.at[pl.ds(0, ZN - 1)], ar.at[2])
        r3[z] = a2[...]
        a3[...] = jnp.sum(r3[...], axis=0)
        for k in range(1, YN):
            n = wrap(y + k, YN)
            away(a3, r4.at[y], as_.at[3], ar.at[3], {"seq": z * YN + n}).start()

    def readout_6():
        drain(r4.at[pl.ds(0, YN - 1)], ar.at[3])
        r4[y] = a3[...]
        to = rg.at[:, :, pl.ds(pl.multiple_of(c * HW + i * W, D), W)]
        pltpu.make_async_copy(r4, to, ls).start()
        for k in range(NI):
            n = wrap(i + k, NI)
            for core in (c, 1 - c) if k else (1 - c,):
                away(r4, to, as_.at[4], ar.at[4], {"cfg": core, "img": n}).start()

    steps = dict(
        widen_all=widen_all, readout_1=readout_1, readout_2=readout_2, readout_3=readout_3,
        readout_4=readout_4, readout_5=readout_5, readout_6=readout_6,
    )

    def key_grads(n, carry):
        zs = at_distance(n, -1)
        block = qbuf[pl.ds(zs * YN, YN)].reshape(QB, D)
        g_t = gl[zs]
        shift = delta[zs]

        def one(rows, dq_t):
            gp = jnp.dot(narrow[rows], g_t, preferred_element_type=F32)
            ds = (weights[zs, rows].astype(F32) * (gp - shift)).astype(BF16)
            gk[rows] += jnp.dot(ds, block, preferred_element_type=F32)
            return dq_t + jnp.dot(keys_t[:, rows], ds, preferred_element_type=F32)

        dq_t = over_keys(one, jnp.zeros((D, QB), F32))
        dqb[pl.ds(zs * YN, YN)] = (dq_t.T * fscale).astype(BF16).reshape(YN, HALF, D)
        for yy in range(YN):
            t = zs * YN + yy
            put(dqb.at[t], grad.at[0, mine, cols_home], dqs, dqr, branch, t)
        for at, what in EVENTS:
            pl.when(n == min(at, ZN - 1))(steps[what])
        return carry

    lax.fori_loop(0, ZN, key_grads, 0)

    def image_keys(p):
        base = 2 * p * n3
        a = gk[base : base + n3].reshape(S, third, D)
        b = gk[base + n3 : base + 2 * n3].reshape(S, third, D)
        return jnp.concatenate([a, b], axis=1) * fscale

    def text_keys(p):
        k = gk[NKI + p * H * TXT : NKI + (p + 1) * H * TXT]
        k = (k * fscale).reshape(H, TXT, D)
        return jnp.concatenate([k, jnp.zeros_like(k)], axis=1)

    ko[...] = image_keys(1).astype(BF16)
    swaps[1].start()
    kto[...] = text_keys(1).astype(BF16)
    swaps[2].start()
    swaps[1].wait_recv()
    kf[...] = (image_keys(0) + xk[...].astype(F32)).astype(BF16)

    def send_key_grads(k, carry):
        zt = at_distance(k, 1)
        for yy in range(YN):
            t = zt * YN + yy
            put(kf.at[t], grad.at[1, mine, cols_home], dks, dkr, branch, t)
        return carry

    lax.fori_loop(0, ZN, send_key_grads, 0)
    swaps[2].wait_recv()
    ktf[...] = (text_keys(0) + xkt[...].astype(F32)).astype(BF16)

    def send_text_keys(k, carry):
        put(ktf.at[k], ktb.at[head], kts, ktr, branch, c * H + k)
        return carry

    lax.fori_loop(0, H, send_text_keys, 0)

    readout_6()

    def sent(k, carry):
        chip = 2 * k + c
        for odd in range(2):
            src = 2 * k + odd
            drain(kv.at[1, src], fs.at[src])
        drain(text.at[1, k], fts.at[k])
        for j in range(2):
            @pl.when(jnp.logical_not(jnp.logical_and(chip == s, j == c)))
            def _():
                drain(kv.at[0, 0], ks.at[k, j])
                drain(qbuf.at[0], qs.at[k, j])

        @pl.when(jnp.logical_not(jnp.logical_and(chip == s, side == c)))
        def _():
            drain(text.at[0, 0], ts.at[k])

        return carry

    lax.fori_loop(0, H, sent, 0)
    drain(got.at[pl.ds(0, S - 1)], ms)
    drain(g_all.at[pl.ds(0, S - 1)], gs)
    drain(parts.at[pl.ds(0, S - 1)], ps)
    if NI > 1:
        drain(rewards.at[pl.ds(0, NI - 1)], rs)
    for w in swaps:
        w.wait_send()
    drain(rx, as_.at[0])
    if NI > 1:
        drain(r1.at[pl.ds(0, NI - 1)], as_.at[5])
    drain(r2.at[pl.ds(0, YN - 1)], as_.at[1])
    if ZN > 1:
        drain(r3.at[pl.ds(0, ZN - 1)], as_.at[2])
    drain(r4.at[pl.ds(0, YN - 1)], as_.at[3])
    drain(rgp.at[:, pl.ds(0, (NP - 1) * W)], as_.at[4])
    drain(r4, ls)
    drain(rgp.at[:, pl.ds(0, (NP - 1) * W)], ar.at[4])

    def swapped_u(r, carry):
        swap_u(r).wait_send()
        return carry

    lax.fori_loop(0, NG, swapped_u, 0)
    drain(dv, dvsem)
    text_here = jnp.logical_and(branch == c, s // H == c)

    @pl.when(branch == c)
    def _():
        drain(uf.at[pl.ds(0, S - 1)], us)
        drain(dqb.at[pl.ds(0, S - 1)], dqs)
        drain(kf.at[pl.ds(0, S - 1)], dks)

    @pl.when(branch != c)
    def _():
        drain(uf, us)
        drain(dqb, dqs)
        drain(kf, dks)

    @pl.when(text_here)
    def _():
        drain(utf.at[pl.ds(0, H - 1)], uts)
        drain(ktf.at[pl.ds(0, H - 1)], kts)

    @pl.when(jnp.logical_not(text_here))
    def _():
        drain(utf, uts)
        drain(ktf, kts)

    drain(ktb, ktr)

    def text_home(h, carry):
        at = pl.ds(pl.multiple_of(h * D, D), D)
        t = ktb[h].astype(F32)
        tgrad[:, at] = jnp.where(iota(t.shape, 0) < TXT, t, tgrad[:, at].astype(F32)).astype(BF16)
        return carry

    lax.fori_loop(0, H, text_home, 0)
    drain(grad.at[0], dqr)
    drain(grad.at[1], dkr)


EVENTS = (
    (1, "widen_all"),
    (1, "readout_1"),
    (2, "readout_2"),
    (4, "readout_3"),
    (5, "readout_4"),
    (7, "readout_5"),
)


def step_call(S, NI, guidance, rate, reward, img, tx, rt, noise, old):
    H, ZN, NP = S // 2, S // YN, 2 * NI
    HD = rt.shape[1]
    W, RY, third = HD // NP, C // YN, HALF // 2
    NK = (2 * HALF + TXT) * S
    dma = pltpu.SemaphoreType.DMA
    tile = (8, D)
    b = lambda *shape: pltpu.VMEM(shape, BF16)
    w = lambda *shape: pltpu.VMEM(shape, F32)
    return pl.pallas_call(
        functools.partial(step_kernel, S, NI),
        out_shape=(
            jax.ShapeDtypeStruct(img.shape, BF16),
            jax.ShapeDtypeStruct((2 * TXT, HD), BF16),
            jax.ShapeDtypeStruct((YN, RY, HD), F32),
            jax.ShapeDtypeStruct((1, 1), F32),
        ),
        in_specs=[SMEM, SMEM, SMEM, ANY, VMEM, VMEM, VMEM, VMEM],
        out_specs=(ANY, VMEM, ANY, SMEM),
        scratch_shapes=[
            b(*img.shape[1:]),
            b(H, 2, third, D),
            b(H, 2 * TXT, D),
            b(2, S, HALF + third, D),
            b(2, H, 2 * TXT, D),
            b(S, HALF, D),
            b(NK, 2 * D),
            b(D, NK),
            b(NK, D),
            b(C + ONES, NK),
            w(NK, QB),
            w(NK, QB),
            *([b(SB, QB)] * 4),
            b(TXT * S, QB),
            b(ZN, NK, QB),
            w(ZN, C, QB),
            w(ZN, 1, QB),
            b(S, C // 2, D),
            b(S, C // 2, D),
            b(C // 2, D),
            b(S, C // 2, D),
            w(*tile),
            w(S, *tile),
            w(2, *tile),
            w(NI, *tile),
            w(*tile),
            b(ZN, 2 * C, QB),
            b(ZN, QB, D),
            w(ZN, 1, QB),
            w(NK, D),
            b(S, third, D),
            b(S, third, D),
            w(S, third, D),
            b(S, third, D),
            b(H, 2 * TXT, D),
            b(H, 2 * TXT, D),
            b(H, 2 * TXT, D),
            b(S, HALF, D),
            b(S, HALF, D),
            b(S, HALF, D),
            b(H, 2 * TXT, D),
            b(H, 2 * TXT, D),
            b(H, 2 * TXT, D),
            b(S, HALF, D),
            b(H, 2, third, D),
            b(H, 2 * TXT, D),
            b(H, 2 * TXT, D),
            b(*img.shape[1:]),
            w(C, HD),
            w(C, NI * W),
            w(C, NI * W),
            b(C, NI * W),
            b(NI, C, W),
            w(C, W),
            w(YN, RY, W),
            w(RY, W),
            w(ZN, RY, W),
            w(RY, W),
            w(YN, RY, W),
            dma,
            dma((H, 2)), dma((S,)),
            dma((H, 2)), dma((S,)),
            dma((H,)), dma((H,)),
            dma((S,)), dma((S,)),
            dma((H,)), dma((H,)),
            dma, dma,
            dma, dma,
            dma, dma,
            dma, dma,
            dma, dma,
            dma((3,)), dma((3,)),
            dma((max(1, third * S // SB),)), dma((max(1, third * S // SB),)),
            dma, dma,
            dma, dma,
            dma, dma,
            dma, dma,
            dma, dma,
            dma,
            dma((6,)), dma((6,)),
            dma,
        ],
        compiler_params=pltpu.CompilerParams(
            collective_id=0, has_side_effects=True, vmem_limit_bytes=LIMIT
        ),
        name="step",
    )(guidance, rate, reward, img, tx, rt, noise, old)


def on_device(S, NI, img_qkv, txt_kv, readout, old_velocity, noise, step_ratio, rewards, guidance):
    img = img_qkv[0, 0].transpose(1, 0, 2)
    text = txt_kv[0, 0]
    tx = jnp.concatenate([text[:, 0], text[:, 1]], axis=0)
    scalar = lambda x: x.reshape(1, 1)
    grad, tgrad, rg, ratio = step_call(
        S, NI, scalar(guidance), scalar(step_ratio), scalar(rewards), img, tx, readout.T, noise[0].T, old_velocity[0].T
    )
    img_grad = grad.transpose(1, 0, 2)[None, None]
    txt_grad = jnp.stack([tgrad[:TXT], tgrad[TXT:]], axis=1)[None, None]
    return (img_grad, txt_grad, rg.reshape(C, -1).T, ratio.reshape(1))


def solution(mesh):
    S, NI = mesh.shape["seq"], mesh.shape["img"]
    placed = (
        P("cfg", "img", "seq", None, None),
        P("cfg", "img", "seq", None, None),
        P(),
        P("img", "seq", None),
        P("img", "seq", None),
        P("img"),
        P("img"),
        P(),
    )
    return jax.shard_map(
        functools.partial(on_device, S, NI),
        mesh=mesh,
        in_specs=placed,
        out_specs=(
            P("cfg", "img", "seq", None, None),
            P("cfg", "img", "seq", None, None),
            P(),
            P("img"),
        ),
        check_vma=False,
    )
```

```python
import functools

import jax
import jax.numpy as jnp
from jax import lax
from jax.experimental import pallas as pl
from jax.experimental.pallas import tpu as pltpu
from jax.sharding import PartitionSpec as P

D = 128
C = 64
HALF = 64
TXT = 8
YN = 4
QB = 256
KB = 1024
SB = 256
ONES = 16
MESH = pl.DeviceIdType.MESH
F32 = jnp.float32
BF16 = jnp.bfloat16
NT = (((1,), (1,)), ((), ()))
TN = (((0,), (0,)), ((), ()))
ANY = pl.BlockSpec(memory_space=pl.ANY)
VMEM = pl.BlockSpec(memory_space=pltpu.VMEM)
SMEM = pl.BlockSpec(memory_space=pltpu.SMEM)
LIMIT = 60 * 1024 * 1024


def iota(shape, dim):
    return lax.broadcasted_iota(jnp.int32, shape, dim)


def put(src, dst, send, recv, core, chip):
    here = jnp.logical_and(core == lax.axis_index("cfg"), chip == lax.axis_index("seq"))

    @pl.when(here)
    def _():
        pltpu.make_async_copy(src, dst, recv).start()

    @pl.when(jnp.logical_not(here))
    def _():
        away(src, dst, send, recv, {"cfg": core, "seq": chip}).start()


def away(src, dst, send, recv, device):
    return pltpu.make_async_remote_copy(
        src_ref=src,
        dst_ref=dst,
        send_sem=send,
        recv_sem=recv,
        device_id=device,
        device_id_type=MESH,
    )


def drain(ref, sem):
    pltpu.make_async_copy(ref, ref, sem).wait()


def wrap(at, size):
    return jnp.where(at >= size, at - size, at)


def signal_plane(chips):
    c, s = lax.axis_index("cfg"), lax.axis_index("seq")
    barrier = pltpu.get_barrier_semaphore()

    def tell(device):
        pl.semaphore_signal(barrier, inc=1, device_id=device, device_id_type=MESH)

    def one(k, carry):
        chip = wrap(s + k, chips)
        tell({"cfg": c, "seq": chip})
        tell({"cfg": 1 - c, "seq": chip})
        return carry

    lax.fori_loop(1, chips, one, 0)
    tell({"cfg": 1 - c})
    return barrier


def pack_pair(x):
    top, low = x[: C // 2], x[C // 2 :]
    lower = iota(top.shape, 1) < HALF
    return (
        jnp.where(lower, top, pltpu.roll(low, HALF, 1)),
        jnp.where(lower, pltpu.roll(top, HALF, 1), low),
    )


def unpack_pair(a, b):
    lower = iota(a.shape, 1) < HALF
    return jnp.concatenate(
        [jnp.where(lower, a, pltpu.roll(b, HALF, 1)), jnp.where(lower, pltpu.roll(a, HALF, 1), b)], axis=0
    )


def own_tokens(x):
    a, b = pack_pair(x)
    return jnp.where(lax.axis_index("cfg") == 0, a, b)


def step_kernel(
    S, NI, guidance, rate, reward, img, txt, rt, noise, old,
    grad, tgrad, rg, ratio,
    tx, vbuf, vrp, txb, kv, text, qbuf, keys, keys_t, narrow, narrow_t, scores_a, scores_b, hold_0, hold_1, hold_2, hold_3, hold_text, weights, out_t, linv,
    msg, got, g_own, g_all, part, parts, pair, rewards, reward_own, gl, gl_cols, delta, gk, factor, held,
    uo, xu, uown, uf, uto, xut, utf, ko, xk, kf, kto, xkt, ktf, dqb, ub, utb, ktb, dv, dkt, dvt, rgp, rx, rh, rhb, r1, a1, r2, a2, r3, a3, r4,
    vsem, ks, kr, qs, qr, ts, tr, fs, fr, fts, ftr, ms, mr, gs, gr, ps, pr, pairs, pairr, rs, rr,
    xs, xr, xus, xur, us, ur, uts, utr, dqs, dqr, dks, dkr, kts, ktr, dvsem, as_, ar, ls,
):
    H = S // 2
    ZN = S // YN
    NP = 2 * NI
    W = rgp.shape[1] // NP
    RY = C // YN
    NK = keys.shape[0]
    NKI = 2 * HALF * S
    holds = (hold_0, hold_1, hold_2, hold_3)[: min(KB, NKI) // SB]
    third = HALF // 2
    n3 = third * S
    c, i, s = lax.axis_index("cfg"), lax.axis_index("img"), lax.axis_index("seq")
    head, branch = s // 2, lax.rem(s, 2)
    y, z = lax.rem(s, YN), s // YN
    other = {"cfg": 1 - c}

    vcopy = pltpu.make_async_copy(img.at[2], vbuf, vsem)
    vcopy.start()
    barrier = signal_plane(S)
    for k in range(1, NI):
        for core in range(2):
            pl.semaphore_signal(
                barrier, inc=1, device_id={"cfg": core, "img": wrap(i + k, NI)}, device_id_type=MESH
            )
    words = txt[...].astype(F32)
    tx[...] = jnp.concatenate([words[:, 0], words[:, 1]], axis=0).astype(BF16)
    vcopy.wait()
    reward_own[...] = jnp.full(reward_own.shape, reward[0, 0], F32)

    def squeeze(h):
        cols = pl.ds(pl.multiple_of(h * D, D), D)
        r = rt[:, cols]
        twice = jnp.concatenate([r, r], axis=0)
        x = lax.dot_general(vbuf[:, cols], twice, NT, preferred_element_type=F32)
        low = iota((third, D), 1) < C
        for j in range(2):
            first = x[HALF * j : HALF * j + third]
            second = x[HALF * j + third : HALF * j + HALF]
            vrp[h, j] = jnp.where(low, first, second).astype(BF16)
        t = tx[:, cols]
        yv = lax.dot_general(t, twice, NT, preferred_element_type=F32)
        yv = jnp.where(iota(yv.shape, 1) < C, yv, 0.0)
        txb[h] = jnp.where(iota(yv.shape, 0) < TXT, t.astype(F32), yv).astype(BF16)

    def some(count, body):
        at_once = 4 if count % 4 == 0 else 1

        def trip(k, carry):
            for j in range(at_once):
                body(k * at_once + j)
            return carry

        lax.fori_loop(0, count // at_once, trip, 0)

    some(H, squeeze)
    pl.semaphore_wait(barrier, 2 * S - 1 + 2 * (NI - 1))

    side = s // H

    def at_distance(n, sign):
        half = (n + 1) // 2
        far = jnp.where(n == 2 * half, ZN - half, half)
        return wrap(z + far, ZN) if sign > 0 else wrap(z + ZN - far, ZN)

    def in_turn(n, sign):
        if ZN < 4:
            return at_distance(n, sign)
        return at_distance(jnp.where(n == 0, 0, jnp.where(n <= ZN - 3, n + 2, n - (ZN - 3))), sign)

    def send_keys(k, carry):
        zt = at_distance(k // 2, 1)
        h = 2 * zt + lax.rem(k, 2)
        chip = 2 * h + c
        cols = pl.ds(pl.multiple_of(h * D, D), D)
        for j in range(2):
            put(img.at[1, pl.ds(HALF * j, HALF), cols], kv.at[0, s, pl.ds(0, HALF)], ks.at[h, j], kr.at[s], j, chip)
            put(vrp.at[h, j], kv.at[0, s, pl.ds(HALF, third)], ks.at[h, j], kr.at[s], j, chip)
        put(txb.at[h], text.at[0, lax.rem(s, H)], ts.at[h], tr.at[lax.rem(s, H)], side, chip)
        return carry

    lax.fori_loop(0, H, send_keys, 0)

    def send_queries(k, carry):
        zt = in_turn(k // 2, 1)
        h = 2 * zt + lax.rem(k, 2)
        chip = 2 * h + c
        cols = pl.ds(pl.multiple_of(h * D, D), D)
        for j in range(2):
            put(img.at[0, pl.ds(HALF * j, HALF), cols], qbuf.at[s], qs.at[h, j], qr.at[s], j, chip)
        return carry

    lax.fori_loop(0, H, send_queries, 0)
    for k in range(1, NI):
        away(reward_own, rewards.at[i], rs, rr, {"img": wrap(i + k, NI)}).start()

    narrow_t[C:] = jnp.where(iota((ONES, NK), 0) == 0, 1.0, 0.0).astype(BF16)

    def lay_out(p, zs):
        four = pl.ds(zs * YN, YN)
        packed = kv[p, four, HALF:, :].reshape(third * YN, D)
        turned = packed.astype(F32).T
        for ab in range(2):
            rows = pl.ds(pl.multiple_of((2 * p + ab) * n3 + zs * (third * YN), third * YN), third * YN)
            block = kv[p, four, third * ab : third * ab + third, :].reshape(third * YN, D)
            keys[rows, :D] = block
            keys[rows, D:] = block
            keys_t[:, rows] = block.astype(F32).T.astype(BF16)
            one = turned[C * ab : C * ab + C]
            narrow_t[:C, rows] = one.astype(BF16)
            narrow[rows] = jnp.concatenate([one, one], axis=0).T.astype(BF16)

    def arrive(n, carry):
        zs = at_distance(n, -1)
        for yy in range(YN):
            src = zs * YN + yy
            drain(kv.at[0, src], kr.at[src])
            away(kv.at[0, src], kv.at[1, src], fs.at[src], fr.at[src], other).start()
        lay_out(0, zs)
        return carry

    lax.fori_loop(0, ZN, arrive, 0)

    def arrive_text(k, carry):
        drain(text.at[0, k], tr.at[k])
        away(text.at[0, k], text.at[1, k], fts.at[k], ftr.at[k], other).start()
        return carry

    lax.fori_loop(0, H, arrive_text, 0)

    def arrive_other(n, carry):
        zs = at_distance(n, -1)
        for yy in range(YN):
            drain(kv.at[1, zs * YN + yy], fr.at[zs * YN + yy])
        lay_out(1, zs)
        return carry

    lax.fori_loop(0, ZN, arrive_other, 0)

    def arrive_other_text(k, carry):
        drain(text.at[1, k], ftr.at[k])
        return carry

    lax.fori_loop(0, H, arrive_other_text, 0)
    words = text[...].astype(F32)
    tk = words[:, :, :TXT, :].reshape(TXT * S, D)
    tv = words[:, :, TXT:, :].reshape(TXT * S, D)
    last = pl.ds(NKI, TXT * S)
    keys[last, :D] = tk.astype(BF16)
    keys[last, D:] = tk.astype(BF16)
    keys_t[:, last] = tk.T.astype(BF16)
    tvt = tv.T[:C]
    narrow_t[:C, last] = tvt.astype(BF16)
    narrow[last] = jnp.concatenate([tvt, tvt], axis=0).T.astype(BF16)

    def over_keys(body, carry):
        for at in range(0, NK, SB):
            carry = body(slice(at, min(at + SB, NK)), carry)
        return carry

    def queries_t(zs):
        for yy in range(YN):
            drain(qbuf.at[zs * YN + yy], qr.at[zs * YN + yy])
        x = qbuf[pl.ds(zs * YN, YN)].reshape(QB, D).astype(F32).T * (D ** (-0.5) * 1.4426950408889634)
        hi = x.astype(BF16)
        return jnp.concatenate([hi, (x - hi.astype(F32)).astype(BF16)], axis=0)

    def score(buf, rows, q_t, top):
        st = jnp.dot(keys[rows], q_t, preferred_element_type=F32)
        buf[rows] = st
        return jnp.maximum(top, jnp.max(st.reshape(st.shape[0] // 8, 8, QB), axis=0))

    def weigh(buf, zs, rows, top, hold):
        e = jnp.exp2(buf[rows] - top).astype(BF16)
        weights[zs, rows] = e
        hold[...] = e

    def mix(rows, hold, mixed):
        return mixed + jnp.dot(narrow_t[:, rows], hold[...], preferred_element_type=F32)

    low_top = jnp.full((8, QB), -jnp.inf, F32)
    no_mix = jnp.zeros((C + ONES, QB), F32)
    branch_share = jnp.where(branch == 0, guidance[0, 0], 1.0 - guidance[0, 0])
    parts_of = NKI // KB
    subs = KB // SB

    def chunk(k, sub):
        return pl.ds(pl.multiple_of(k * KB + sub * SB, SB), SB)

    def first_scores(q_t):
        def body(k, t):
            for sub in range(subs):
                t = score(scores_a, chunk(k, sub), q_t, t)
            return t

        return score(scores_a, last, q_t, lax.fori_loop(0, parts_of, body, low_top))

    def attend(n, now, then, top8, ahead):
        zs = in_turn(n, -1)
        top = jnp.max(top8, axis=0, keepdims=True)
        q_t = queries_t(in_turn(n + 1, -1)) if ahead else None
        next8 = score(then, last, q_t, low_top) if ahead else low_top
        weigh(now, zs, last, top, hold_text)
        mixed = mix(last, hold_text, no_mix)
        holds[subs - 1][...] = jnp.zeros((SB, QB), BF16)

        def body(k, carry):
            next8, mixed = carry
            for sub in range(subs):
                before = chunk(jnp.maximum(k - 1, 0), subs - 1) if sub == 0 else chunk(k, sub - 1)
                mixed = mix(before, holds[sub - 1], mixed)
                if ahead:
                    next8 = score(then, chunk(k, sub), q_t, next8)
                weigh(now, zs, chunk(k, sub), top, holds[sub])
            return next8, mixed

        next8, mixed = lax.fori_loop(0, parts_of, body, (next8, mixed))
        mixed = mix(chunk(parts_of - 1, subs - 1), holds[subs - 1], mixed)
        inverse = 1.0 / mixed[C : C + 1]
        linv[zs] = inverse
        normal = mixed[:C] * inverse
        out_t[zs] = normal
        for m in range(QB // D):
            a, b = pack_pair(normal[:, D * m : D * m + D] * branch_share)
            for yy, part_of in ((2 * m, a), (2 * m + 1, b)):
                msg[zs * YN + yy] = part_of.astype(BF16)
        for yy in range(YN):
            t = zs * YN + yy
            put(msg.at[t], got.at[s], ms, mr, c, t)
        return next8

    top = first_scores(queries_t(in_turn(0, -1)))

    def two(m, top):
        top = attend(2 * m, scores_a, scores_b, top, True)
        return attend(2 * m + 1, scores_b, scores_a, top, True)

    top = lax.fori_loop(0, ZN // 2 - 1, two, top)
    if ZN > 1:
        top = attend(ZN - 2, scores_a, scores_b, top, True)
        attend(ZN - 1, scores_b, scores_a, top, False)
    else:
        attend(0, scores_a, scores_b, top, False)

    noise_own = own_tokens(noise[...])
    old_own = own_tokens(old[...])
    drain(got, mr)
    guided = jnp.sum(got[...].astype(F32), axis=0)
    step = rate[0, 0]
    deviation = step * (guided - old_own)
    g_own[...] = (noise_own - deviation).astype(BF16)

    def share(k, carry):
        zt = at_distance(k, 1)
        for yy in range(YN):
            put(g_own, g_all.at[s], gs, gr.at[s], c, zt * YN + yy)
        return carry

    lax.fori_loop(0, ZN, share, 0)
    partial = jnp.sum(noise_own * deviation - 0.5 * deviation * deviation)
    part[...] = jnp.full(part.shape, partial, F32)

    def tell(k, carry):
        put(part, parts.at[s], ps, pr, c, k)
        return carry

    lax.fori_loop(0, S, tell, 0)
    gk[...] = jnp.zeros_like(gk)

    cols_home = pl.ds(pl.multiple_of(head * D, D), D)
    mine = pl.ds(pl.multiple_of(HALF * c, HALF), HALF)
    FIRST = min(3, ZN)

    def divide(n):
        zs = at_distance(n, -1)
        for yy in range(YN):
            drain(g_all.at[zs * YN + yy], gr.at[zs * YN + yy])
        g_t = jnp.concatenate(
            [
                unpack_pair(g_all[zs * YN + 2 * m].astype(F32), g_all[zs * YN + 2 * m + 1].astype(F32))
                for m in range(QB // D)
            ],
            axis=1,
        )
        g_t = g_t * linv[zs]
        hi = g_t.astype(BF16)
        lo = (g_t - hi.astype(F32)).astype(BF16)
        hi32 = hi.astype(F32)
        gl[zs] = jnp.concatenate([hi, lo], axis=0)
        delta[zs] = jnp.sum((hi32 + lo.astype(F32)) * out_t[zs], axis=0, keepdims=True)
        gl_cols[zs] = jnp.concatenate([hi32, hi32], axis=0).T.astype(BF16)

    def key_grads(n):
        zs = at_distance(n, -1)
        block = qbuf[pl.ds(zs * YN, YN)].reshape(QB, D)
        g_t = gl[zs]
        shift = delta[zs]

        def one(rows, dq_t):
            gp = jnp.dot(narrow[rows], g_t, preferred_element_type=F32)
            ds = (weights[zs, rows].astype(F32) * (gp - shift)).astype(BF16)
            gk[rows] += jnp.dot(ds, block, preferred_element_type=F32)
            return dq_t + jnp.dot(keys_t[:, rows], ds, preferred_element_type=F32)

        return over_keys(one, jnp.zeros((D, QB), F32)).T

    def send_query_grads(n, rows):
        zs = at_distance(n, -1)
        dqb[pl.ds(zs * YN, YN)] = (rows * (factor[...] * D ** (-0.5))).astype(BF16).reshape(YN, HALF, D)
        for yy in range(YN):
            t = zs * YN + yy
            put(dqb.at[t], grad.at[0, mine, cols_home], dqs, dqr, branch, t)

    def first_blocks(n, carry):
        divide(n)
        held[n] = key_grads(n)
        return carry

    lax.fori_loop(0, FIRST, first_blocks, 0)

    def other_blocks(n, carry):
        divide(n)
        return carry

    lax.fori_loop(FIRST, ZN, other_blocks, 0)

    drain(parts, pr)
    pair[0] = jnp.sum(parts[...], axis=0)
    swap = away(pair.at[0], pair.at[1], pairs, pairr, other)
    swap.start()

    def settle():
        if NI > 1:
            drain(rewards.at[pl.ds(0, NI - 1)], rr)
        own_reward = reward_own[...]
        rewards[i] = own_reward
        mean = jnp.sum(rewards[...], axis=0) / NI
        square = jnp.sum(rewards[...] * rewards[...], axis=0) / NI
        deviates = jnp.sqrt(jnp.maximum(square - mean * mean, 0.0))
        advantage = (own_reward - mean) / jnp.maximum(deviates, 1.0)
        swap.wait()
        ratio_now = jnp.exp((pair[0] + pair[1]) / (2 * S * HALF * C))
        clipped = jnp.clip(ratio_now, 0.8, 1.2)
        keep = ratio_now * advantage <= clipped * advantage
        gain = jnp.where(keep, -ratio_now * advantage, 0.0)
        ratio[0, 0] = jnp.max(ratio_now)
        factor[...] = gain * (step * branch_share)

    NG = max(1, n3 // SB)
    GS = S // NG
    GR = third * GS

    def narrow_grad(rows):
        total = jnp.dot(weights[0, rows], gl_cols[0], preferred_element_type=F32)
        for zs in range(1, ZN):
            total = total + jnp.dot(weights[zs, rows], gl_cols[zs], preferred_element_type=F32)
        return total

    def paired(p, r):
        a, b = (
            narrow_grad(pl.ds(pl.multiple_of((2 * p + ab) * n3 + r * GR, GR), GR)) for ab in range(2)
        )
        return jnp.where(iota(a.shape, 1) < C, a, b).reshape(GS, third, D)

    def swap_u(r):
        srcs = pl.ds(r * GS, GS)
        return away(uo.at[srcs], xu.at[srcs], xus.at[r], xur.at[r], other)

    def send_u(r):
        swap_u(r).wait_recv()
        srcs = pl.ds(r * GS, GS)
        uf[srcs] = ((uown[srcs] + xu[srcs].astype(F32)) * factor[...]).astype(BF16)

        def one(k, carry):
            t = r * GS + k
            put(uf.at[t], ub.at[head, c], us, ur, branch, t)
            return carry

        lax.fori_loop(0, GS, one, 0)

    def group(k):
        return wrap(z * NG // ZN + k, NG)

    swaps = [
        away(uto, xut, xs.at[0], xr.at[0], other),
        away(ko, xk, xs.at[1], xr.at[1], other),
        away(kto, xkt, xs.at[2], xr.at[2], other),
    ]
    both_texts = narrow_grad(last)
    both_texts = jnp.where(iota(both_texts.shape, 1) < C, both_texts, 0.0).reshape(2, H, TXT, D)
    no_keys = jnp.zeros((H, TXT, D), F32)
    uto[...] = jnp.concatenate([no_keys, both_texts[1]], axis=1).astype(BF16)
    swaps[0].start()

    def narrow_group(k, carry):
        r = group(k)
        srcs = pl.ds(r * GS, GS)
        uo[srcs] = paired(1, r).astype(BF16)
        swap_u(r).start()
        uown[srcs] = paired(0, r)

        pl.when(k == min(1, NG - 1))(settle)

        @pl.when(k > 0)
        def _():
            send_u(group(k - 1))

        return carry

    lax.fori_loop(0, NG, narrow_group, 0)
    swaps[0].wait_recv()
    utf[...] = (
        (jnp.concatenate([no_keys, both_texts[0]], axis=1) + xut[...].astype(F32)) * factor[...]
    ).astype(BF16)

    def send_text(k, carry):
        put(utf.at[k], utb.at[head], uts, utr, branch, c * H + k)
        return carry

    lax.fori_loop(0, H, send_text, 0)
    send_u(group(NG - 1))

    def send_held(n, carry):
        send_query_grads(n, held[n])
        return carry

    lax.fori_loop(0, FIRST, send_held, 0)

    def widen_all():
        drain(ub, ur)
        drain(utb, utr)

        def widen(h):
            at = pl.ds(pl.multiple_of(h * D, D), D)
            r = rt[:, at]
            twice = jnp.concatenate([r, r], axis=0)
            low = iota((third, D), 1) < C
            u0, u1 = ub[h, 0].astype(F32), ub[h, 1].astype(F32)
            spaced = jnp.concatenate(
                [
                    jnp.where(low, u0, 0.0),
                    jnp.where(low, 0.0, u0),
                    jnp.where(low, u1, 0.0),
                    jnp.where(low, 0.0, u1),
                    utb[h].astype(F32),
                ],
                axis=0,
            )
            wide = jnp.dot(spaced.astype(BF16), twice, preferred_element_type=F32)
            dv[:, at] = wide[: 2 * HALF].astype(BF16)
            dvt[:, at] = wide[2 * HALF + TXT :]
            values = jnp.concatenate([vbuf[:, at], tx[:, at]], axis=0)
            res = jnp.dot(spaced.T.astype(BF16), values, preferred_element_type=F32)
            rgp[:, at] = res[:C] + res[C:]

        some(H, widen)
        pltpu.make_async_copy(dv, grad.at[2], dvsem).start()

    HW = NI * W

    def half(core):
        return pl.ds(pl.multiple_of(core * HW, D), HW)

    def piece(n):
        return pl.ds(pl.multiple_of(n * W, D), W)

    def strip(n):
        return pl.ds(pl.multiple_of(n * RY, 8), RY)

    def readout_1():
        away(rgp.at[:, half(1 - c)], rx, as_.at[0], ar.at[0], other).start()

    def readout_2():
        drain(rx, ar.at[0])
        rh[...] = rgp[:, half(c)] + rx[...]
        rhb[...] = rh[...].astype(BF16)
        for k in range(1, NI):
            n = wrap(i + k, NI)
            away(rhb.at[:, piece(n)], r1.at[i], as_.at[5], ar.at[5], {"img": n}).start()

    def readout_3():
        if NI > 1:
            drain(r1.at[pl.ds(0, NI - 1)], ar.at[5])
        r1[i] = jnp.zeros((C, W), BF16)
        a1[...] = jnp.sum(r1[...].astype(F32), axis=0) + rh[:, piece(i)]
        for k in range(1, YN):
            n = wrap(y + k, YN)
            away(a1.at[strip(n)], r2.at[y], as_.at[1], ar.at[1], {"seq": z * YN + n}).start()

    def readout_4():
        drain(r2.at[pl.ds(0, YN - 1)], ar.at[1])
        r2[y] = a1[strip(y), :]
        a2[...] = jnp.sum(r2[...], axis=0)
        for k in range(1, ZN):
            n = wrap(z + k, ZN)
            away(a2, r3.at[z], as_.at[2], ar.at[2], {"seq": n * YN + y}).start()

    def readout_5():
        if ZN > 1:
            drain(r3.at[pl.ds(0, ZN - 1)], ar.at[2])
        r3[z] = a2[...]
        a3[...] = jnp.sum(r3[...], axis=0)
        for k in range(1, YN):
            n = wrap(y + k, YN)
            away(a3, r4.at[y], as_.at[3], ar.at[3], {"seq": z * YN + n}).start()

    def readout_6():
        drain(r4.at[pl.ds(0, YN - 1)], ar.at[3])
        r4[y] = a3[...]
        to = rg.at[:, :, pl.ds(pl.multiple_of(c * HW + i * W, D), W)]
        pltpu.make_async_copy(r4, to, ls).start()
        for k in range(NI):
            n = wrap(i + k, NI)
            for core in (c, 1 - c) if k else (1 - c,):
                away(r4, to, as_.at[4], ar.at[4], {"cfg": core, "img": n}).start()

    steps = dict(
        widen_all=widen_all, readout_1=readout_1, readout_2=readout_2, readout_3=readout_3,
        readout_4=readout_4,
    )

    def other_key_grads(n, carry):
        send_query_grads(n, key_grads(n))
        for at, what in EVENTS:
            pl.when(n == min(at, ZN - 1))(steps[what])
        return carry

    lax.fori_loop(FIRST, ZN, other_key_grads, 0)
    if ZN <= FIRST:
        for at, what in EVENTS:
            steps[what]()

    def image_keys(p):
        base = 2 * p * n3
        a = gk[base : base + n3].reshape(S, third, D)
        b = gk[base + n3 : base + 2 * n3].reshape(S, third, D)
        return jnp.concatenate([a, b], axis=1) * (factor[...] * D ** (-0.5))

    def text_keys(p):
        k = gk[NKI + p * H * TXT : NKI + (p + 1) * H * TXT]
        k = (k * (factor[...] * D ** (-0.5))).reshape(H, TXT, D)
        return jnp.concatenate([k, jnp.zeros_like(k)], axis=1)

    ko[...] = image_keys(1).astype(BF16)
    swaps[1].start()
    kto[...] = text_keys(1).astype(BF16)
    swaps[2].start()
    swaps[1].wait_recv()
    kf[...] = (image_keys(0) + xk[...].astype(F32)).astype(BF16)

    def send_key_grads(k, carry):
        zt = at_distance(ZN - 1 - k, 1)
        for yy in range(YN):
            t = zt * YN + yy
            put(kf.at[t], grad.at[1, mine, cols_home], dks, dkr, branch, t)
        return carry

    lax.fori_loop(0, ZN // 2, send_key_grads, 0)
    readout_5()
    lax.fori_loop(ZN // 2, ZN, send_key_grads, 0)
    swaps[2].wait_recv()
    ktf[...] = (text_keys(0) + xkt[...].astype(F32)).astype(BF16)

    def send_text_keys(k, carry):
        put(ktf.at[k], ktb.at[head], kts, ktr, branch, c * H + k)
        return carry

    lax.fori_loop(0, H, send_text_keys, 0)
    readout_6()

    def sent(k, carry):
        chip = 2 * k + c
        for odd in range(2):
            src = 2 * k + odd
            drain(kv.at[1, src], fs.at[src])
        drain(text.at[1, k], fts.at[k])
        for j in range(2):
            @pl.when(jnp.logical_not(jnp.logical_and(chip == s, j == c)))
            def _():
                drain(kv.at[0, 0], ks.at[k, j])
                drain(qbuf.at[0], qs.at[k, j])

        @pl.when(jnp.logical_not(jnp.logical_and(chip == s, side == c)))
        def _():
            drain(text.at[0, 0], ts.at[k])

        return carry

    lax.fori_loop(0, H, sent, 0)
    drain(got.at[pl.ds(0, S - 1)], ms)
    drain(g_all.at[pl.ds(0, S - 1)], gs)
    drain(parts.at[pl.ds(0, S - 1)], ps)
    if NI > 1:
        drain(rewards.at[pl.ds(0, NI - 1)], rs)
    for w in swaps:
        w.wait_send()
    drain(rx, as_.at[0])
    if NI > 1:
        drain(r1.at[pl.ds(0, NI - 1)], as_.at[5])
    drain(r2.at[pl.ds(0, YN - 1)], as_.at[1])
    if ZN > 1:
        drain(r3.at[pl.ds(0, ZN - 1)], as_.at[2])
    drain(r4.at[pl.ds(0, YN - 1)], as_.at[3])
    drain(rgp.at[:, pl.ds(0, (NP - 1) * W)], as_.at[4])
    drain(r4, ls)
    drain(rgp.at[:, pl.ds(0, (NP - 1) * W)], ar.at[4])

    def swapped_u(r, carry):
        swap_u(r).wait_send()
        return carry

    lax.fori_loop(0, NG, swapped_u, 0)
    drain(dv, dvsem)
    text_here = jnp.logical_and(branch == c, s // H == c)

    @pl.when(branch == c)
    def _():
        drain(uf.at[pl.ds(0, S - 1)], us)
        drain(dqb.at[pl.ds(0, S - 1)], dqs)
        drain(kf.at[pl.ds(0, S - 1)], dks)

    @pl.when(branch != c)
    def _():
        drain(uf, us)
        drain(dqb, dqs)
        drain(kf, dks)

    @pl.when(text_here)
    def _():
        drain(utf.at[pl.ds(0, H - 1)], uts)
        drain(ktf.at[pl.ds(0, H - 1)], kts)

    @pl.when(jnp.logical_not(text_here))
    def _():
        drain(utf, uts)
        drain(ktf, kts)

    drain(ktb, ktr)

    def text_home(h, carry):
        at = pl.ds(pl.multiple_of(h * D, D), D)
        dkt[:, at] = ktb[h].astype(F32)[:TXT]
        return carry

    lax.fori_loop(0, H, text_home, 0)
    tgrad[...] = jnp.stack([dkt[...], dvt[...]], axis=1).astype(BF16)
    drain(grad.at[0], dqr)
    drain(grad.at[1], dkr)


EVENTS = (
    (4, "widen_all"),
    (4, "readout_1"),
    (5, "readout_2"),
    (6, "readout_3"),
    (7, "readout_4"),
)


def step_call(S, NI, guidance, rate, reward, img, txt, rt, noise, old):
    H, ZN, NP = S // 2, S // YN, 2 * NI
    HD = rt.shape[1]
    W, RY, third = HD // NP, C // YN, HALF // 2
    NK = (2 * HALF + TXT) * S
    dma = pltpu.SemaphoreType.DMA
    tile = (1, D)
    b = lambda *shape: pltpu.VMEM(shape, BF16)
    w = lambda *shape: pltpu.VMEM(shape, F32)
    return pl.pallas_call(
        functools.partial(step_kernel, S, NI),
        out_shape=(
            jax.ShapeDtypeStruct(img.shape, BF16),
            jax.ShapeDtypeStruct((TXT, 2, HD), BF16),
            jax.ShapeDtypeStruct((YN, RY, HD), F32),
            jax.ShapeDtypeStruct((1, 1), F32),
        ),
        in_specs=[SMEM, SMEM, SMEM, ANY, VMEM, VMEM, VMEM, VMEM],
        out_specs=(ANY, VMEM, ANY, SMEM),
        scratch_shapes=[
            b(2 * TXT, HD),
            b(*img.shape[1:]),
            b(H, 2, third, D),
            b(H, 2 * TXT, D),
            b(2, S, HALF + third, D),
            b(2, H, 2 * TXT, D),
            b(S, HALF, D),
            b(NK, 2 * D),
            b(D, NK),
            b(NK, D),
            b(C + ONES, NK),
            w(NK, QB),
            w(NK, QB),
            *([b(SB, QB)] * 4),
            b(TXT * S, QB),
            b(ZN, NK, QB),
            w(ZN, C, QB),
            w(ZN, 1, QB),
            b(S, C // 2, D),
            b(S, C // 2, D),
            b(C // 2, D),
            b(S, C // 2, D),
            w(*tile),
            w(S, *tile),
            w(2, *tile),
            w(NI, *tile),
            w(*tile),
            b(ZN, 2 * C, QB),
            b(ZN, QB, D),
            w(ZN, 1, QB),
            w(NK, D),
            w(*tile),
            w(min(3, ZN), QB, D),
            b(S, third, D),
            b(S, third, D),
            w(S, third, D),
            b(S, third, D),
            b(H, 2 * TXT, D),
            b(H, 2 * TXT, D),
            b(H, 2 * TXT, D),
            b(S, HALF, D),
            b(S, HALF, D),
            b(S, HALF, D),
            b(H, 2 * TXT, D),
            b(H, 2 * TXT, D),
            b(H, 2 * TXT, D),
            b(S, HALF, D),
            b(H, 2, third, D),
            b(H, 2 * TXT, D),
            b(H, 2 * TXT, D),
            b(*img.shape[1:]),
            w(TXT, HD),
            w(TXT, HD),
            w(C, HD),
            w(C, NI * W),
            w(C, NI * W),
            b(C, NI * W),
            b(NI, C, W),
            w(C, W),
            w(YN, RY, W),
            w(RY, W),
            w(ZN, RY, W),
            w(RY, W),
            w(YN, RY, W),
            dma,
            dma((H, 2)), dma((S,)),
            dma((H, 2)), dma((S,)),
            dma((H,)), dma((H,)),
            dma((S,)), dma((S,)),
            dma((H,)), dma((H,)),
            dma, dma,
            dma, dma((S,)),
            dma, dma,
            dma, dma,
            dma, dma,
            dma((3,)), dma((3,)),
            dma((max(1, third * S // SB),)), dma((max(1, third * S // SB),)),
            dma, dma,
            dma, dma,
            dma, dma,
            dma, dma,
            dma, dma,
            dma,
            dma((6,)), dma((6,)),
            dma,
        ],
        compiler_params=pltpu.CompilerParams(
            collective_id=0, has_side_effects=True, vmem_limit_bytes=LIMIT
        ),
        name="step",
    )(guidance, rate, reward, img, txt, rt, noise, old)


def on_device(S, NI, img_qkv, txt_kv, readout, old_velocity, noise, step_ratio, rewards, guidance):
    img = img_qkv[0, 0].transpose(1, 0, 2)
    text = txt_kv[0, 0]
    scalar = lambda x: x.reshape(1, 1)
    grad, tgrad, rg, ratio = step_call(
        S, NI, scalar(guidance), scalar(step_ratio), scalar(rewards), img, text, readout.T, noise[0].T, old_velocity[0].T
    )
    img_grad = grad.transpose(1, 0, 2)[None, None]
    return (img_grad, tgrad[None, None], rg.reshape(C, -1).T, ratio.reshape(1))


def solution(mesh):
    S, NI = mesh.shape["seq"], mesh.shape["img"]
    placed = (
        P("cfg", "img", "seq", None, None),
        P("cfg", "img", "seq", None, None),
        P(),
        P("img", "seq", None),
        P("img", "seq", None),
        P("img"),
        P("img"),
        P(),
    )
    return jax.shard_map(
        functools.partial(on_device, S, NI),
        mesh=mesh,
        in_specs=placed,
        out_specs=(
            P("cfg", "img", "seq", None, None),
            P("cfg", "img", "seq", None, None),
            P(),
            P("img"),
        ),
        check_vma=False,
    )
```

```python
import functools

import jax
import jax.numpy as jnp
from jax import lax
from jax.experimental import pallas as pl
from jax.experimental.pallas import tpu as pltpu
from jax.sharding import PartitionSpec as P

D = 128
C = 64
HALF = 64
TXT = 8
YN = 4
QB = 256
KB = 4096
SB = 256
BB = 2176
UB = 512
ONES = 16
MESH = pl.DeviceIdType.MESH
F32 = jnp.float32
BF16 = jnp.bfloat16
NT = (((1,), (1,)), ((), ()))
TN = (((0,), (0,)), ((), ()))
ANY = pl.BlockSpec(memory_space=pl.ANY)
VMEM = pl.BlockSpec(memory_space=pltpu.VMEM)
SMEM = pl.BlockSpec(memory_space=pltpu.SMEM)
LIMIT = 60 * 1024 * 1024


def iota(shape, dim):
    return lax.broadcasted_iota(jnp.int32, shape, dim)


def put(src, dst, send, recv, core, chip):
    here = jnp.logical_and(core == lax.axis_index("cfg"), chip == lax.axis_index("seq"))

    @pl.when(here)
    def _():
        pltpu.make_async_copy(src, dst, recv).start()

    @pl.when(jnp.logical_not(here))
    def _():
        away(src, dst, send, recv, {"cfg": core, "seq": chip}).start()


def away(src, dst, send, recv, device):
    return pltpu.make_async_remote_copy(
        src_ref=src,
        dst_ref=dst,
        send_sem=send,
        recv_sem=recv,
        device_id=device,
        device_id_type=MESH,
    )


def drain(ref, sem):
    pltpu.make_async_copy(ref, ref, sem).wait()


def wrap(at, size):
    return jnp.where(at >= size, at - size, at)


def signal_plane(chips):
    c, s = lax.axis_index("cfg"), lax.axis_index("seq")
    barrier = pltpu.get_barrier_semaphore()

    def tell(device):
        pl.semaphore_signal(barrier, inc=1, device_id=device, device_id_type=MESH)

    def one(k, carry):
        chip = wrap(s + k, chips)
        tell({"cfg": c, "seq": chip})
        tell({"cfg": 1 - c, "seq": chip})
        return carry

    lax.fori_loop(1, chips, one, 0)
    tell({"cfg": 1 - c})
    return barrier


def pack_pair(x):
    top, low = x[: C // 2], x[C // 2 :]
    lower = iota(top.shape, 1) < HALF
    return (
        jnp.where(lower, top, pltpu.roll(low, HALF, 1)),
        jnp.where(lower, pltpu.roll(top, HALF, 1), low),
    )


def unpack_pair(a, b):
    lower = iota(a.shape, 1) < HALF
    return jnp.concatenate(
        [jnp.where(lower, a, pltpu.roll(b, HALF, 1)), jnp.where(lower, pltpu.roll(a, HALF, 1), b)], axis=0
    )


def own_tokens(x):
    a, b = pack_pair(x)
    return jnp.where(lax.axis_index("cfg") == 0, a, b)


def step_kernel(
    S, NI, guidance, rate, reward, img, txt, rt, noise, old,
    grad, tgrad, rg, ratio,
    tx, vbuf, vrp, txb, kv, text, qbuf, keys, keys_t, narrow, narrow_t, scores_a, scores_b, hold, hold_text, weights, out_t, linv,
    msg, got, g_own, g_all, part, parts, pair, rewards, reward_own, gl, gl_cols, delta, gk, factor, held,
    uo, xu, uown, uf, uto, xut, utf, ko, xk, kf, kto, xkt, ktf, dqb, ub, utb, ktb, dv, dkt, dvt, rgp, rgb, r1, a1, r2, a2, r3, a3, r4, r4b,
    vsem, ks, kr, qs, qr, ts, tr, fs, fr, fts, ftr, ms, mr, gs, gr, ps, pr, pairs, pairr, rs, rr,
    xs, xr, xus, xur, us, ur, uts, utr, dqs, dqr, dks, dkr, kts, ktr, dvsem, as_, ar, ls,
):
    H = S // 2
    ZN = S // YN
    NP = 2 * NI
    W = rgp.shape[1] // NP
    RY = C // YN
    NK = keys.shape[0]
    NKI = 2 * HALF * S
    KT = min(KB, NKI)
    subs = KT // SB
    third = HALF // 2
    n3 = third * S
    c, i, s = lax.axis_index("cfg"), lax.axis_index("img"), lax.axis_index("seq")
    head, branch = s // 2, lax.rem(s, 2)
    y, z = lax.rem(s, YN), s // YN
    other = {"cfg": 1 - c}

    vcopy = pltpu.make_async_copy(img.at[2], vbuf, vsem)
    vcopy.start()
    barrier = signal_plane(S)
    for k in range(1, NI):
        for core in range(2):
            pl.semaphore_signal(
                barrier, inc=1, device_id={"cfg": core, "img": wrap(i + k, NI)}, device_id_type=MESH
            )
    words = txt[...].astype(F32)
    tx[...] = jnp.concatenate([words[:, 0], words[:, 1]], axis=0).astype(BF16)
    vcopy.wait()
    reward_own[...] = jnp.full(reward_own.shape, reward[0, 0], F32)

    def squeeze(h):
        cols = pl.ds(pl.multiple_of(h * D, D), D)
        r = rt[:, cols]
        twice = jnp.concatenate([r, r], axis=0)
        x = lax.dot_general(vbuf[:, cols], twice, NT, preferred_element_type=F32)
        low = iota((third, D), 1) < C
        for j in range(2):
            first = x[HALF * j : HALF * j + third]
            second = x[HALF * j + third : HALF * j + HALF]
            vrp[h, j] = jnp.where(low, first, second).astype(BF16)
        t = tx[:, cols]
        yv = lax.dot_general(t, twice, NT, preferred_element_type=F32)
        yv = jnp.where(iota(yv.shape, 1) < C, yv, 0.0)
        txb[h] = jnp.where(iota(yv.shape, 0) < TXT, t.astype(F32), yv).astype(BF16)

    def some(count, body):
        at_once = 4 if count % 4 == 0 else 1

        def trip(k, carry):
            for j in range(at_once):
                body(k * at_once + j)
            return carry

        lax.fori_loop(0, count // at_once, trip, 0)

    some(H, squeeze)
    pl.semaphore_wait(barrier, 2 * S - 1 + 2 * (NI - 1))

    side = s // H

    def at_distance(n, sign):
        half = (n + 1) // 2
        far = jnp.where(n == 2 * half, ZN - half, half)
        return wrap(z + far, ZN) if sign > 0 else wrap(z + ZN - far, ZN)

    def in_turn(n, sign):
        if ZN < 4:
            return at_distance(n, sign)
        return at_distance(jnp.where(n == 0, 0, jnp.where(n <= ZN - 3, n + 2, n - (ZN - 3))), sign)

    def send_keys(k, carry):
        zt = at_distance(ZN - 1 - k // 2, 1)
        h = 2 * zt + lax.rem(k, 2)
        chip = 2 * h + c
        cols = pl.ds(pl.multiple_of(h * D, D), D)
        for j in range(2):
            put(img.at[1, pl.ds(HALF * j, HALF), cols], kv.at[0, s, pl.ds(0, HALF)], ks.at[h, j], kr.at[s], j, chip)
            put(vrp.at[h, j], kv.at[0, s, pl.ds(HALF, third)], ks.at[h, j], kr.at[s], j, chip)
        put(txb.at[h], text.at[0, lax.rem(s, H)], ts.at[h], tr.at[lax.rem(s, H)], side, chip)
        return carry

    lax.fori_loop(0, H, send_keys, 0)

    def send_queries(k, carry):
        zt = in_turn(k // 2, 1)
        h = 2 * zt + lax.rem(k, 2)
        chip = 2 * h + c
        cols = pl.ds(pl.multiple_of(h * D, D), D)
        for j in range(2):
            put(img.at[0, pl.ds(HALF * j, HALF), cols], qbuf.at[s], qs.at[h, j], qr.at[s], j, chip)
        return carry

    lax.fori_loop(0, H, send_queries, 0)
    for k in range(1, NI):
        away(reward_own, rewards.at[i], rs, rr, {"img": wrap(i + k, NI)}).start()

    narrow_t[C:] = jnp.where(iota((ONES, NK), 0) == 0, 1.0, 0.0).astype(BF16)

    def lay_out(p, zs):
        four = pl.ds(zs * YN, YN)
        packed = kv[p, four, HALF:, :].reshape(third * YN, D)
        turned = packed.astype(F32).T
        for ab in range(2):
            rows = pl.ds(pl.multiple_of((2 * p + ab) * n3 + zs * (third * YN), third * YN), third * YN)
            block = kv[p, four, third * ab : third * ab + third, :].reshape(third * YN, D)
            keys[rows, :D] = block
            keys[rows, D:] = block
            keys_t[:, rows] = block.astype(F32).T.astype(BF16)
            one = turned[C * ab : C * ab + C]
            narrow_t[:C, rows] = one.astype(BF16)
            narrow[rows] = jnp.concatenate([one, one], axis=0).T.astype(BF16)

    def arrive(n, carry):
        zs = at_distance(ZN - 1 - n, -1)
        for yy in range(YN):
            src = zs * YN + yy
            drain(kv.at[0, src], kr.at[src])
            away(kv.at[0, src], kv.at[1, src], fs.at[src], fr.at[src], other).start()
        lay_out(0, zs)
        return carry

    lax.fori_loop(0, ZN, arrive, 0)

    def arrive_text(k, carry):
        drain(text.at[0, k], tr.at[k])
        away(text.at[0, k], text.at[1, k], fts.at[k], ftr.at[k], other).start()
        return carry

    lax.fori_loop(0, H, arrive_text, 0)

    def arrive_other(n, carry):
        zs = at_distance(ZN - 1 - n, -1)
        for yy in range(YN):
            drain(kv.at[1, zs * YN + yy], fr.at[zs * YN + yy])
        lay_out(1, zs)
        return carry

    lax.fori_loop(0, ZN, arrive_other, 0)

    def arrive_other_text(k, carry):
        drain(text.at[1, k], ftr.at[k])
        return carry

    lax.fori_loop(0, H, arrive_other_text, 0)
    words = text[...].astype(F32)
    tk = words[:, :, :TXT, :].reshape(TXT * S, D)
    tv = words[:, :, TXT:, :].reshape(TXT * S, D)
    last = pl.ds(NKI, TXT * S)
    keys[last, :D] = tk.astype(BF16)
    keys[last, D:] = tk.astype(BF16)
    keys_t[:, last] = tk.T.astype(BF16)
    tvt = tv.T[:C]
    narrow_t[:C, last] = tvt.astype(BF16)
    narrow[last] = jnp.concatenate([tvt, tvt], axis=0).T.astype(BF16)

    def over_keys(body, carry):
        for at in range(0, NK, BB):
            carry = body(slice(at, min(at + BB, NK)), carry)
        return carry

    def queries_t(zs):
        for yy in range(YN):
            drain(qbuf.at[zs * YN + yy], qr.at[zs * YN + yy])
        x = qbuf[pl.ds(zs * YN, YN)].reshape(QB, D).astype(F32).T * (D ** (-0.5) * 1.4426950408889634)
        hi = x.astype(BF16)
        return jnp.concatenate([hi, (x - hi.astype(F32)).astype(BF16)], axis=0)

    def score(buf, rows, q_t, top):
        st = jnp.dot(keys[rows], q_t, preferred_element_type=F32)
        buf[rows] = st
        return jnp.maximum(top, jnp.max(st.reshape(st.shape[0] // 8, 8, QB), axis=0))

    def weigh(buf, zs, rows, top, hold):
        e = jnp.exp2(buf[rows] - top).astype(BF16)
        weights[zs, rows] = e
        hold[...] = e

    def mix(rows, hold, mixed):
        return mixed + jnp.dot(narrow_t[:, rows], hold[...], preferred_element_type=F32)

    low_top = jnp.full((8, QB), -jnp.inf, F32)
    no_mix = jnp.zeros((C + ONES, QB), F32)
    branch_share = jnp.where(branch == 0, guidance[0, 0], 1.0 - guidance[0, 0])
    parts_of = NKI // KT

    def chunk(k, sub):
        return pl.ds(pl.multiple_of(k * KT + sub * SB, SB), SB)

    def first_scores(q_t):
        def body(k, t):
            for sub in range(subs):
                t = score(scores_a, chunk(k, sub), q_t, t)
            return t

        return score(scores_a, last, q_t, lax.fori_loop(0, parts_of, body, low_top))

    def attend(n, now, then, top8, ahead):
        zs = in_turn(n, -1)
        top = jnp.max(top8, axis=0, keepdims=True)
        q_t = queries_t(in_turn(n + 1, -1)) if ahead else None
        next8 = score(then, last, q_t, low_top) if ahead else low_top
        weigh(now, zs, last, top, hold_text)
        mixed = mix(last, hold_text, no_mix)
        hold[subs - 1] = jnp.zeros((SB, QB), BF16)

        def body(k, carry):
            next8, mixed = carry
            for sub in range(subs):
                before = chunk(jnp.maximum(k - 1, 0), subs - 1) if sub == 0 else chunk(k, sub - 1)
                mixed = mix(before, hold.at[(sub - 1) % subs], mixed)
                if ahead:
                    next8 = score(then, chunk(k, sub), q_t, next8)
                weigh(now, zs, chunk(k, sub), top, hold.at[sub])
            return next8, mixed

        next8, mixed = lax.fori_loop(0, parts_of, body, (next8, mixed))
        mixed = mix(chunk(parts_of - 1, subs - 1), hold.at[subs - 1], mixed)
        inverse = 1.0 / mixed[C : C + 1]
        linv[zs] = inverse
        normal = mixed[:C] * inverse
        out_t[zs] = normal
        for m in range(QB // D):
            a, b = pack_pair(normal[:, D * m : D * m + D] * branch_share)
            for yy, part_of in ((2 * m, a), (2 * m + 1, b)):
                msg[zs * YN + yy] = part_of.astype(BF16)
        for yy in range(YN):
            t = zs * YN + yy
            put(msg.at[t], got.at[s], ms, mr, c, t)
        return next8

    top = first_scores(queries_t(in_turn(0, -1)))

    def two(m, top):
        top = attend(2 * m, scores_a, scores_b, top, True)
        return attend(2 * m + 1, scores_b, scores_a, top, True)

    top = lax.fori_loop(0, ZN // 2 - 1, two, top)
    if ZN > 1:
        top = attend(ZN - 2, scores_a, scores_b, top, True)
        attend(ZN - 1, scores_b, scores_a, top, False)
    else:
        attend(0, scores_a, scores_b, top, False)

    noise_own = own_tokens(noise[...])
    old_own = own_tokens(old[...])
    drain(got, mr)
    guided = jnp.sum(got[...].astype(F32), axis=0)
    step = rate[0, 0]
    deviation = step * (guided - old_own)
    g_own[...] = (noise_own - deviation).astype(BF16)

    def share(k, carry):
        zt = at_distance(k, 1)
        for yy in range(YN):
            put(g_own, g_all.at[s], gs, gr.at[s], c, zt * YN + yy)
        return carry

    lax.fori_loop(0, ZN, share, 0)
    partial = jnp.sum(noise_own * deviation - 0.5 * deviation * deviation)
    part[...] = jnp.full(part.shape, partial, F32)

    def tell(k, carry):
        put(part, parts.at[s], ps, pr, c, k)
        return carry

    lax.fori_loop(0, S, tell, 0)
    gk[...] = jnp.zeros_like(gk)

    cols_home = pl.ds(pl.multiple_of(head * D, D), D)
    mine = pl.ds(pl.multiple_of(HALF * c, HALF), HALF)
    FIRST = min(3, ZN)

    def divide(n):
        zs = at_distance(n, -1)
        for yy in range(YN):
            drain(g_all.at[zs * YN + yy], gr.at[zs * YN + yy])
        g_t = jnp.concatenate(
            [
                unpack_pair(g_all[zs * YN + 2 * m].astype(F32), g_all[zs * YN + 2 * m + 1].astype(F32))
                for m in range(QB // D)
            ],
            axis=1,
        )
        g_t = g_t * linv[zs]
        hi = g_t.astype(BF16)
        lo = (g_t - hi.astype(F32)).astype(BF16)
        hi32 = hi.astype(F32)
        gl[zs] = jnp.concatenate([hi, lo], axis=0)
        delta[zs] = jnp.sum((hi32 + lo.astype(F32)) * out_t[zs], axis=0, keepdims=True)
        gl_cols[zs] = jnp.concatenate([hi32, hi32], axis=0).T.astype(BF16)

    def key_grads(n):
        zs = at_distance(n, -1)
        block = qbuf[pl.ds(zs * YN, YN)].reshape(QB, D)
        g_t = gl[zs]
        shift = delta[zs]

        def one(rows, dq_t):
            gp = jnp.dot(narrow[rows], g_t, preferred_element_type=F32)
            ds = (weights[zs, rows].astype(F32) * (gp - shift)).astype(BF16)
            gk[rows] += jnp.dot(ds, block, preferred_element_type=F32)
            return dq_t + jnp.dot(keys_t[:, rows], ds, preferred_element_type=F32)

        return over_keys(one, jnp.zeros((D, QB), F32)).T

    def send_query_grads(n, rows):
        zs = at_distance(n, -1)
        dqb[pl.ds(zs * YN, YN)] = (rows * (factor[...] * D ** (-0.5))).astype(BF16).reshape(YN, HALF, D)
        for yy in range(YN):
            t = zs * YN + yy
            put(dqb.at[t], grad.at[0, mine, cols_home], dqs, dqr, branch, t)

    def first_blocks(n, carry):
        divide(n)
        held[n] = key_grads(n)
        return carry

    lax.fori_loop(0, FIRST, first_blocks, 0)

    def other_blocks(n, carry):
        divide(n)
        return carry

    lax.fori_loop(FIRST, ZN, other_blocks, 0)

    drain(parts, pr)
    pair[0] = jnp.sum(parts[...], axis=0)
    swap = away(pair.at[0], pair.at[1], pairs, pairr, other)
    swap.start()

    def settle():
        if NI > 1:
            drain(rewards.at[pl.ds(0, NI - 1)], rr)
        own_reward = reward_own[...]
        rewards[i] = own_reward
        mean = jnp.sum(rewards[...], axis=0) / NI
        square = jnp.sum(rewards[...] * rewards[...], axis=0) / NI
        deviates = jnp.sqrt(jnp.maximum(square - mean * mean, 0.0))
        advantage = (own_reward - mean) / jnp.maximum(deviates, 1.0)
        swap.wait()
        ratio_now = jnp.exp((pair[0] + pair[1]) / (2 * S * HALF * C))
        clipped = jnp.clip(ratio_now, 0.8, 1.2)
        keep = ratio_now * advantage <= clipped * advantage
        gain = jnp.where(keep, -ratio_now * advantage, 0.0)
        ratio[0, 0] = jnp.max(ratio_now)
        factor[...] = gain * (step * branch_share)

    NG = max(1, n3 // UB)
    GS = S // NG
    GR = third * GS

    def narrow_grad(rows):
        total = jnp.dot(weights[0, rows], gl_cols[0], preferred_element_type=F32)
        for zs in range(1, ZN):
            total = total + jnp.dot(weights[zs, rows], gl_cols[zs], preferred_element_type=F32)
        return total

    def paired(p, r):
        a, b = (
            narrow_grad(pl.ds(pl.multiple_of((2 * p + ab) * n3 + r * GR, GR), GR)) for ab in range(2)
        )
        return jnp.where(iota(a.shape, 1) < C, a, b).reshape(GS, third, D)

    def swap_u(r):
        srcs = pl.ds(r * GS, GS)
        return away(uo.at[srcs], xu.at[srcs], xus.at[r], xur.at[r], other)

    def send_u(r):
        swap_u(r).wait_recv()
        srcs = pl.ds(r * GS, GS)
        uf[srcs] = ((uown[srcs] + xu[srcs].astype(F32)) * factor[...]).astype(BF16)

        def one(k, carry):
            t = r * GS + k
            put(uf.at[t], ub.at[head, c], us, ur, branch, t)
            return carry

        lax.fori_loop(0, GS, one, 0)

    def group(k):
        return wrap(z * NG // ZN + k, NG)

    swaps = [
        away(uto, xut, xs.at[0], xr.at[0], other),
        away(ko, xk, xs.at[1], xr.at[1], other),
        away(kto, xkt, xs.at[2], xr.at[2], other),
    ]
    both_texts = narrow_grad(last)
    both_texts = jnp.where(iota(both_texts.shape, 1) < C, both_texts, 0.0).reshape(2, H, TXT, D)
    no_keys = jnp.zeros((H, TXT, D), F32)
    uto[...] = jnp.concatenate([no_keys, both_texts[1]], axis=1).astype(BF16)
    swaps[0].start()

    def narrow_group(k, carry):
        r = group(k)
        srcs = pl.ds(r * GS, GS)
        uo[srcs] = paired(1, r).astype(BF16)
        swap_u(r).start()
        pl.when(k == min(1, NG - 1))(settle)

        @pl.when(k > 0)
        def _():
            send_u(group(k - 1))

        uown[srcs] = paired(0, r)

        return carry

    lax.fori_loop(0, NG, narrow_group, 0)
    swaps[0].wait_recv()
    utf[...] = (
        (jnp.concatenate([no_keys, both_texts[0]], axis=1) + xut[...].astype(F32)) * factor[...]
    ).astype(BF16)

    def send_text(k, carry):
        put(utf.at[k], utb.at[head], uts, utr, branch, c * H + k)
        return carry

    lax.fori_loop(0, H, send_text, 0)
    send_u(group(NG - 1))

    def send_held(n, carry):
        send_query_grads(n, held[n])
        return carry

    lax.fori_loop(0, FIRST, send_held, 0)

    def widen_all():
        drain(ub, ur)
        drain(utb, utr)

        def widen(h):
            at = pl.ds(pl.multiple_of(h * D, D), D)
            r = rt[:, at]
            twice = jnp.concatenate([r, r], axis=0)
            low = iota((third, D), 1) < C
            u0, u1 = ub[h, 0].astype(F32), ub[h, 1].astype(F32)
            spaced = jnp.concatenate(
                [
                    jnp.where(low, u0, 0.0),
                    jnp.where(low, 0.0, u0),
                    jnp.where(low, u1, 0.0),
                    jnp.where(low, 0.0, u1),
                    utb[h].astype(F32),
                ],
                axis=0,
            )
            wide = jnp.dot(spaced.astype(BF16), twice, preferred_element_type=F32)
            dv[:, at] = wide[: 2 * HALF].astype(BF16)
            dvt[:, at] = wide[2 * HALF + TXT :]
            values = jnp.concatenate([vbuf[:, at], tx[:, at]], axis=0)
            res = jnp.dot(spaced.T.astype(BF16), values, preferred_element_type=F32)
            rgp[:, at] = res[:C] + res[C:]

        some(H, widen)
        pltpu.make_async_copy(dv, grad.at[2], dvsem).start()

    me = 2 * i + c

    def piece(n):
        return pl.ds(pl.multiple_of(n * W, D), W)

    def strip(n):
        return pl.ds(pl.multiple_of(n * RY, 8), RY)

    def peers():
        for k in range(NI):
            n = wrap(i + k, NI)
            for core in (c, 1 - c) if k else (1 - c,):
                yield 2 * n + core, {"cfg": core, "img": n}

    def readout_1():
        rgb[...] = rgp[...].astype(BF16)
        for n, device in peers():
            away(rgb.at[:, piece(n)], r1.at[me], as_.at[0], ar.at[0], device).start()

    def readout_3():
        drain(r1.at[pl.ds(0, NP - 1)], ar.at[0])
        r1[me] = jnp.zeros((C, W), BF16)
        a1[...] = jnp.sum(r1[...].astype(F32), axis=0) + rgp[:, piece(me)]
        for k in range(1, YN):
            n = wrap(y + k, YN)
            away(a1.at[strip(n)], r2.at[y], as_.at[1], ar.at[1], {"seq": z * YN + n}).start()

    def readout_4():
        drain(r2.at[pl.ds(0, YN - 1)], ar.at[1])
        r2[y] = a1[strip(y), :]
        a2[...] = jnp.sum(r2[...], axis=0)
        for k in range(1, ZN):
            n = wrap(z + k, ZN)
            away(a2, r3.at[z], as_.at[2], ar.at[2], {"seq": n * YN + y}).start()

    def readout_5():
        if ZN > 1:
            drain(r3.at[pl.ds(0, ZN - 1)], ar.at[2])
        r3[z] = a2[...]
        a3[...] = jnp.sum(r3[...], axis=0)
        for k in range(1, YN):
            n = wrap(y + k, YN)
            away(a3, r4.at[y], as_.at[3], ar.at[3], {"seq": z * YN + n}).start()

    def readout_6():
        drain(r4.at[pl.ds(0, YN - 1)], ar.at[3])
        r4[y] = a3[...]
        r4b[...] = r4[...].astype(BF16)
        to = rg.at[:, :, piece(me)]
        pltpu.make_async_copy(r4b, to, ls).start()
        for _, device in peers():
            away(r4b, to, as_.at[4], ar.at[4], device).start()

    def other_key_grads(n, carry):
        send_query_grads(n, key_grads(n))
        return carry

    lax.fori_loop(FIRST, ZN, other_key_grads, 0)

    def image_keys(p):
        base = 2 * p * n3
        a = gk[base : base + n3].reshape(S, third, D)
        b = gk[base + n3 : base + 2 * n3].reshape(S, third, D)
        return jnp.concatenate([a, b], axis=1) * (factor[...] * D ** (-0.5))

    def text_keys(p):
        k = gk[NKI + p * H * TXT : NKI + (p + 1) * H * TXT]
        k = (k * (factor[...] * D ** (-0.5))).reshape(H, TXT, D)
        return jnp.concatenate([k, jnp.zeros_like(k)], axis=1)

    ko[...] = image_keys(1).astype(BF16)
    swaps[1].start()
    kto[...] = text_keys(1).astype(BF16)
    swaps[2].start()
    widen_all()
    readout_1()
    swaps[1].wait_recv()
    kf[...] = (image_keys(0) + xk[...].astype(F32)).astype(BF16)

    def send_key_grads(k, carry):
        zt = at_distance(ZN - 1 - k, 1)
        for yy in range(YN):
            t = zt * YN + yy
            put(kf.at[t], grad.at[1, mine, cols_home], dks, dkr, branch, t)
        return carry

    lax.fori_loop(0, ZN // 4, send_key_grads, 0)
    readout_3()
    readout_4()
    lax.fori_loop(ZN // 4, ZN, send_key_grads, 0)
    swaps[2].wait_recv()
    ktf[...] = (text_keys(0) + xkt[...].astype(F32)).astype(BF16)

    def send_text_keys(k, carry):
        put(ktf.at[k], ktb.at[head], kts, ktr, branch, c * H + k)
        return carry

    lax.fori_loop(0, H, send_text_keys, 0)

    readout_5()
    readout_6()

    def sent(k, carry):
        chip = 2 * k + c
        for odd in range(2):
            src = 2 * k + odd
            drain(kv.at[1, src], fs.at[src])
        drain(text.at[1, k], fts.at[k])
        for j in range(2):
            @pl.when(jnp.logical_not(jnp.logical_and(chip == s, j == c)))
            def _():
                drain(kv.at[0, 0], ks.at[k, j])
                drain(qbuf.at[0], qs.at[k, j])

        @pl.when(jnp.logical_not(jnp.logical_and(chip == s, side == c)))
        def _():
            drain(text.at[0, 0], ts.at[k])

        return carry

    lax.fori_loop(0, H, sent, 0)
    drain(got.at[pl.ds(0, S - 1)], ms)
    drain(g_all.at[pl.ds(0, S - 1)], gs)
    drain(parts.at[pl.ds(0, S - 1)], ps)
    if NI > 1:
        drain(rewards.at[pl.ds(0, NI - 1)], rs)
    for w in swaps:
        w.wait_send()
    drain(r1.at[pl.ds(0, NP - 1)], as_.at[0])
    drain(r2.at[pl.ds(0, YN - 1)], as_.at[1])
    if ZN > 1:
        drain(r3.at[pl.ds(0, ZN - 1)], as_.at[2])
    drain(r4.at[pl.ds(0, YN - 1)], as_.at[3])
    rest = dv.at[pl.ds(0, C), pl.ds(0, (NP - 1) * W)]
    drain(rest, as_.at[4])
    drain(r4b, ls)
    drain(rest, ar.at[4])

    def swapped_u(r, carry):
        swap_u(r).wait_send()
        return carry

    lax.fori_loop(0, NG, swapped_u, 0)
    drain(dv, dvsem)
    text_here = jnp.logical_and(branch == c, s // H == c)

    @pl.when(branch == c)
    def _():
        drain(uf.at[pl.ds(0, S - 1)], us)
        drain(dqb.at[pl.ds(0, S - 1)], dqs)
        drain(kf.at[pl.ds(0, S - 1)], dks)

    @pl.when(branch != c)
    def _():
        drain(uf, us)
        drain(dqb, dqs)
        drain(kf, dks)

    @pl.when(text_here)
    def _():
        drain(utf.at[pl.ds(0, H - 1)], uts)
        drain(ktf.at[pl.ds(0, H - 1)], kts)

    @pl.when(jnp.logical_not(text_here))
    def _():
        drain(utf, uts)
        drain(ktf, kts)

    drain(ktb, ktr)

    def text_home(h, carry):
        at = pl.ds(pl.multiple_of(h * D, D), D)
        dkt[:, at] = ktb[h].astype(F32)[:TXT]
        return carry

    lax.fori_loop(0, H, text_home, 0)
    tgrad[...] = jnp.stack([dkt[...], dvt[...]], axis=1).astype(BF16)
    drain(grad.at[0], dqr)
    drain(grad.at[1], dkr)


def step_call(S, NI, guidance, rate, reward, img, txt, rt, noise, old):
    H, ZN, NP = S // 2, S // YN, 2 * NI
    HD = rt.shape[1]
    W, RY, third = HD // NP, C // YN, HALF // 2
    NK = (2 * HALF + TXT) * S
    dma = pltpu.SemaphoreType.DMA
    tile = (1, D)
    b = lambda *shape: pltpu.VMEM(shape, BF16)
    w = lambda *shape: pltpu.VMEM(shape, F32)
    return pl.pallas_call(
        functools.partial(step_kernel, S, NI),
        out_shape=(
            jax.ShapeDtypeStruct(img.shape, BF16),
            jax.ShapeDtypeStruct((TXT, 2, HD), BF16),
            jax.ShapeDtypeStruct((YN, RY, HD), BF16),
            jax.ShapeDtypeStruct((1, 1), F32),
        ),
        in_specs=[SMEM, SMEM, SMEM, ANY, VMEM, VMEM, VMEM, VMEM],
        out_specs=(ANY, VMEM, ANY, SMEM),
        scratch_shapes=[
            b(2 * TXT, HD),
            b(*img.shape[1:]),
            b(H, 2, third, D),
            b(H, 2 * TXT, D),
            b(2, S, HALF + third, D),
            b(2, H, 2 * TXT, D),
            b(S, HALF, D),
            b(NK, 2 * D),
            b(D, NK),
            b(NK, D),
            b(C + ONES, NK),
            w(NK, QB),
            w(NK, QB),
            b(KB // SB, SB, QB),
            b(TXT * S, QB),
            b(ZN, NK, QB),
            w(ZN, C, QB),
            w(ZN, 1, QB),
            b(S, C // 2, D),
            b(S, C // 2, D),
            b(C // 2, D),
            b(S, C // 2, D),
            w(*tile),
            w(S, *tile),
            w(2, *tile),
            w(NI, *tile),
            w(*tile),
            b(ZN, 2 * C, QB),
            b(ZN, QB, D),
            w(ZN, 1, QB),
            w(NK, D),
            w(*tile),
            w(min(3, ZN), QB, D),
            b(S, third, D),
            b(S, third, D),
            w(S, third, D),
            b(S, third, D),
            b(H, 2 * TXT, D),
            b(H, 2 * TXT, D),
            b(H, 2 * TXT, D),
            b(S, HALF, D),
            b(S, HALF, D),
            b(S, HALF, D),
            b(H, 2 * TXT, D),
            b(H, 2 * TXT, D),
            b(H, 2 * TXT, D),
            b(S, HALF, D),
            b(H, 2, third, D),
            b(H, 2 * TXT, D),
            b(H, 2 * TXT, D),
            b(*img.shape[1:]),
            w(TXT, HD),
            w(TXT, HD),
            w(C, HD),
            b(C, HD),
            b(NP, C, W),
            w(C, W),
            w(YN, RY, W),
            w(RY, W),
            w(ZN, RY, W),
            w(RY, W),
            w(YN, RY, W),
            b(YN, RY, W),
            dma,
            dma((H, 2)), dma((S,)),
            dma((H, 2)), dma((S,)),
            dma((H,)), dma((H,)),
            dma((S,)), dma((S,)),
            dma((H,)), dma((H,)),
            dma, dma,
            dma, dma((S,)),
            dma, dma,
            dma, dma,
            dma, dma,
            dma((3,)), dma((3,)),
            dma((max(1, third * S // UB),)), dma((max(1, third * S // UB),)),
            dma, dma,
            dma, dma,
            dma, dma,
            dma, dma,
            dma, dma,
            dma,
            dma((5,)), dma((5,)),
            dma,
        ],
        compiler_params=pltpu.CompilerParams(
            collective_id=0, has_side_effects=True, vmem_limit_bytes=LIMIT
        ),
        name="step",
    )(guidance, rate, reward, img, txt, rt, noise, old)


def on_device(S, NI, img_qkv, txt_kv, readout, old_velocity, noise, step_ratio, rewards, guidance):
    img = img_qkv[0, 0].transpose(1, 0, 2)
    text = txt_kv[0, 0]
    scalar = lambda x: x.reshape(1, 1)
    grad, tgrad, rg, ratio = step_call(
        S, NI, scalar(guidance), scalar(step_ratio), scalar(rewards), img, text, readout.T, noise[0].T, old_velocity[0].T
    )
    img_grad = grad.transpose(1, 0, 2)[None, None]
    return (img_grad, tgrad[None, None], rg.reshape(C, -1).T.astype(F32), ratio.reshape(1))


def solution(mesh):
    S, NI = mesh.shape["seq"], mesh.shape["img"]
    placed = (
        P("cfg", "img", "seq", None, None),
        P("cfg", "img", "seq", None, None),
        P(),
        P("img", "seq", None),
        P("img", "seq", None),
        P("img"),
        P("img"),
        P(),
    )
    return jax.shard_map(
        functools.partial(on_device, S, NI),
        mesh=mesh,
        in_specs=placed,
        out_specs=(
            P("cfg", "img", "seq", None, None),
            P("cfg", "img", "seq", None, None),
            P(),
            P("img"),
        ),
        check_vma=False,
    )
```

```python
import functools

import jax
import jax.numpy as jnp
from jax import lax
from jax.experimental import pallas as pl
from jax.experimental.pallas import tpu as pltpu
from jax.sharding import PartitionSpec as P

D = 128
C = 64
HALF = 64
TXT = 8
YN = 4
QB = 256
KB = 4096
SB = 256
BB = 2176
UB = 512
ONES = 16
MESH = pl.DeviceIdType.MESH
F32 = jnp.float32
BF16 = jnp.bfloat16
NT = (((1,), (1,)), ((), ()))
TN = (((0,), (0,)), ((), ()))
ANY = pl.BlockSpec(memory_space=pl.ANY)
VMEM = pl.BlockSpec(memory_space=pltpu.VMEM)
SMEM = pl.BlockSpec(memory_space=pltpu.SMEM)
LIMIT = 60 * 1024 * 1024


def iota(shape, dim):
    return lax.broadcasted_iota(jnp.int32, shape, dim)


def put(src, dst, send, recv, core, chip):
    here = jnp.logical_and(core == lax.axis_index("cfg"), chip == lax.axis_index("seq"))

    @pl.when(here)
    def _():
        pltpu.make_async_copy(src, dst, recv).start()

    @pl.when(jnp.logical_not(here))
    def _():
        away(src, dst, send, recv, {"cfg": core, "seq": chip}).start()


def away(src, dst, send, recv, device):
    return pltpu.make_async_remote_copy(
        src_ref=src,
        dst_ref=dst,
        send_sem=send,
        recv_sem=recv,
        device_id=device,
        device_id_type=MESH,
    )


def drain(ref, sem):
    pltpu.make_async_copy(ref, ref, sem).wait()


def wrap(at, size):
    return jnp.where(at >= size, at - size, at)


def signal_plane(chips):
    c, s = lax.axis_index("cfg"), lax.axis_index("seq")
    barrier = pltpu.get_barrier_semaphore()

    def tell(device):
        pl.semaphore_signal(barrier, inc=1, device_id=device, device_id_type=MESH)

    def one(k, carry):
        chip = wrap(s + k, chips)
        tell({"cfg": c, "seq": chip})
        tell({"cfg": 1 - c, "seq": chip})
        return carry

    lax.fori_loop(1, chips, one, 0)
    tell({"cfg": 1 - c})
    return barrier


def pack_pair(x):
    top, low = x[: C // 2], x[C // 2 :]
    lower = iota(top.shape, 1) < HALF
    return (
        jnp.where(lower, top, pltpu.roll(low, HALF, 1)),
        jnp.where(lower, pltpu.roll(top, HALF, 1), low),
    )


def unpack_pair(a, b):
    lower = iota(a.shape, 1) < HALF
    return jnp.concatenate(
        [jnp.where(lower, a, pltpu.roll(b, HALF, 1)), jnp.where(lower, pltpu.roll(a, HALF, 1), b)], axis=0
    )


def own_tokens(x):
    a, b = pack_pair(x)
    return jnp.where(lax.axis_index("cfg") == 0, a, b)


def step_kernel(
    S, NI, guidance, rate, reward, img, txt, rt, noise, old,
    grad, tgrad, rg, ratio,
    tx, vbuf, vrp, txb, kv, text, qbuf, keys, keys_t, narrow, narrow_t, scores_a, scores_b, hold, hold_text, weights, out_t, linv,
    msg, got, g_own, g_all, part, parts, pair, rewards, reward_own, gl, gl_cols, delta, gk, factor, held,
    uo, xu, uown, uf, uto, xut, utf, ko, xk, kf, kto, xkt, ktf, dqb, ub, utb, ktb, dv, dkt, dvt, rgp, rgb, r1, a2, r3, a3,
    vsem, ks, kr, qs, qr, ts, tr, fs, fr, fts, ftr, ms, mr, gs, gr, ps, pr, pairs, pairr, rs, rr,
    xs, xr, xus, xur, us, ur, uts, utr, dqs, dqr, dks, dkr, kts, ktr, dvsem, as_, ar, ls,
):
    H = S // 2
    ZN = S // YN
    NP = 2 * NI
    W = rgp.shape[1] // NP
    RY = C // YN
    NK = keys.shape[0]
    NKI = 2 * HALF * S
    KT = min(KB, NKI)
    subs = KT // SB
    third = HALF // 2
    n3 = third * S
    c, i, s = lax.axis_index("cfg"), lax.axis_index("img"), lax.axis_index("seq")
    head, branch = s // 2, lax.rem(s, 2)
    y, z = lax.rem(s, YN), s // YN
    other = {"cfg": 1 - c}

    vcopy = pltpu.make_async_copy(img.at[2], vbuf, vsem)
    vcopy.start()
    barrier = signal_plane(S)
    for k in range(1, NI):
        for core in range(2):
            for yy in range(YN):
                pl.semaphore_signal(
                    barrier,
                    inc=1,
                    device_id={"cfg": core, "img": wrap(i + k, NI), "seq": z * YN + yy},
                    device_id_type=MESH,
                )
    words = txt[...].astype(F32)
    tx[...] = jnp.concatenate([words[:, 0], words[:, 1]], axis=0).astype(BF16)
    vcopy.wait()
    reward_own[...] = jnp.full(reward_own.shape, reward[0, 0], F32)

    def squeeze(h):
        cols = pl.ds(pl.multiple_of(h * D, D), D)
        r = rt[:, cols]
        twice = jnp.concatenate([r, r], axis=0)
        x = lax.dot_general(vbuf[:, cols], twice, NT, preferred_element_type=F32)
        low = iota((third, D), 1) < C
        for j in range(2):
            first = x[HALF * j : HALF * j + third]
            second = x[HALF * j + third : HALF * j + HALF]
            vrp[h, j] = jnp.where(low, first, second).astype(BF16)
        t = tx[:, cols]
        yv = lax.dot_general(t, twice, NT, preferred_element_type=F32)
        yv = jnp.where(iota(yv.shape, 1) < C, yv, 0.0)
        txb[h] = jnp.where(iota(yv.shape, 0) < TXT, t.astype(F32), yv).astype(BF16)

    def some(count, body):
        at_once = 4 if count % 4 == 0 else 1

        def trip(k, carry):
            for j in range(at_once):
                body(k * at_once + j)
            return carry

        lax.fori_loop(0, count // at_once, trip, 0)

    some(H, squeeze)
    pl.semaphore_wait(barrier, 2 * S - 1 + 2 * (NI - 1) * YN)

    side = s // H

    def at_distance(n, sign):
        half = (n + 1) // 2
        far = jnp.where(n == 2 * half, ZN - half, half)
        return wrap(z + far, ZN) if sign > 0 else wrap(z + ZN - far, ZN)

    def in_turn(n, sign):
        if ZN < 4:
            return at_distance(n, sign)
        return at_distance(jnp.where(n == 0, 0, jnp.where(n <= ZN - 3, n + 2, n - (ZN - 3))), sign)

    def send_keys(k, carry):
        zt = at_distance(ZN - 1 - k // 2, 1)
        h = 2 * zt + lax.rem(k, 2)
        chip = 2 * h + c
        cols = pl.ds(pl.multiple_of(h * D, D), D)
        for j in range(2):
            put(img.at[1, pl.ds(HALF * j, HALF), cols], kv.at[0, s, pl.ds(0, HALF)], ks.at[h, j], kr.at[s], j, chip)
            put(vrp.at[h, j], kv.at[0, s, pl.ds(HALF, third)], ks.at[h, j], kr.at[s], j, chip)
        put(txb.at[h], text.at[0, lax.rem(s, H)], ts.at[h], tr.at[lax.rem(s, H)], side, chip)
        return carry

    lax.fori_loop(0, H, send_keys, 0)

    def send_queries(k, carry):
        zt = in_turn(k // 2, 1)
        h = 2 * zt + lax.rem(k, 2)
        chip = 2 * h + c
        cols = pl.ds(pl.multiple_of(h * D, D), D)
        for j in range(2):
            put(img.at[0, pl.ds(HALF * j, HALF), cols], qbuf.at[s], qs.at[h, j], qr.at[s], j, chip)
        return carry

    lax.fori_loop(0, H, send_queries, 0)
    for k in range(1, NI):
        away(reward_own, rewards.at[i], rs, rr, {"img": wrap(i + k, NI)}).start()

    narrow_t[C:] = jnp.where(iota((ONES, NK), 0) == 0, 1.0, 0.0).astype(BF16)

    def lay_out(p, zs):
        four = pl.ds(zs * YN, YN)
        packed = kv[p, four, HALF:, :].reshape(third * YN, D)
        turned = packed.astype(F32).T
        for ab in range(2):
            rows = pl.ds(pl.multiple_of((2 * p + ab) * n3 + zs * (third * YN), third * YN), third * YN)
            block = kv[p, four, third * ab : third * ab + third, :].reshape(third * YN, D)
            keys[rows, :D] = block
            keys[rows, D:] = block
            keys_t[:, rows] = block.astype(F32).T.astype(BF16)
            one = turned[C * ab : C * ab + C]
            narrow_t[:C, rows] = one.astype(BF16)
            narrow[rows] = jnp.concatenate([one, one], axis=0).T.astype(BF16)

    def arrive(n, carry):
        zs = at_distance(ZN - 1 - n, -1)
        for yy in range(YN):
            src = zs * YN + yy
            drain(kv.at[0, src], kr.at[src])
            away(kv.at[0, src], kv.at[1, src], fs.at[src], fr.at[src], other).start()
        lay_out(0, zs)
        return carry

    lax.fori_loop(0, ZN, arrive, 0)

    def arrive_text(k, carry):
        drain(text.at[0, k], tr.at[k])
        away(text.at[0, k], text.at[1, k], fts.at[k], ftr.at[k], other).start()
        return carry

    lax.fori_loop(0, H, arrive_text, 0)

    def arrive_other(n, carry):
        zs = at_distance(ZN - 1 - n, -1)
        for yy in range(YN):
            drain(kv.at[1, zs * YN + yy], fr.at[zs * YN + yy])
        lay_out(1, zs)
        return carry

    lax.fori_loop(0, ZN, arrive_other, 0)

    def arrive_other_text(k, carry):
        drain(text.at[1, k], ftr.at[k])
        return carry

    lax.fori_loop(0, H, arrive_other_text, 0)
    words = text[...].astype(F32)
    tk = words[:, :, :TXT, :].reshape(TXT * S, D)
    tv = words[:, :, TXT:, :].reshape(TXT * S, D)
    last = pl.ds(NKI, TXT * S)
    keys[last, :D] = tk.astype(BF16)
    keys[last, D:] = tk.astype(BF16)
    keys_t[:, last] = tk.T.astype(BF16)
    tvt = tv.T[:C]
    narrow_t[:C, last] = tvt.astype(BF16)
    narrow[last] = jnp.concatenate([tvt, tvt], axis=0).T.astype(BF16)

    def over_keys(body, carry):
        for at in range(0, NK, BB):
            carry = body(slice(at, min(at + BB, NK)), carry)
        return carry

    def queries_t(zs):
        for yy in range(YN):
            drain(qbuf.at[zs * YN + yy], qr.at[zs * YN + yy])
        x = qbuf[pl.ds(zs * YN, YN)].reshape(QB, D).astype(F32).T * (D ** (-0.5) * 1.4426950408889634)
        hi = x.astype(BF16)
        return jnp.concatenate([hi, (x - hi.astype(F32)).astype(BF16)], axis=0)

    def score(buf, rows, q_t, top):
        st = jnp.dot(keys[rows], q_t, preferred_element_type=F32)
        buf[rows] = st
        return jnp.maximum(top, jnp.max(st.reshape(st.shape[0] // 8, 8, QB), axis=0))

    def weigh(buf, zs, rows, top, hold):
        e = jnp.exp2(buf[rows] - top).astype(BF16)
        weights[zs, rows] = e
        hold[...] = e

    def mix(rows, hold, mixed):
        return mixed + jnp.dot(narrow_t[:, rows], hold[...], preferred_element_type=F32)

    low_top = jnp.full((8, QB), -jnp.inf, F32)
    no_mix = jnp.zeros((C + ONES, QB), F32)
    branch_share = jnp.where(branch == 0, guidance[0, 0], 1.0 - guidance[0, 0])
    parts_of = NKI // KT

    def chunk(k, sub):
        return pl.ds(pl.multiple_of(k * KT + sub * SB, SB), SB)

    def first_scores(q_t):
        def body(k, t):
            for sub in range(subs):
                t = score(scores_a, chunk(k, sub), q_t, t)
            return t

        return score(scores_a, last, q_t, lax.fori_loop(0, parts_of, body, low_top))

    def attend(n, now, then, top8, ahead):
        zs = in_turn(n, -1)
        top = jnp.max(top8, axis=0, keepdims=True)
        q_t = queries_t(in_turn(n + 1, -1)) if ahead else None
        next8 = score(then, last, q_t, low_top) if ahead else low_top
        weigh(now, zs, last, top, hold_text)
        mixed = mix(last, hold_text, no_mix)
        hold[subs - 1] = jnp.zeros((SB, QB), BF16)

        def body(k, carry):
            next8, mixed = carry
            for sub in range(subs):
                before = chunk(jnp.maximum(k - 1, 0), subs - 1) if sub == 0 else chunk(k, sub - 1)
                mixed = mix(before, hold.at[(sub - 1) % subs], mixed)
                if ahead:
                    next8 = score(then, chunk(k, sub), q_t, next8)
                weigh(now, zs, chunk(k, sub), top, hold.at[sub])
            return next8, mixed

        next8, mixed = lax.fori_loop(0, parts_of, body, (next8, mixed))
        mixed = mix(chunk(parts_of - 1, subs - 1), hold.at[subs - 1], mixed)
        inverse = 1.0 / mixed[C : C + 1]
        linv[zs] = inverse
        normal = mixed[:C] * inverse
        out_t[zs] = normal
        for m in range(QB // D):
            a, b = pack_pair(normal[:, D * m : D * m + D] * branch_share)
            for yy, part_of in ((2 * m, a), (2 * m + 1, b)):
                msg[zs * YN + yy] = part_of.astype(BF16)
        for yy in range(YN):
            t = zs * YN + yy
            put(msg.at[t], got.at[s], ms, mr, c, t)
        return next8

    top = first_scores(queries_t(in_turn(0, -1)))

    def two(m, top):
        top = attend(2 * m, scores_a, scores_b, top, True)
        return attend(2 * m + 1, scores_b, scores_a, top, True)

    top = lax.fori_loop(0, ZN // 2 - 1, two, top)
    if ZN > 1:
        top = attend(ZN - 2, scores_a, scores_b, top, True)
        attend(ZN - 1, scores_b, scores_a, top, False)
    else:
        attend(0, scores_a, scores_b, top, False)

    noise_own = own_tokens(noise[...])
    old_own = own_tokens(old[...])
    drain(got, mr)
    guided = jnp.sum(got[...].astype(F32), axis=0)
    step = rate[0, 0]
    deviation = step * (guided - old_own)
    g_own[...] = (noise_own - deviation).astype(BF16)

    def share(k, carry):
        zt = at_distance(k, 1)
        for yy in range(YN):
            put(g_own, g_all.at[s], gs, gr.at[s], c, zt * YN + yy)
        return carry

    lax.fori_loop(0, ZN, share, 0)
    partial = jnp.sum(noise_own * deviation - 0.5 * deviation * deviation)
    part[...] = jnp.full(part.shape, partial, F32)

    def tell(k, carry):
        put(part, parts.at[s], ps, pr, c, k)
        return carry

    lax.fori_loop(0, S, tell, 0)
    gk[...] = jnp.zeros_like(gk)

    cols_home = pl.ds(pl.multiple_of(head * D, D), D)
    mine = pl.ds(pl.multiple_of(HALF * c, HALF), HALF)
    FIRST = min(3, ZN)

    def divide(n):
        zs = at_distance(n, -1)
        for yy in range(YN):
            drain(g_all.at[zs * YN + yy], gr.at[zs * YN + yy])
        g_t = jnp.concatenate(
            [
                unpack_pair(g_all[zs * YN + 2 * m].astype(F32), g_all[zs * YN + 2 * m + 1].astype(F32))
                for m in range(QB // D)
            ],
            axis=1,
        )
        g_t = g_t * linv[zs]
        hi = g_t.astype(BF16)
        lo = (g_t - hi.astype(F32)).astype(BF16)
        hi32 = hi.astype(F32)
        gl[zs] = jnp.concatenate([hi, lo], axis=0)
        delta[zs] = jnp.sum((hi32 + lo.astype(F32)) * out_t[zs], axis=0, keepdims=True)
        gl_cols[zs] = jnp.concatenate([hi32, hi32], axis=0).T.astype(BF16)

    def key_grads(n):
        zs = at_distance(n, -1)
        block = qbuf[pl.ds(zs * YN, YN)].reshape(QB, D)
        g_t = gl[zs]
        shift = delta[zs]

        def one(rows, dq_t):
            gp = jnp.dot(narrow[rows], g_t, preferred_element_type=F32)
            ds = (weights[zs, rows].astype(F32) * (gp - shift)).astype(BF16)
            gk[rows] += jnp.dot(ds, block, preferred_element_type=F32)
            return dq_t + jnp.dot(keys_t[:, rows], ds, preferred_element_type=F32)

        return over_keys(one, jnp.zeros((D, QB), F32)).T

    def send_query_grads(n, rows):
        zs = at_distance(n, -1)
        dqb[pl.ds(zs * YN, YN)] = (rows * (factor[...] * D ** (-0.5))).astype(BF16).reshape(YN, HALF, D)
        for yy in range(YN):
            t = zs * YN + yy
            put(dqb.at[t], grad.at[0, mine, cols_home], dqs, dqr, branch, t)

    def first_blocks(n, carry):
        divide(n)
        held[n] = key_grads(n)
        return carry

    lax.fori_loop(0, FIRST, first_blocks, 0)

    def other_blocks(n, carry):
        divide(n)
        return carry

    lax.fori_loop(FIRST, ZN, other_blocks, 0)

    drain(parts, pr)
    pair[0] = jnp.sum(parts[...], axis=0)
    swap = away(pair.at[0], pair.at[1], pairs, pairr, other)
    swap.start()

    def settle():
        if NI > 1:
            drain(rewards.at[pl.ds(0, NI - 1)], rr)
        own_reward = reward_own[...]
        rewards[i] = own_reward
        mean = jnp.sum(rewards[...], axis=0) / NI
        square = jnp.sum(rewards[...] * rewards[...], axis=0) / NI
        deviates = jnp.sqrt(jnp.maximum(square - mean * mean, 0.0))
        advantage = (own_reward - mean) / jnp.maximum(deviates, 1.0)
        swap.wait()
        ratio_now = jnp.exp((pair[0] + pair[1]) / (2 * S * HALF * C))
        clipped = jnp.clip(ratio_now, 0.8, 1.2)
        keep = ratio_now * advantage <= clipped * advantage
        gain = jnp.where(keep, -ratio_now * advantage, 0.0)
        ratio[0, 0] = jnp.max(ratio_now)
        factor[...] = gain * (step * branch_share)

    NG = max(1, n3 // UB)
    GS = S // NG
    GR = third * GS

    def narrow_grad(rows):
        total = jnp.dot(weights[0, rows], gl_cols[0], preferred_element_type=F32)
        for zs in range(1, ZN):
            total = total + jnp.dot(weights[zs, rows], gl_cols[zs], preferred_element_type=F32)
        return total

    def paired(p, r):
        a, b = (
            narrow_grad(pl.ds(pl.multiple_of((2 * p + ab) * n3 + r * GR, GR), GR)) for ab in range(2)
        )
        return jnp.where(iota(a.shape, 1) < C, a, b).reshape(GS, third, D)

    def swap_u(r):
        srcs = pl.ds(r * GS, GS)
        return away(uo.at[srcs], xu.at[srcs], xus.at[r], xur.at[r], other)

    def send_u(r):
        swap_u(r).wait_recv()
        srcs = pl.ds(r * GS, GS)
        uf[srcs] = ((uown[srcs] + xu[srcs].astype(F32)) * factor[...]).astype(BF16)

        def one(k, carry):
            t = r * GS + k
            put(uf.at[t], ub.at[head, c], us, ur, branch, t)
            return carry

        lax.fori_loop(0, GS, one, 0)

    def group(k):
        return wrap(z * NG // ZN + k, NG)

    swaps = [
        away(uto, xut, xs.at[0], xr.at[0], other),
        away(ko, xk, xs.at[1], xr.at[1], other),
        away(kto, xkt, xs.at[2], xr.at[2], other),
    ]
    both_texts = narrow_grad(last)
    both_texts = jnp.where(iota(both_texts.shape, 1) < C, both_texts, 0.0).reshape(2, H, TXT, D)
    no_keys = jnp.zeros((H, TXT, D), F32)
    uto[...] = jnp.concatenate([no_keys, both_texts[1]], axis=1).astype(BF16)
    swaps[0].start()

    def narrow_group(k, carry):
        r = group(k)
        srcs = pl.ds(r * GS, GS)
        uo[srcs] = paired(1, r).astype(BF16)
        swap_u(r).start()
        pl.when(k == min(1, NG - 1))(settle)

        @pl.when(k > 0)
        def _():
            send_u(group(k - 1))

        uown[srcs] = paired(0, r)

        return carry

    lax.fori_loop(0, NG, narrow_group, 0)
    swaps[0].wait_recv()
    utf[...] = (
        (jnp.concatenate([no_keys, both_texts[0]], axis=1) + xut[...].astype(F32)) * factor[...]
    ).astype(BF16)

    def send_text(k, carry):
        put(utf.at[k], utb.at[head], uts, utr, branch, c * H + k)
        return carry

    lax.fori_loop(0, H, send_text, 0)
    send_u(group(NG - 1))

    def send_held(n, carry):
        send_query_grads(n, held[n])
        return carry

    lax.fori_loop(0, FIRST, send_held, 0)

    def widen_all():
        drain(ub, ur)
        drain(utb, utr)

        def widen(h):
            at = pl.ds(pl.multiple_of(h * D, D), D)
            r = rt[:, at]
            twice = jnp.concatenate([r, r], axis=0)
            low = iota((third, D), 1) < C
            u0, u1 = ub[h, 0].astype(F32), ub[h, 1].astype(F32)
            spaced = jnp.concatenate(
                [
                    jnp.where(low, u0, 0.0),
                    jnp.where(low, 0.0, u0),
                    jnp.where(low, u1, 0.0),
                    jnp.where(low, 0.0, u1),
                    utb[h].astype(F32),
                ],
                axis=0,
            )
            wide = jnp.dot(spaced.astype(BF16), twice, preferred_element_type=F32)
            dv[:, at] = wide[: 2 * HALF].astype(BF16)
            dvt[:, at] = wide[2 * HALF + TXT :]
            values = jnp.concatenate([vbuf[:, at], tx[:, at]], axis=0)
            res = jnp.dot(spaced.T.astype(BF16), values, preferred_element_type=F32)
            rgp[:, at] = res[:C] + res[C:]

        some(H, widen)
        pltpu.make_async_copy(dv, grad.at[2], dvsem).start()

    me = 2 * i + c

    def piece(n):
        return pl.ds(pl.multiple_of(n * W, D), W)

    def strip(n):
        return pl.ds(pl.multiple_of(n * RY, RY), RY)

    def peers():
        for k in range(YN):
            yy = wrap(y + k, YN)
            for kk in range(NI):
                n = wrap(i + kk, NI)
                for core in (c, 1 - c) if k + kk else (1 - c,):
                    yield 2 * n + core, yy, {"cfg": core, "img": n, "seq": z * YN + yy}

    def readout_1():
        rgb[...] = rgp[...].astype(BF16)
        for n, yy, device in peers():
            away(rgb.at[strip(yy), piece(n)], r1.at[y * NP + me], as_.at[0], ar.at[0], device).start()

    def readout_2():
        drain(r1.at[pl.ds(0, NP * YN - 1)], ar.at[0])
        r1[y * NP + me] = rgb[strip(y), piece(me)]
        a2[...] = jnp.sum(r1[...].astype(F32), axis=0).astype(BF16)
        for k in range(1, ZN):
            n = wrap(z + k, ZN)
            away(a2, r3.at[z], as_.at[1], ar.at[1], {"seq": n * YN + y}).start()

    def readout_3():
        if ZN > 1:
            drain(r3.at[pl.ds(0, ZN - 1)], ar.at[1])
        r3[z] = a2[...]
        a3[...] = jnp.sum(r3[...].astype(F32), axis=0).astype(BF16)
        to = rg.at[y, :, piece(me)]
        pltpu.make_async_copy(a3, to, ls).start()
        for _, _, device in peers():
            away(a3, to, as_.at[2], ar.at[2], device).start()

    def other_key_grads(n, carry):
        send_query_grads(n, key_grads(n))
        return carry

    lax.fori_loop(FIRST, ZN, other_key_grads, 0)

    def image_keys(p):
        base = 2 * p * n3
        a = gk[base : base + n3].reshape(S, third, D)
        b = gk[base + n3 : base + 2 * n3].reshape(S, third, D)
        return jnp.concatenate([a, b], axis=1) * (factor[...] * D ** (-0.5))

    def text_keys(p):
        k = gk[NKI + p * H * TXT : NKI + (p + 1) * H * TXT]
        k = (k * (factor[...] * D ** (-0.5))).reshape(H, TXT, D)
        return jnp.concatenate([k, jnp.zeros_like(k)], axis=1)

    ko[...] = image_keys(1).astype(BF16)
    swaps[1].start()
    kto[...] = text_keys(1).astype(BF16)
    swaps[2].start()
    widen_all()
    readout_1()
    swaps[1].wait_recv()
    kf[...] = (image_keys(0) + xk[...].astype(F32)).astype(BF16)

    def send_key_grads(k, carry):
        zt = at_distance(ZN - 1 - k, 1)
        for yy in range(YN):
            t = zt * YN + yy
            put(kf.at[t], grad.at[1, mine, cols_home], dks, dkr, branch, t)
        return carry

    lax.fori_loop(0, ZN // 8, send_key_grads, 0)
    readout_2()
    lax.fori_loop(ZN // 8, ZN, send_key_grads, 0)
    swaps[2].wait_recv()
    ktf[...] = (text_keys(0) + xkt[...].astype(F32)).astype(BF16)

    def send_text_keys(k, carry):
        put(ktf.at[k], ktb.at[head], kts, ktr, branch, c * H + k)
        return carry

    lax.fori_loop(0, H, send_text_keys, 0)

    readout_3()

    def sent(k, carry):
        chip = 2 * k + c
        for odd in range(2):
            src = 2 * k + odd
            drain(kv.at[1, src], fs.at[src])
        drain(text.at[1, k], fts.at[k])
        for j in range(2):
            @pl.when(jnp.logical_not(jnp.logical_and(chip == s, j == c)))
            def _():
                drain(kv.at[0, 0], ks.at[k, j])
                drain(qbuf.at[0], qs.at[k, j])

        @pl.when(jnp.logical_not(jnp.logical_and(chip == s, side == c)))
        def _():
            drain(text.at[0, 0], ts.at[k])

        return carry

    lax.fori_loop(0, H, sent, 0)
    drain(got.at[pl.ds(0, S - 1)], ms)
    drain(g_all.at[pl.ds(0, S - 1)], gs)
    drain(parts.at[pl.ds(0, S - 1)], ps)
    if NI > 1:
        drain(rewards.at[pl.ds(0, NI - 1)], rs)
    for w in swaps:
        w.wait_send()
    rest = r1.at[pl.ds(0, NP * YN - 1)]
    drain(rest, as_.at[0])
    if ZN > 1:
        drain(r3.at[pl.ds(0, ZN - 1)], as_.at[1])
    drain(rest, as_.at[2])
    drain(a3, ls)
    drain(rest, ar.at[2])

    def swapped_u(r, carry):
        swap_u(r).wait_send()
        return carry

    lax.fori_loop(0, NG, swapped_u, 0)
    drain(dv, dvsem)
    text_here = jnp.logical_and(branch == c, s // H == c)

    @pl.when(branch == c)
    def _():
        drain(uf.at[pl.ds(0, S - 1)], us)
        drain(dqb.at[pl.ds(0, S - 1)], dqs)
        drain(kf.at[pl.ds(0, S - 1)], dks)

    @pl.when(branch != c)
    def _():
        drain(uf, us)
        drain(dqb, dqs)
        drain(kf, dks)

    @pl.when(text_here)
    def _():
        drain(utf.at[pl.ds(0, H - 1)], uts)
        drain(ktf.at[pl.ds(0, H - 1)], kts)

    @pl.when(jnp.logical_not(text_here))
    def _():
        drain(utf, uts)
        drain(ktf, kts)

    drain(ktb, ktr)

    def text_home(h, carry):
        at = pl.ds(pl.multiple_of(h * D, D), D)
        dkt[:, at] = ktb[h].astype(F32)[:TXT]
        return carry

    lax.fori_loop(0, H, text_home, 0)
    tgrad[...] = jnp.stack([dkt[...], dvt[...]], axis=1).astype(BF16)
    drain(grad.at[0], dqr)
    drain(grad.at[1], dkr)


def step_call(S, NI, guidance, rate, reward, img, txt, rt, noise, old):
    H, ZN, NP = S // 2, S // YN, 2 * NI
    HD = rt.shape[1]
    W, RY, third = HD // NP, C // YN, HALF // 2
    NK = (2 * HALF + TXT) * S
    dma = pltpu.SemaphoreType.DMA
    tile = (1, D)
    b = lambda *shape: pltpu.VMEM(shape, BF16)
    w = lambda *shape: pltpu.VMEM(shape, F32)
    return pl.pallas_call(
        functools.partial(step_kernel, S, NI),
        out_shape=(
            jax.ShapeDtypeStruct(img.shape, BF16),
            jax.ShapeDtypeStruct((TXT, 2, HD), BF16),
            jax.ShapeDtypeStruct((YN, RY, HD), BF16),
            jax.ShapeDtypeStruct((1, 1), F32),
        ),
        in_specs=[SMEM, SMEM, SMEM, ANY, VMEM, VMEM, VMEM, VMEM],
        out_specs=(ANY, VMEM, ANY, SMEM),
        scratch_shapes=[
            b(2 * TXT, HD),
            b(*img.shape[1:]),
            b(H, 2, third, D),
            b(H, 2 * TXT, D),
            b(2, S, HALF + third, D),
            b(2, H, 2 * TXT, D),
            b(S, HALF, D),
            b(NK, 2 * D),
            b(D, NK),
            b(NK, D),
            b(C + ONES, NK),
            w(NK, QB),
            w(NK, QB),
            b(KB // SB, SB, QB),
            b(TXT * S, QB),
            b(ZN, NK, QB),
            w(ZN, C, QB),
            w(ZN, 1, QB),
            b(S, C // 2, D),
            b(S, C // 2, D),
            b(C // 2, D),
            b(S, C // 2, D),
            w(*tile),
            w(S, *tile),
            w(2, *tile),
            w(NI, *tile),
            w(*tile),
            b(ZN, 2 * C, QB),
            b(ZN, QB, D),
            w(ZN, 1, QB),
            w(NK, D),
            w(*tile),
            w(min(3, ZN), QB, D),
            b(S, third, D),
            b(S, third, D),
            w(S, third, D),
            b(S, third, D),
            b(H, 2 * TXT, D),
            b(H, 2 * TXT, D),
            b(H, 2 * TXT, D),
            b(S, HALF, D),
            b(S, HALF, D),
            b(S, HALF, D),
            b(H, 2 * TXT, D),
            b(H, 2 * TXT, D),
            b(H, 2 * TXT, D),
            b(S, HALF, D),
            b(H, 2, third, D),
            b(H, 2 * TXT, D),
            b(H, 2 * TXT, D),
            b(*img.shape[1:]),
            w(TXT, HD),
            w(TXT, HD),
            w(C, HD),
            b(C, HD),
            b(NP * YN, RY, W),
            b(RY, W),
            b(ZN, RY, W),
            b(RY, W),
            dma,
            dma((H, 2)), dma((S,)),
            dma((H, 2)), dma((S,)),
            dma((H,)), dma((H,)),
            dma((S,)), dma((S,)),
            dma((H,)), dma((H,)),
            dma, dma,
            dma, dma((S,)),
            dma, dma,
            dma, dma,
            dma, dma,
            dma((3,)), dma((3,)),
            dma((max(1, third * S // UB),)), dma((max(1, third * S // UB),)),
            dma, dma,
            dma, dma,
            dma, dma,
            dma, dma,
            dma, dma,
            dma,
            dma((3,)), dma((3,)),
            dma,
        ],
        compiler_params=pltpu.CompilerParams(
            collective_id=0, has_side_effects=True, vmem_limit_bytes=LIMIT
        ),
        name="step",
    )(guidance, rate, reward, img, txt, rt, noise, old)


def on_device(S, NI, img_qkv, txt_kv, readout, old_velocity, noise, step_ratio, rewards, guidance):
    img = img_qkv[0, 0].transpose(1, 0, 2)
    text = txt_kv[0, 0]
    scalar = lambda x: x.reshape(1, 1)
    grad, tgrad, rg, ratio = step_call(
        S, NI, scalar(guidance), scalar(step_ratio), scalar(rewards), img, text, readout.T, noise[0].T, old_velocity[0].T
    )
    img_grad = grad.transpose(1, 0, 2)[None, None]
    return (img_grad, tgrad[None, None], rg.reshape(C, -1).T.astype(F32), ratio.reshape(1))


def solution(mesh):
    S, NI = mesh.shape["seq"], mesh.shape["img"]
    placed = (
        P("cfg", "img", "seq", None, None),
        P("cfg", "img", "seq", None, None),
        P(),
        P("img", "seq", None),
        P("img", "seq", None),
        P("img"),
        P("img"),
        P(),
    )
    return jax.shard_map(
        functools.partial(on_device, S, NI),
        mesh=mesh,
        in_specs=placed,
        out_specs=(
            P("cfg", "img", "seq", None, None),
            P("cfg", "img", "seq", None, None),
            P(),
            P("img"),
        ),
        check_vma=False,
    )
```

```python
import functools

import jax
import jax.numpy as jnp
from jax import lax
from jax.experimental import pallas as pl
from jax.experimental.pallas import tpu as pltpu
from jax.sharding import PartitionSpec as P

D = 128
C = 64
HALF = 64
TXT = 8
YN = 4
QB = 256
KB = 4096
SB = 256
BB = 2176
UB = 512
ONES = 16
MESH = pl.DeviceIdType.MESH
F32 = jnp.float32
BF16 = jnp.bfloat16
NT = (((1,), (1,)), ((), ()))
TN = (((0,), (0,)), ((), ()))
ANY = pl.BlockSpec(memory_space=pl.ANY)
VMEM = pl.BlockSpec(memory_space=pltpu.VMEM)
SMEM = pl.BlockSpec(memory_space=pltpu.SMEM)
LIMIT = 60 * 1024 * 1024


def iota(shape, dim):
    return lax.broadcasted_iota(jnp.int32, shape, dim)


def put(src, dst, send, recv, core, chip):
    here = jnp.logical_and(core == lax.axis_index("cfg"), chip == lax.axis_index("seq"))

    @pl.when(here)
    def _():
        pltpu.make_async_copy(src, dst, recv).start()

    @pl.when(jnp.logical_not(here))
    def _():
        away(src, dst, send, recv, {"cfg": core, "seq": chip}).start()


def away(src, dst, send, recv, device):
    return pltpu.make_async_remote_copy(
        src_ref=src,
        dst_ref=dst,
        send_sem=send,
        recv_sem=recv,
        device_id=device,
        device_id_type=MESH,
    )


def drain(ref, sem):
    pltpu.make_async_copy(ref, ref, sem).wait()


def wrap(at, size):
    return jnp.where(at >= size, at - size, at)


def signal_plane(chips):
    c, s = lax.axis_index("cfg"), lax.axis_index("seq")
    barrier = pltpu.get_barrier_semaphore()

    def tell(device):
        pl.semaphore_signal(barrier, inc=1, device_id=device, device_id_type=MESH)

    def one(k, carry):
        chip = wrap(s + k, chips)
        tell({"cfg": c, "seq": chip})
        tell({"cfg": 1 - c, "seq": chip})
        return carry

    lax.fori_loop(1, chips, one, 0)
    tell({"cfg": 1 - c})
    return barrier


def pack_pair(x):
    top, low = x[: C // 2], x[C // 2 :]
    lower = iota(top.shape, 1) < HALF
    return (
        jnp.where(lower, top, pltpu.roll(low, HALF, 1)),
        jnp.where(lower, pltpu.roll(top, HALF, 1), low),
    )


def unpack_pair(a, b):
    lower = iota(a.shape, 1) < HALF
    return jnp.concatenate(
        [jnp.where(lower, a, pltpu.roll(b, HALF, 1)), jnp.where(lower, pltpu.roll(a, HALF, 1), b)], axis=0
    )


def own_tokens(x):
    a, b = pack_pair(x)
    return jnp.where(lax.axis_index("cfg") == 0, a, b)


def step_kernel(
    S, NI, guidance, rate, reward, img, txt, rt, noise, old,
    grad, tgrad, rg, ratio,
    tx, vbuf, vrp, txb, kv, text, qbuf, keys, keys_t, narrow, narrow_t, scores_a, scores_b, hold, hold_text, weights, out_t, linv,
    msg, got, g_own, g_all, part, parts, pair, rewards, reward_own, gl, gl_cols, delta, gk, factor, held,
    uo, xu, uown, uf, uto, xut, utf, ko, xk, kf, kto, xkt, ktf, dqb, ub, utb, ktb, dv, dkt, dvt, rgp, rgb, r1, a2, r3, a3,
    vsem, ks, kr, qs, qr, ts, tr, fs, fr, fts, ftr, ms, mr, gs, gr, ps, pr, pairs, pairr, rs, rr,
    xs, xr, xus, xur, us, ur, uts, utr, dqs, dqr, dks, dkr, kts, ktr, dvsem, as_, ar, ls,
):
    H = S // 2
    ZN = S // YN
    NP = 2 * NI
    W = rgp.shape[1] // NP
    RY = C // YN
    NK = keys.shape[0]
    NKI = 2 * HALF * S
    KT = min(KB, NKI)
    subs = KT // SB
    third = HALF // 2
    n3 = third * S
    c, i, s = lax.axis_index("cfg"), lax.axis_index("img"), lax.axis_index("seq")
    head, branch = s // 2, lax.rem(s, 2)
    y, z = lax.rem(s, YN), s // YN
    other = {"cfg": 1 - c}

    vcopy = pltpu.make_async_copy(img.at[2], vbuf, vsem)
    vcopy.start()
    barrier = signal_plane(S)
    for k in range(1, NI):
        for core in range(2):
            for yy in range(YN):
                pl.semaphore_signal(
                    barrier,
                    inc=1,
                    device_id={"cfg": core, "img": wrap(i + k, NI), "seq": z * YN + yy},
                    device_id_type=MESH,
                )
    words = txt[...].astype(F32)
    tx[...] = jnp.concatenate([words[:, 0], words[:, 1]], axis=0).astype(BF16)
    vcopy.wait()
    reward_own[...] = jnp.full(reward_own.shape, reward[0, 0], F32)

    def squeeze(h):
        cols = pl.ds(pl.multiple_of(h * D, D), D)
        r = rt[:, cols]
        twice = jnp.concatenate([r, r], axis=0)
        x = lax.dot_general(vbuf[:, cols], twice, NT, preferred_element_type=F32)
        low = iota((third, D), 1) < C
        for j in range(2):
            first = x[HALF * j : HALF * j + third]
            second = x[HALF * j + third : HALF * j + HALF]
            vrp[h, j] = jnp.where(low, first, second).astype(BF16)
        t = tx[:, cols]
        yv = lax.dot_general(t, twice, NT, preferred_element_type=F32)
        yv = jnp.where(iota(yv.shape, 1) < C, yv, 0.0)
        txb[h] = jnp.where(iota(yv.shape, 0) < TXT, t.astype(F32), yv).astype(BF16)

    def some(count, body):
        at_once = 4 if count % 4 == 0 else 1

        def trip(k, carry):
            for j in range(at_once):
                body(k * at_once + j)
            return carry

        lax.fori_loop(0, count // at_once, trip, 0)

    some(H, squeeze)
    pl.semaphore_wait(barrier, 2 * S - 1 + 2 * (NI - 1) * YN)

    side = s // H

    def at_distance(n, sign):
        half = (n + 1) // 2
        far = jnp.where(n == 2 * half, ZN - half, half)
        return wrap(z + far, ZN) if sign > 0 else wrap(z + ZN - far, ZN)

    def in_turn(n, sign):
        if ZN < 4:
            return at_distance(n, sign)
        return at_distance(jnp.where(n == 0, 0, jnp.where(n <= ZN - 3, n + 2, n - (ZN - 3))), sign)

    def send_keys(k, carry):
        zt = at_distance(ZN - 1 - k // 2, 1)
        h = 2 * zt + lax.rem(k, 2)
        chip = 2 * h + c
        cols = pl.ds(pl.multiple_of(h * D, D), D)
        for j in range(2):
            put(img.at[1, pl.ds(HALF * j, HALF), cols], kv.at[0, s, pl.ds(0, HALF)], ks.at[h, j], kr.at[s], j, chip)
            put(vrp.at[h, j], kv.at[0, s, pl.ds(HALF, third)], ks.at[h, j], kr.at[s], j, chip)
        put(txb.at[h], text.at[0, lax.rem(s, H)], ts.at[h], tr.at[lax.rem(s, H)], side, chip)
        return carry

    lax.fori_loop(0, H, send_keys, 0)

    def send_queries(k, carry):
        zt = in_turn(k // 2, 1)
        h = 2 * zt + lax.rem(k, 2)
        chip = 2 * h + c
        cols = pl.ds(pl.multiple_of(h * D, D), D)
        for j in range(2):
            put(img.at[0, pl.ds(HALF * j, HALF), cols], qbuf.at[s], qs.at[h, j], qr.at[s], j, chip)
        return carry

    lax.fori_loop(0, H, send_queries, 0)
    for k in range(1, NI):
        away(reward_own, rewards.at[i], rs, rr, {"img": wrap(i + k, NI)}).start()

    narrow_t[C:] = jnp.where(iota((ONES, NK), 0) == 0, 1.0, 0.0).astype(BF16)

    def lay_out(p, zs):
        four = pl.ds(zs * YN, YN)
        packed = kv[p, four, HALF:, :].reshape(third * YN, D)
        turned = packed.astype(F32).T
        for ab in range(2):
            rows = pl.ds(pl.multiple_of((2 * p + ab) * n3 + zs * (third * YN), third * YN), third * YN)
            block = kv[p, four, third * ab : third * ab + third, :].reshape(third * YN, D)
            keys[rows, :D] = block
            keys[rows, D:] = block
            keys_t[:, rows] = block.astype(F32).T.astype(BF16)
            one = turned[C * ab : C * ab + C]
            narrow_t[:C, rows] = one.astype(BF16)
            narrow[rows] = jnp.concatenate([one, one], axis=0).T.astype(BF16)

    def arrive(n, carry):
        zs = at_distance(ZN - 1 - n, -1)
        for yy in range(YN):
            src = zs * YN + yy
            drain(kv.at[0, src], kr.at[src])
            away(kv.at[0, src], kv.at[1, src], fs.at[src], fr.at[src], other).start()
        lay_out(0, zs)
        return carry

    lax.fori_loop(0, ZN, arrive, 0)

    def arrive_text(k, carry):
        drain(text.at[0, k], tr.at[k])
        away(text.at[0, k], text.at[1, k], fts.at[k], ftr.at[k], other).start()
        return carry

    lax.fori_loop(0, H, arrive_text, 0)

    def arrive_other(n, carry):
        zs = at_distance(ZN - 1 - n, -1)
        for yy in range(YN):
            drain(kv.at[1, zs * YN + yy], fr.at[zs * YN + yy])
        lay_out(1, zs)
        return carry

    lax.fori_loop(0, ZN, arrive_other, 0)

    def arrive_other_text(k, carry):
        drain(text.at[1, k], ftr.at[k])
        return carry

    lax.fori_loop(0, H, arrive_other_text, 0)
    words = text[...].astype(F32)
    tk = words[:, :, :TXT, :].reshape(TXT * S, D)
    tv = words[:, :, TXT:, :].reshape(TXT * S, D)
    last = pl.ds(NKI, TXT * S)
    keys[last, :D] = tk.astype(BF16)
    keys[last, D:] = tk.astype(BF16)
    keys_t[:, last] = tk.T.astype(BF16)
    tvt = tv.T[:C]
    narrow_t[:C, last] = tvt.astype(BF16)
    narrow[last] = jnp.concatenate([tvt, tvt], axis=0).T.astype(BF16)

    def over_keys(body, carry):
        for at in range(0, NK, BB):
            carry = body(slice(at, min(at + BB, NK)), carry)
        return carry

    def queries_t(zs):
        for yy in range(YN):
            drain(qbuf.at[zs * YN + yy], qr.at[zs * YN + yy])
        x = qbuf[pl.ds(zs * YN, YN)].reshape(QB, D).astype(F32).T * (D ** (-0.5) * 1.4426950408889634)
        hi = x.astype(BF16)
        return jnp.concatenate([hi, (x - hi.astype(F32)).astype(BF16)], axis=0)

    def score(buf, rows, q_t, top):
        st = jnp.dot(keys[rows], q_t, preferred_element_type=F32)
        buf[rows] = st
        return jnp.maximum(top, jnp.max(st.reshape(st.shape[0] // 8, 8, QB), axis=0))

    def weigh(buf, zs, rows, top, hold):
        e = jnp.exp2(buf[rows] - top).astype(BF16)
        weights[zs, rows] = e
        hold[...] = e

    def mix(rows, hold, mixed):
        return mixed + jnp.dot(narrow_t[:, rows], hold[...], preferred_element_type=F32)

    low_top = jnp.full((8, QB), -jnp.inf, F32)
    no_mix = jnp.zeros((C + ONES, QB), F32)
    branch_share = jnp.where(branch == 0, guidance[0, 0], 1.0 - guidance[0, 0])
    parts_of = NKI // KT

    def chunk(k, sub):
        return pl.ds(pl.multiple_of(k * KT + sub * SB, SB), SB)

    def first_scores(q_t):
        def body(k, t):
            for sub in range(subs):
                t = score(scores_a, chunk(k, sub), q_t, t)
            return t

        return score(scores_a, last, q_t, lax.fori_loop(0, parts_of, body, low_top))

    def attend(n, now, then, top8, ahead):
        zs = in_turn(n, -1)
        top = jnp.max(top8, axis=0, keepdims=True)
        q_t = queries_t(in_turn(n + 1, -1)) if ahead else None
        next8 = score(then, last, q_t, low_top) if ahead else low_top
        weigh(now, zs, last, top, hold_text)
        mixed = mix(last, hold_text, no_mix)
        hold[subs - 1] = jnp.zeros((SB, QB), BF16)

        def body(k, carry):
            next8, mixed = carry
            for sub in range(subs):
                before = chunk(jnp.maximum(k - 1, 0), subs - 1) if sub == 0 else chunk(k, sub - 1)
                mixed = mix(before, hold.at[(sub - 1) % subs], mixed)
                if ahead:
                    next8 = score(then, chunk(k, sub), q_t, next8)
                weigh(now, zs, chunk(k, sub), top, hold.at[sub])
            return next8, mixed

        next8, mixed = lax.fori_loop(0, parts_of, body, (next8, mixed))
        mixed = mix(chunk(parts_of - 1, subs - 1), hold.at[subs - 1], mixed)
        inverse = 1.0 / mixed[C : C + 1]
        linv[zs] = inverse
        normal = mixed[:C] * inverse
        out_t[zs] = normal
        for m in range(QB // D):
            a, b = pack_pair(normal[:, D * m : D * m + D] * branch_share)
            for yy, part_of in ((2 * m, a), (2 * m + 1, b)):
                msg[zs * YN + yy] = part_of.astype(BF16)
        for yy in range(YN):
            t = zs * YN + yy
            put(msg.at[t], got.at[s], ms, mr, c, t)
        return next8

    top = first_scores(queries_t(in_turn(0, -1)))

    def two(m, top):
        top = attend(2 * m, scores_a, scores_b, top, True)
        return attend(2 * m + 1, scores_b, scores_a, top, True)

    top = lax.fori_loop(0, ZN // 2 - 1, two, top)
    if ZN > 1:
        top = attend(ZN - 2, scores_a, scores_b, top, True)
        attend(ZN - 1, scores_b, scores_a, top, False)
    else:
        attend(0, scores_a, scores_b, top, False)

    noise_own = own_tokens(noise[...])
    old_own = own_tokens(old[...])
    drain(got, mr)
    guided = jnp.sum(got[...].astype(F32), axis=0)
    step = rate[0, 0]
    deviation = step * (guided - old_own)
    g_own[...] = (noise_own - deviation).astype(BF16)

    def share(k, carry):
        zt = at_distance(k, 1)
        for yy in range(YN):
            put(g_own, g_all.at[s], gs, gr.at[s], c, zt * YN + yy)
        return carry

    lax.fori_loop(0, ZN, share, 0)
    partial = jnp.sum(noise_own * deviation - 0.5 * deviation * deviation)
    part[...] = jnp.full(part.shape, partial, F32)

    def tell(k, carry):
        put(part, parts.at[s], ps, pr, c, k)
        return carry

    lax.fori_loop(0, S, tell, 0)
    gk[...] = jnp.zeros_like(gk)

    cols_home = pl.ds(pl.multiple_of(head * D, D), D)
    mine = pl.ds(pl.multiple_of(HALF * c, HALF), HALF)
    FIRST = min(3, ZN)

    def divide(n):
        zs = at_distance(n, -1)
        for yy in range(YN):
            drain(g_all.at[zs * YN + yy], gr.at[zs * YN + yy])
        g_t = jnp.concatenate(
            [
                unpack_pair(g_all[zs * YN + 2 * m].astype(F32), g_all[zs * YN + 2 * m + 1].astype(F32))
                for m in range(QB // D)
            ],
            axis=1,
        )
        g_t = g_t * linv[zs]
        hi = g_t.astype(BF16)
        lo = (g_t - hi.astype(F32)).astype(BF16)
        hi32 = hi.astype(F32)
        gl[zs] = jnp.concatenate([hi, lo], axis=0)
        delta[zs] = jnp.sum((hi32 + lo.astype(F32)) * out_t[zs], axis=0, keepdims=True)
        gl_cols[zs] = jnp.concatenate([hi32, hi32], axis=0).T.astype(BF16)

    def key_grads(n):
        zs = at_distance(n, -1)
        block = qbuf[pl.ds(zs * YN, YN)].reshape(QB, D)
        g_t = gl[zs]
        shift = delta[zs]

        def one(rows, dq_t):
            gp = jnp.dot(narrow[rows], g_t, preferred_element_type=F32)
            ds = (weights[zs, rows].astype(F32) * (gp - shift)).astype(BF16)
            gk[rows] += jnp.dot(ds, block, preferred_element_type=F32)
            return dq_t + jnp.dot(keys_t[:, rows], ds, preferred_element_type=F32)

        return over_keys(one, jnp.zeros((D, QB), F32)).T

    def send_query_grads(n, rows):
        zs = at_distance(n, -1)
        dqb[pl.ds(zs * YN, YN)] = (rows * (factor[...] * D ** (-0.5))).astype(BF16).reshape(YN, HALF, D)
        for yy in range(YN):
            t = zs * YN + yy
            put(dqb.at[t], grad.at[0, mine, cols_home], dqs, dqr, branch, t)

    def first_blocks(n, carry):
        divide(n)
        held[n] = key_grads(n)
        return carry

    lax.fori_loop(0, FIRST, first_blocks, 0)

    def other_blocks(n, carry):
        divide(n)
        return carry

    lax.fori_loop(FIRST, ZN, other_blocks, 0)

    drain(parts, pr)
    pair[0] = jnp.sum(parts[...], axis=0)
    swap = away(pair.at[0], pair.at[1], pairs, pairr, other)
    swap.start()

    def settle():
        if NI > 1:
            drain(rewards.at[pl.ds(0, NI - 1)], rr)
        own_reward = reward_own[...]
        rewards[i] = own_reward
        mean = jnp.sum(rewards[...], axis=0) / NI
        square = jnp.sum(rewards[...] * rewards[...], axis=0) / NI
        deviates = jnp.sqrt(jnp.maximum(square - mean * mean, 0.0))
        advantage = (own_reward - mean) / jnp.maximum(deviates, 1.0)
        swap.wait()
        ratio_now = jnp.exp((pair[0] + pair[1]) / (2 * S * HALF * C))
        clipped = jnp.clip(ratio_now, 0.8, 1.2)
        keep = ratio_now * advantage <= clipped * advantage
        gain = jnp.where(keep, -ratio_now * advantage, 0.0)
        ratio[0, 0] = jnp.max(ratio_now)
        factor[...] = gain * (step * branch_share)

    NG = max(1, n3 // UB)
    GS = S // NG
    GR = third * GS

    def narrow_grad(rows):
        total = jnp.dot(weights[0, rows], gl_cols[0], preferred_element_type=F32)
        for zs in range(1, ZN):
            total = total + jnp.dot(weights[zs, rows], gl_cols[zs], preferred_element_type=F32)
        return total

    def paired(p, r):
        a, b = (
            narrow_grad(pl.ds(pl.multiple_of((2 * p + ab) * n3 + r * GR, GR), GR)) for ab in range(2)
        )
        return jnp.where(iota(a.shape, 1) < C, a, b).reshape(GS, third, D)

    def swap_u(r):
        srcs = pl.ds(r * GS, GS)
        return away(uo.at[srcs], xu.at[srcs], xus.at[r], xur.at[r], other)

    def send_u(r):
        swap_u(r).wait_recv()
        srcs = pl.ds(r * GS, GS)
        uf[srcs] = ((uown[srcs] + xu[srcs].astype(F32)) * factor[...]).astype(BF16)

        def one(k, carry):
            t = r * GS + k
            put(uf.at[t], ub.at[head, c], us, ur, branch, t)
            return carry

        lax.fori_loop(0, GS, one, 0)

    def group(k):
        return wrap(z * NG // ZN + k, NG)

    swaps = [
        away(uto, xut, xs.at[0], xr.at[0], other),
        away(ko, xk, xs.at[1], xr.at[1], other),
        away(kto, xkt, xs.at[2], xr.at[2], other),
    ]
    both_texts = narrow_grad(last)
    both_texts = jnp.where(iota(both_texts.shape, 1) < C, both_texts, 0.0).reshape(2, H, TXT, D)
    no_keys = jnp.zeros((H, TXT, D), F32)
    uto[...] = jnp.concatenate([no_keys, both_texts[1]], axis=1).astype(BF16)
    swaps[0].start()

    def narrow_group(k, carry):
        r = group(k)
        srcs = pl.ds(r * GS, GS)
        uo[srcs] = paired(1, r).astype(BF16)
        swap_u(r).start()
        pl.when(k == min(1, NG - 1))(settle)

        @pl.when(k > 0)
        def _():
            send_u(group(k - 1))

        uown[srcs] = paired(0, r)

        return carry

    lax.fori_loop(0, NG, narrow_group, 0)
    swaps[0].wait_recv()
    utf[...] = (
        (jnp.concatenate([no_keys, both_texts[0]], axis=1) + xut[...].astype(F32)) * factor[...]
    ).astype(BF16)

    def send_text(k, carry):
        put(utf.at[k], utb.at[head], uts, utr, branch, c * H + k)
        return carry

    lax.fori_loop(0, H, send_text, 0)
    send_u(group(NG - 1))

    def send_held(n, carry):
        send_query_grads(n, held[n])
        return carry

    lax.fori_loop(0, FIRST, send_held, 0)

    def widen_all():
        drain(ub, ur)
        drain(utb, utr)

        def widen(h):
            at = pl.ds(pl.multiple_of(h * D, D), D)
            r = rt[:, at]
            twice = jnp.concatenate([r, r], axis=0)
            low = iota((third, D), 1) < C
            u0, u1 = ub[h, 0].astype(F32), ub[h, 1].astype(F32)
            spaced = jnp.concatenate(
                [
                    jnp.where(low, u0, 0.0),
                    jnp.where(low, 0.0, u0),
                    jnp.where(low, u1, 0.0),
                    jnp.where(low, 0.0, u1),
                    utb[h].astype(F32),
                ],
                axis=0,
            )
            wide = jnp.dot(spaced.astype(BF16), twice, preferred_element_type=F32)
            dv[:, at] = wide[: 2 * HALF].astype(BF16)
            dvt[:, at] = wide[2 * HALF + TXT :]
            values = jnp.concatenate([vbuf[:, at], tx[:, at]], axis=0)
            res = jnp.dot(spaced.T.astype(BF16), values, preferred_element_type=F32)
            rgp[:, at] = res[:C] + res[C:]

        some(H, widen)
        pltpu.make_async_copy(dv, grad.at[2], dvsem).start()

    me = 2 * i + c

    def piece(n):
        return pl.ds(pl.multiple_of(n * W, D), W)

    def strip(n):
        return pl.ds(pl.multiple_of(n * RY, RY), RY)

    def peers():
        for k in range(YN):
            yy = wrap(y + k, YN)
            for kk in range(NI):
                n = wrap(i + kk, NI)
                for core in (c, 1 - c) if k + kk else (1 - c,):
                    yield 2 * n + core, yy, {"cfg": core, "img": n, "seq": z * YN + yy}

    def readout_1():
        rgb[...] = rgp[...].astype(BF16)
        for n, yy, device in peers():
            away(rgb.at[strip(yy), piece(n)], r1.at[y * NP + me], as_.at[0], ar.at[0], device).start()

    def readout_2():
        drain(r1.at[pl.ds(0, NP * YN - 1)], ar.at[0])
        r1[y * NP + me] = rgb[strip(y), piece(me)]
        a2[...] = jnp.sum(r1[...].astype(F32), axis=0).astype(BF16)
        for k in range(1, ZN):
            n = wrap(z + k, ZN)
            away(a2, r3.at[z], as_.at[1], ar.at[1], {"seq": n * YN + y}).start()

    def readout_3():
        if ZN > 1:
            drain(r3.at[pl.ds(0, ZN - 1)], ar.at[1])
        r3[z] = a2[...]
        a3[...] = jnp.sum(r3[...].astype(F32), axis=0).astype(BF16)
        to = rg.at[y, :, piece(me)]
        pltpu.make_async_copy(a3, to, ls).start()
        for _, _, device in peers():
            away(a3, to, as_.at[2], ar.at[2], device).start()

    def other_key_grads(n, carry):
        send_query_grads(n, key_grads(n))
        return carry

    lax.fori_loop(FIRST, ZN, other_key_grads, 0)

    def image_keys(p):
        base = 2 * p * n3
        a = gk[base : base + n3].reshape(S, third, D)
        b = gk[base + n3 : base + 2 * n3].reshape(S, third, D)
        return jnp.concatenate([a, b], axis=1) * (factor[...] * D ** (-0.5))

    def text_keys(p):
        k = gk[NKI + p * H * TXT : NKI + (p + 1) * H * TXT]
        k = (k * (factor[...] * D ** (-0.5))).reshape(H, TXT, D)
        return jnp.concatenate([k, jnp.zeros_like(k)], axis=1)

    widen_all()
    readout_1()
    ko[...] = image_keys(1).astype(BF16)
    swaps[1].start()
    kto[...] = text_keys(1).astype(BF16)
    swaps[2].start()
    swaps[1].wait_recv()
    kf[...] = (image_keys(0) + xk[...].astype(F32)).astype(BF16)

    def send_key_grads(k, carry):
        zt = at_distance(ZN - 1 - k, 1)
        for yy in range(YN):
            t = zt * YN + yy
            put(kf.at[t], grad.at[1, mine, cols_home], dks, dkr, branch, t)
        return carry

    readout_2()
    lax.fori_loop(0, ZN, send_key_grads, 0)
    swaps[2].wait_recv()
    ktf[...] = (text_keys(0) + xkt[...].astype(F32)).astype(BF16)

    def send_text_keys(k, carry):
        put(ktf.at[k], ktb.at[head], kts, ktr, branch, c * H + k)
        return carry

    lax.fori_loop(0, H, send_text_keys, 0)

    readout_3()

    def sent(k, carry):
        chip = 2 * k + c
        for odd in range(2):
            src = 2 * k + odd
            drain(kv.at[1, src], fs.at[src])
        drain(text.at[1, k], fts.at[k])
        for j in range(2):
            @pl.when(jnp.logical_not(jnp.logical_and(chip == s, j == c)))
            def _():
                drain(kv.at[0, 0], ks.at[k, j])
                drain(qbuf.at[0], qs.at[k, j])

        @pl.when(jnp.logical_not(jnp.logical_and(chip == s, side == c)))
        def _():
            drain(text.at[0, 0], ts.at[k])

        return carry

    lax.fori_loop(0, H, sent, 0)
    drain(got.at[pl.ds(0, S - 1)], ms)
    drain(g_all.at[pl.ds(0, S - 1)], gs)
    drain(parts.at[pl.ds(0, S - 1)], ps)
    if NI > 1:
        drain(rewards.at[pl.ds(0, NI - 1)], rs)
    for w in swaps:
        w.wait_send()
    rest = r1.at[pl.ds(0, NP * YN - 1)]
    drain(rest, as_.at[0])
    if ZN > 1:
        drain(r3.at[pl.ds(0, ZN - 1)], as_.at[1])
    drain(rest, as_.at[2])
    drain(a3, ls)
    drain(rest, ar.at[2])

    def swapped_u(r, carry):
        swap_u(r).wait_send()
        return carry

    lax.fori_loop(0, NG, swapped_u, 0)
    drain(dv, dvsem)
    text_here = jnp.logical_and(branch == c, s // H == c)

    @pl.when(branch == c)
    def _():
        drain(uf.at[pl.ds(0, S - 1)], us)
        drain(dqb.at[pl.ds(0, S - 1)], dqs)
        drain(kf.at[pl.ds(0, S - 1)], dks)

    @pl.when(branch != c)
    def _():
        drain(uf, us)
        drain(dqb, dqs)
        drain(kf, dks)

    @pl.when(text_here)
    def _():
        drain(utf.at[pl.ds(0, H - 1)], uts)
        drain(ktf.at[pl.ds(0, H - 1)], kts)

    @pl.when(jnp.logical_not(text_here))
    def _():
        drain(utf, uts)
        drain(ktf, kts)

    drain(ktb, ktr)

    def text_home(h, carry):
        at = pl.ds(pl.multiple_of(h * D, D), D)
        dkt[:, at] = ktb[h].astype(F32)[:TXT]
        return carry

    lax.fori_loop(0, H, text_home, 0)
    tgrad[...] = jnp.stack([dkt[...], dvt[...]], axis=1).astype(BF16)
    drain(grad.at[0], dqr)
    drain(grad.at[1], dkr)


def step_call(S, NI, guidance, rate, reward, img, txt, rt, noise, old):
    H, ZN, NP = S // 2, S // YN, 2 * NI
    HD = rt.shape[1]
    W, RY, third = HD // NP, C // YN, HALF // 2
    NK = (2 * HALF + TXT) * S
    dma = pltpu.SemaphoreType.DMA
    tile = (1, D)
    b = lambda *shape: pltpu.VMEM(shape, BF16)
    w = lambda *shape: pltpu.VMEM(shape, F32)
    return pl.pallas_call(
        functools.partial(step_kernel, S, NI),
        out_shape=(
            jax.ShapeDtypeStruct(img.shape, BF16),
            jax.ShapeDtypeStruct((TXT, 2, HD), BF16),
            jax.ShapeDtypeStruct((YN, RY, HD), BF16),
            jax.ShapeDtypeStruct((1, 1), F32),
        ),
        in_specs=[SMEM, SMEM, SMEM, ANY, VMEM, VMEM, VMEM, VMEM],
        out_specs=(ANY, VMEM, ANY, SMEM),
        scratch_shapes=[
            b(2 * TXT, HD),
            b(*img.shape[1:]),
            b(H, 2, third, D),
            b(H, 2 * TXT, D),
            b(2, S, HALF + third, D),
            b(2, H, 2 * TXT, D),
            b(S, HALF, D),
            b(NK, 2 * D),
            b(D, NK),
            b(NK, D),
            b(C + ONES, NK),
            w(NK, QB),
            w(NK, QB),
            b(KB // SB, SB, QB),
            b(TXT * S, QB),
            b(ZN, NK, QB),
            w(ZN, C, QB),
            w(ZN, 1, QB),
            b(S, C // 2, D),
            b(S, C // 2, D),
            b(C // 2, D),
            b(S, C // 2, D),
            w(*tile),
            w(S, *tile),
            w(2, *tile),
            w(NI, *tile),
            w(*tile),
            b(ZN, 2 * C, QB),
            b(ZN, QB, D),
            w(ZN, 1, QB),
            w(NK, D),
            w(*tile),
            w(min(3, ZN), QB, D),
            b(S, third, D),
            b(S, third, D),
            w(S, third, D),
            b(S, third, D),
            b(H, 2 * TXT, D),
            b(H, 2 * TXT, D),
            b(H, 2 * TXT, D),
            b(S, HALF, D),
            b(S, HALF, D),
            b(S, HALF, D),
            b(H, 2 * TXT, D),
            b(H, 2 * TXT, D),
            b(H, 2 * TXT, D),
            b(S, HALF, D),
            b(H, 2, third, D),
            b(H, 2 * TXT, D),
            b(H, 2 * TXT, D),
            b(*img.shape[1:]),
            w(TXT, HD),
            w(TXT, HD),
            w(C, HD),
            b(C, HD),
            b(NP * YN, RY, W),
            b(RY, W),
            b(ZN, RY, W),
            b(RY, W),
            dma,
            dma((H, 2)), dma((S,)),
            dma((H, 2)), dma((S,)),
            dma((H,)), dma((H,)),
            dma((S,)), dma((S,)),
            dma((H,)), dma((H,)),
            dma, dma,
            dma, dma((S,)),
            dma, dma,
            dma, dma,
            dma, dma,
            dma((3,)), dma((3,)),
            dma((max(1, third * S // UB),)), dma((max(1, third * S // UB),)),
            dma, dma,
            dma, dma,
            dma, dma,
            dma, dma,
            dma, dma,
            dma,
            dma((3,)), dma((3,)),
            dma,
        ],
        compiler_params=pltpu.CompilerParams(
            collective_id=0, has_side_effects=True, vmem_limit_bytes=LIMIT
        ),
        name="step",
    )(guidance, rate, reward, img, txt, rt, noise, old)


def on_device(S, NI, img_qkv, txt_kv, readout, old_velocity, noise, step_ratio, rewards, guidance):
    img = img_qkv[0, 0].transpose(1, 0, 2)
    text = txt_kv[0, 0]
    scalar = lambda x: x.reshape(1, 1)
    grad, tgrad, rg, ratio = step_call(
        S, NI, scalar(guidance), scalar(step_ratio), scalar(rewards), img, text, readout.T, noise[0].T, old_velocity[0].T
    )
    img_grad = grad.transpose(1, 0, 2)[None, None]
    return (img_grad, tgrad[None, None], rg.reshape(C, -1).T.astype(F32), ratio.reshape(1))


def solution(mesh):
    S, NI = mesh.shape["seq"], mesh.shape["img"]
    placed = (
        P("cfg", "img", "seq", None, None),
        P("cfg", "img", "seq", None, None),
        P(),
        P("img", "seq", None),
        P("img", "seq", None),
        P("img"),
        P("img"),
        P(),
    )
    return jax.shard_map(
        functools.partial(on_device, S, NI),
        mesh=mesh,
        in_specs=placed,
        out_specs=(
            P("cfg", "img", "seq", None, None),
            P("cfg", "img", "seq", None, None),
            P(),
            P("img"),
        ),
        check_vma=False,
    )
```
